32 devices in a mesh: pts: 4 (over x, core), snap: 8 (over z, y).
Axes of the slice: x: 2, y: 2, z: 4, core: 2. Of those that a mesh axis runs over, the one named last changes fastest.
Arguments:
- snapshots: float32 [4096, 8192], P('pts', 'snap'), may hold values from -8 to 8
- modes_init: float32 [4096, 128], P('pts'), may hold values from -6 to 6
- coefs_init: float32 [128, 8192], P(None, 'snap'), may hold values from -0.09375 to 0.09375
Outputs:
- modes: float32 [4096, 128], P('pts')
- amplitudes: float32 [128, 8192], P(None, 'snap')
The draws below stay inside these ranges and needn't reach their ends.
All inputs are finite; a program needn't handle non-finite values.
Results may differ from the reference program's by a relative error of at most 0.0003.
Values sent between devices are 32-bit elements; how exact they have to be, the bound alone decides.
A program may use at most 64 MiB of HBM per device.

```python
import jax
import jax.numpy as jnp
from jax import lax

RANK = 128
S_DEV = 1024
OUTER = 2
INNER = 2
NP = 4096
NS = 8192
N_SNAP = 8


def shard_levels(key, extent, split, least, top_value):
    loudness = 1.0
    for position, shards_of in split:
        draws = jax.random.uniform(jax.random.fold_in(jax.random.fold_in(key, 6), position), (shards_of,), jnp.float32, least / len(split), top_value / len(split))
        loudness = loudness * jnp.repeat(jnp.exp(draws), extent[position] // shards_of).reshape((-1,) + (1,) * (len(extent) - 1 - position))
    return loudness


def normal_values(key, dims, scale, most, split=(), held_as=jnp.bfloat16):
    level = shard_levels(key, dims, split, -0.22, 0.18) if split else 1.0
    entries = jax.random.normal(key, dims, jnp.float32) * scale * level
    return jnp.minimum(jnp.maximum(entries, -most), most).astype(held_as)


def setup_inputs(seed: int = 0) -> dict:
    arg_keys = jax.random.split(jax.random.key(seed), 4)
    snapshots = normal_values(arg_keys[0], (NP, NS), 1.0, 8.0, ((0, 4), (1, 8)), jnp.float32)
    modes_init = normal_values(arg_keys[1], (NP, RANK), 1.0, 6.0, ((0, 4),), jnp.float32)
    coefs_init = normal_values(arg_keys[2], (RANK, NS), NP ** -0.5, 0.09375, ((1, 8),), jnp.float32)
    return {"snapshots": snapshots, "modes_init": modes_init, "coefs_init": coefs_init}


HUBER = 1.345
RIDGE = 0.01

def high_dot(left, right):
    return jnp.dot(left.astype(jnp.float32), right.astype(jnp.float32), preferred_element_type=jnp.float32, precision=lax.Precision.HIGHEST)

def column_block(snapshots, coefs, index):
    start = (index * S_DEV).astype(jnp.int32)
    block = lax.dynamic_slice_in_dim(snapshots, start, S_DEV, 1)
    coef_block = lax.dynamic_slice_in_dim(coefs, start, S_DEV, 1)
    return (block, coef_block)

def error_block(snapshots, modes, coefs, index):
    block, coef_block = column_block(snapshots, coefs, index)
    return (block - high_dot(modes, coef_block), coef_block)

def find_limit(snapshots, modes, coefs):
    blocks = jnp.arange(N_SNAP, dtype=jnp.int32)

    def squares(index):
        error, unused = error_block(snapshots, modes, coefs, index)
        return jnp.sum(error * error)
    total = jnp.sum(lax.map(squares, blocks))
    return HUBER * jnp.sqrt(total / (NP * NS) + 1e-06)

def reference(snapshots, modes_init, coefs_init):
    modes = modes_init
    coefs = coefs_init
    eye = jnp.eye(RANK, dtype=jnp.float32)
    blocks = jnp.arange(N_SNAP, dtype=jnp.int32)
    for outer in range(OUTER):
        gram = high_dot(modes.T, modes) + RIDGE * eye
        factor = jnp.linalg.cholesky(gram)
        for inner in range(INNER):
            limit = find_limit(snapshots, modes, coefs)

            def project(index):
                error, unused = error_block(snapshots, modes, coefs, index)
                return high_dot(modes.T, jnp.clip(error, -limit, limit))
            pieces = lax.map(project, blocks)
            product = jnp.transpose(pieces, (1, 0, 2)).reshape(RANK, NS)
            coefs = coefs + jax.scipy.linalg.cho_solve((factor, True), product)
        limit = find_limit(snapshots, modes, coefs)
        hess = high_dot(coefs, coefs.T) + RIDGE * eye
        hfactor = jnp.linalg.cholesky(hess)

        def accumulate(total, index):
            error, coef_block = error_block(snapshots, modes, coefs, index)
            return (total + high_dot(jnp.clip(error, -limit, limit), coef_block.T), None)
        start_total = jnp.zeros((NP, RANK), jnp.float32)
        moment, unused = lax.scan(accumulate, start_total, blocks)
        modes = modes + jax.scipy.linalg.cho_solve((hfactor, True), moment.T).T
    return (modes, coefs * jnp.sqrt(jnp.float32(NP)))
```

```python
import functools

import jax
import jax.numpy as jnp
from jax import lax
from jax.experimental import pallas as pl
from jax.experimental.pallas import tpu as pltpu
from jax.sharding import PartitionSpec as P

OUTER = 2
INNER = 2
PIVOTS = 4
CHUNK = 128
STEP = 256

HUBER = 1.345
RIDGE = 0.01

F32 = jnp.float32
BF16 = jnp.bfloat16
MESH = pl.DeviceIdType.MESH


def split(x):
    hi = x.astype(BF16)
    lo = (x - hi.astype(F32)).astype(BF16)
    return hi, lo


def dot(a, b):
    return jnp.dot(a, b, preferred_element_type=F32)


def quads(x):
    r, c = x.shape[0] // 2, x.shape[1] // 2
    return (x[:r, :c] + x[:r, c:]) + (x[r:, :c] + x[r:, c:])


def pts_peer(me, j, n):
    if n % 2:
        return lax.rem(me + j, n)
    x, c = me // 2, lax.rem(me, 2)
    return lax.rem(x + j // 2, n // 2) * 2 + lax.rem(c + lax.rem(j, 2), 2)


def snap_peer(me, j, n):
    return lax.rem(me + j, n)


def kernel(n_pts, n_snap, s_hbm, m_hbm, c_hbm, m_out, c_out,
           s, e, mcat, mtcat, ccat, ctcat, sq,
           gpart, gslots, gred, gfull, hpart, hslots, hred, hfull,
           lslots, cpart, cslots, xslots, mpart, mslots,
           load_sem, p_send, p_recv, s_send, s_recv, c_send, c_recv, x_send, x_recv,
           l_send, l_recv, m_send, m_recv):
    rows, width = s.shape
    rank = m_out.shape[1]
    pme = lax.axis_index("pts")
    sme = lax.axis_index("snap")
    n_dev = n_pts * n_snap
    me = pme * n_snap + sme
    rw = rows // n_snap
    half = width // 2
    chunks = half // CHUNK
    n_x, n_z = n_pts // 2, n_snap // 2
    px, core = pme // 2, lax.rem(pme, 2)
    sz, sy = sme // 2, lax.rem(sme, 2)
    gw = rank // n_pts
    hw = rank // n_snap
    count = float(rows * n_pts * width * n_snap)
    loads = width // STEP

    def offset(d):
        dx, dc, dz, dy = d
        return {"pts": lax.rem(px + dx, n_x) * 2 + lax.rem(core + dc, 2),
                "snap": lax.rem(sz + dz, n_z) * 2 + lax.rem(sy + dy, 2)}

    def hops(d):
        dx, dc, dz, dy = d
        return min(dx, n_x - dx) + dy + min(dz, n_z - dz) + 0.1 * dc
    others = [(dx, dc, dz, dy) for dx in range(n_x) for dc in range(2) for dz in range(n_z) for dy in range(2)][1:]
    others.sort(key=lambda d: -hops(d))

    barrier = pltpu.get_barrier_semaphore()
    for d in others:
        pl.semaphore_signal(barrier, inc=1, device_id=offset(d), device_id_type=MESH)

    def load_cols(j):
        cols = pl.ds(j * STEP, STEP)
        return pltpu.make_async_copy(s_hbm.at[:, cols], s.at[:, cols], load_sem.at[2 + j])
    load_m = pltpu.make_async_copy(m_hbm, m_out, load_sem.at[0])
    load_c = pltpu.make_async_copy(c_hbm, c_out, load_sem.at[1])
    load_m.start()
    load_c.start()
    for j in range(loads):
        load_cols(j).start()

    def pcopy(site, j, src, dst):
        return pltpu.make_async_remote_copy(
            src_ref=src, dst_ref=dst, send_sem=p_send.at[site, j - 1], recv_sem=p_recv.at[site, j - 1],
            device_id={"pts": pts_peer(pme, j, n_pts)}, device_id_type=MESH)

    def scopy(site, j, src, dst):
        return pltpu.make_async_remote_copy(
            src_ref=src, dst_ref=dst, send_sem=s_send.at[site, j - 1], recv_sem=s_recv.at[site, j - 1],
            device_id={"snap": snap_peer(sme, j, n_snap)}, device_id_type=MESH)

    def ccopy(site, k, src, dst):
        return pltpu.make_async_remote_copy(
            src_ref=src, dst_ref=dst, send_sem=c_send.at[site, k], recv_sem=c_recv.at[site, k],
            device_id={"pts": px * 2 + 1 - core}, device_id_type=MESH)

    def xcopy(site, k, d):
        ref = xslots.at[site, px, k]
        return pltpu.make_async_remote_copy(
            src_ref=ref, dst_ref=ref, send_sem=x_send.at[site, k, d - 1], recv_sem=x_recv.at[site, k, d - 1],
            device_id={"pts": lax.rem(px + d, n_x) * 2 + core}, device_id_type=MESH)

    def lcopy(use, i):
        ref = lslots.at[use, pl.ds(me, 1)]
        return pltpu.make_async_remote_copy(
            src_ref=ref, dst_ref=ref, send_sem=l_send.at[use, i], recv_sem=l_recv.at[use, i],
            device_id=offset(others[i]), device_id_type=MESH)

    def shift(t):
        u = lax.rem(t, n_z)
        dz = n_z // 2 + ((u + 1) // 2) * (1 - 2 * lax.rem(u, 2))
        return dz, 1 - t // n_z

    def mcopy(site, t, src, dst):
        dz, dy = shift(t)
        return pltpu.make_async_remote_copy(
            src_ref=src, dst_ref=dst, send_sem=m_send.at[site, t], recv_sem=m_recv.at[site, t],
            device_id={"snap": lax.rem(sz + dz, n_z) * 2 + lax.rem(sy + dy, 2)}, device_id_type=MESH)

    def rows_to(t):
        dz, dy = shift(t)
        return pl.ds(pl.multiple_of((lax.rem(sz + dz, n_z) * 2 + lax.rem(sy + dy, 2)) * rw, rw), rw)

    def rows_from(t):
        dz, dy = shift(t)
        return pl.ds(pl.multiple_of((lax.rem(sz + n_z - dz, n_z) * 2 + lax.rem(sy + 2 - dy, 2)) * rw, rw), rw)

    def col_chunk(which, k):
        return pl.ds(pl.multiple_of(which * half + k * CHUNK, CHUNK), CHUNK)

    def start(copies):
        for copy in copies:
            copy.start()

    def finish(copies):
        for copy in copies:
            copy.wait_recv()
        for copy in copies:
            copy.wait_send()

    def prepare_rows(part):
        hi, lo = split(m_out[part, :])
        mcat[part, :rank] = hi
        mcat[part, rank:] = lo

    def prepare_mt():
        hi, lo = split(m_out[...].T)
        mtcat[:rank, :] = hi
        mtcat[rank:, :] = lo

    def prepare_cols(cols, value):
        hi, lo = split(value)
        ccat[:rank, cols] = hi
        ccat[rank:, cols] = lo

    def prepare_ct(cols, value):
        hi, lo = split(value.T)
        ctcat[cols, :rank] = hi
        ctcat[cols, rank:] = lo

    def sweep(ref, base, steps):
        lane = lax.broadcasted_iota(jnp.int32, (rank, rank), 1)
        sub = lax.broadcasted_iota(jnp.int32, (rank, rank), 0)
        lane_row = lax.broadcasted_iota(jnp.int32, (1, rank), 1)
        sub_col = lax.broadcasted_iota(jnp.int32, (rank, 1), 0)

        def body(t, carry):
            k = (base + t) * PIVOTS
            full = ref[...]
            cols = [jnp.sum(jnp.where(lane == k + p, full, 0.0), axis=1, keepdims=True) for p in range(PIVOTS)]
            rws = [ref[pl.ds(k + p, 1), :] for p in range(PIVOTS)]
            blk = {}
            for p in range(PIVOTS):
                for q in range(p, PIVOTS):
                    blk[p, q] = jnp.sum(jnp.where(lane_row == k + q, rws[p], 0.0), axis=1, keepdims=True)
            for p in range(PIVOTS):
                inv = 1.0 / blk[p, p]
                row, col = rws[p], cols[p]
                for q in range(p + 1, PIVOTS):
                    f = blk[p, q] * inv
                    rws[q] = jnp.where(lane_row == k + p, f, rws[q] - f * row)
                    cols[q] = jnp.where(sub_col == k + p, f, cols[q] - f * col)
                    for u in range(q, PIVOTS):
                        blk[q, u] = blk[q, u] - f * blk[p, u]
                rowd = row * inv
                full = jnp.where(lane == k + p, col * inv, full - col * rowd)
                full = jnp.where(sub == k + p, jnp.where(lane_row == k + p, -inv, rowd), full)
            ref[...] = full
            return carry
        with jax.named_scope("sweep"):
            lax.fori_loop(0, steps, body, 0)

    def errors(part, n_rows, cols):
        hi, lo = mcat[part, :rank], mcat[part, rank:]
        c = ccat[:, cols]
        fit = dot(jnp.concatenate([hi, hi], 1), c) + dot(jnp.concatenate([lo, lo], 1), c)
        err = s[part, cols] - fit
        e[part, cols] = err
        sq[...] += jnp.sum((err * err).reshape(n_rows // 8, 8, STEP), axis=0)

    def step_cols(j):
        return pl.ds(pl.multiple_of(j * STEP, STEP), STEP)

    def error_rows(part):
        def body(j, carry):
            errors(part, rw, step_cols(j))
            return carry
        lax.fori_loop(0, loads, body, 0)

    def send_limit(use):
        acc = sq[:, :128]
        for k in range(1, STEP // 128):
            acc = acc + sq[:, k * 128:(k + 1) * 128]
        lslots[use, pl.ds(me, 1), :] = jnp.sum(acc, axis=0, keepdims=True)
        start([lcopy(use, i) for i in range(n_dev - 1)])
        sq[...] = jnp.zeros_like(sq)

    def get_limit(use):
        with jax.named_scope("limit"):
            for i in reversed(range(n_dev - 1)):
                lcopy(use, i).wait_recv()
        total = jnp.sum(jnp.sum(lslots[use], axis=0, keepdims=True), axis=1, keepdims=True)
        for i in range(n_dev - 1):
            lcopy(use, i).wait_send()
        return HUBER * jnp.sqrt(total / count + 1e-06)

    eye = (lax.broadcasted_iota(jnp.int32, (rank, rank), 0)
           == lax.broadcasted_iota(jnp.int32, (rank, rank), 1)).astype(F32) * RIDGE

    grs = [pcopy(0, j, gpart.at[pl.ds(pts_peer(pme, j, n_pts) * gw, gw)], gslots.at[j - 1]) for j in range(1, n_pts)]
    gag = [pcopy(1, j, gred, gfull.at[pl.ds(pme * gw, gw)]) for j in range(1, n_pts)]
    hrs = [scopy(0, j, hpart.at[pl.ds(snap_peer(sme, j, n_snap) * hw, hw)], hslots.at[j - 1]) for j in range(1, n_snap)]
    hag = [scopy(1, j, hred, hfull.at[pl.ds(sme * hw, hw)]) for j in range(1, n_snap)]
    own_rows = pl.ds(pl.multiple_of(sme * rw, rw), rw)

    def gram_part():
        prepare_mt()
        gpart[...] = quads(dot(mtcat[...], mcat[...]))

    sq[...] = jnp.zeros_like(sq)
    load_m.wait()
    prepare_rows(pl.ds(0, rows))
    gram_part()
    load_c.wait()
    prepare_cols(pl.ds(0, width), c_out[...])
    with jax.named_scope("barrier"):
        pl.semaphore_wait(barrier, n_dev - 1)
    start(grs)
    for j in range(loads):
        load_cols(j).wait()
    with jax.named_scope("err0"):
        def first(j, carry):
            errors(pl.ds(0, rows), rows, step_cols(j))
            return carry
        lax.fori_loop(0, loads, first, 0)
    send_limit(0)

    def outer(o, carry):
        more = o < OUTER - 1
        finish(grs)
        own = gpart[pl.ds(pme * gw, gw), :]
        for j in range(1, n_pts):
            own = own + gslots[j - 1]
        gred[...] = own
        gfull[pl.ds(pme * gw, gw), :] = own
        start(gag)

        for inner in range(INNER):
            limit = get_limit(inner)

            def give(k):
                return ccopy(inner, k, cpart.at[k], cslots.at[inner, k])

            def spread(k):
                ref = c_out.at[:, col_chunk(core, k)]
                return ccopy(INNER + inner, k, ref, ref)

            def products(t, carry):
                last = t == 2 * chunks - 1
                theirs = (t == 0) | ((lax.rem(t, 2) == 1) & (t < 2 * chunks - 1))
                k = jnp.where(theirs, (t + 1) // 2, jnp.where(last, chunks - 1, t // 2 - 1))
                which = jnp.where(theirs, 1 - core, core)
                hi, lo = split(jnp.clip(e[:, col_chunk(which, k)], -limit, limit))
                value = quads(dot(mtcat[...], jnp.concatenate([hi, lo], 1)))

                @pl.when(theirs)
                def _():
                    cpart[k] = value
                    give(k).start()

                @pl.when(jnp.logical_not(theirs))
                def _():
                    give(k).wait_recv()
                    xslots[inner, px, k] = value + cslots[inner, k]
                    for d in range(1, n_x):
                        xcopy(inner, k, d).start()
                return carry
            with jax.named_scope("products"):
                lax.fori_loop(0, 2 * chunks, products, 0)
            if inner == 0:
                finish(gag)
                gfull[...] = gfull[...] + eye
                sweep(gfull, 0, rank // PIVOTS)

            def update(t, carry):
                j = t // 2
                mine = lax.rem(t, 2) == 0
                per = STEP // CHUNK

                def own_cols(i, carry):
                    k = j * per + i
                    for d in range(1, n_x):
                        xcopy(inner, k, d).wait_recv()
                    share = xslots[inner, 0, k]
                    for x in range(1, n_x):
                        share = share + xslots[inner, x, k]
                    step = jnp.dot(gfull[...], share, preferred_element_type=F32, precision=lax.Precision.HIGHEST)
                    cols = col_chunk(core, k)
                    value = c_out[:, cols] - step
                    c_out[:, cols] = value
                    spread(k).start()
                    prepare_cols(cols, value)
                    if inner == INNER - 1:
                        prepare_ct(cols, value)
                    return carry

                def their_cols(i, carry):
                    k = j * per + i
                    spread(k).wait_recv()
                    cols = col_chunk(1 - core, k)
                    value = c_out[:, cols]
                    prepare_cols(cols, value)
                    if inner == INNER - 1:
                        prepare_ct(cols, value)
                    return carry

                @pl.when(mine)
                def _():
                    lax.fori_loop(0, per, own_cols, 0)

                @pl.when(jnp.logical_not(mine))
                def _():
                    lax.fori_loop(0, per, their_cols, 0)
                which = jnp.where(mine, core, 1 - core)
                with jax.named_scope("errchunk"):
                    errors(pl.ds(0, rows), rows, pl.ds(pl.multiple_of(which * half + j * STEP, STEP), STEP))
                return carry
            with jax.named_scope("update"):
                lax.fori_loop(0, loads, update, 0)
            send_limit(inner + 1)

            def settle(k, carry):
                spread(k).wait_send()
                give(k).wait_send()
                for d in range(1, n_x):
                    xcopy(inner, k, d).wait_send()
                return carry
            lax.fori_loop(0, chunks, settle, 0)

        with jax.named_scope("hpart"):
            hpart[...] = quads(dot(ccat[...], ctcat[...]))
            start(hrs)
        with jax.named_scope("hrs"):
            finish(hrs)
        own = hpart[pl.ds(sme * hw, hw), :]
        for j in range(1, n_snap):
            own = own + hslots[j - 1]
        hred[...] = own
        hfull[pl.ds(sme * hw, hw), :] = own
        start(hag)
        limit = get_limit(INNER)

        def moment(part):
            hi, lo = split(jnp.clip(e[part, :], -limit, limit))
            return quads(dot(jnp.concatenate([hi, lo], 0), ctcat[...]))

        def reduce_to(t):
            return mcopy(0, t, mpart.at[t], mslots.at[t])

        def gather(t):
            ref = m_out.at[own_rows]
            return mcopy(1, t, ref, ref)

        def moments(t, carry):
            mpart[t] = moment(rows_to(t))

            @pl.when(t < n_snap - 1)
            def _():
                reduce_to(t).start()
            return carry
        with jax.named_scope("moments"):
            lax.fori_loop(0, n_snap, moments, 0)
        with jax.named_scope("hag"):
            finish(hag)
        hfull[...] = hfull[...] + eye
        sweep(hfull, 0, rank // PIVOTS)
        with jax.named_scope("mwait"):
            for t in range(n_snap - 1):
                reduce_to(t).wait_recv()
        share = mpart[n_snap - 1]
        for t in range(n_snap - 1):
            share = share + mslots[t]
        step = jnp.dot(share, hfull[...], preferred_element_type=F32, precision=lax.Precision.HIGHEST)
        m_out[own_rows, :] = m_out[own_rows, :] - step
        start([gather(t) for t in range(n_snap - 1)])

        @pl.when(more)
        def _():
            prepare_rows(own_rows)
            error_rows(own_rows)

        def arrivals(u, carry):
            t = n_snap - 2 - u
            gather(t).wait_recv()

            @pl.when(more)
            def _():
                prepare_rows(rows_from(t))
                error_rows(rows_from(t))
            return carry
        with jax.named_scope("arrivals"):
            lax.fori_loop(0, n_snap - 1, arrivals, 0)

        @pl.when(more)
        def _():
            send_limit(0)
            gram_part()
            start(grs)
        for t in range(n_snap - 1):
            reduce_to(t).wait_send()
            gather(t).wait_send()
        return carry
    lax.fori_loop(0, OUTER, outer, 0)


def shards(n_pts, n_snap, snapshots, modes_init, coefs_init):
    rows, width = snapshots.shape
    rank = modes_init.shape[1]
    rw, gw, hw = rows // n_snap, rank // n_pts, rank // n_snap
    chunks, n_x, n_dev = width // 2 // CHUNK, n_pts // 2, n_pts * n_snap
    points = float(rows * n_pts)
    vmem, dma = pltpu.VMEM, pltpu.SemaphoreType.DMA
    scratch = [
        vmem((rows, width), F32), vmem((rows, width), F32),
        vmem((rows, 2 * rank), BF16), vmem((2 * rank, rows), BF16),
        vmem((2 * rank, width), BF16), vmem((width, 2 * rank), BF16),
        vmem((8, STEP), F32),
        vmem((rank, rank), F32), vmem((n_pts - 1, gw, rank), F32), vmem((gw, rank), F32), vmem((rank, rank), F32),
        vmem((rank, rank), F32), vmem((n_snap - 1, hw, rank), F32), vmem((hw, rank), F32), vmem((rank, rank), F32),
        vmem((INNER + 1, n_dev, 128), F32),
        vmem((chunks, rank, CHUNK), F32), vmem((INNER, chunks, rank, CHUNK), F32),
        vmem((INNER, n_x, chunks, rank, CHUNK), F32),
        vmem((n_snap, rw, rank), F32), vmem((n_snap - 1, rw, rank), F32),
        dma((2 + width // STEP,)),
        dma((2, n_pts - 1)), dma((2, n_pts - 1)),
        dma((2, n_snap - 1)), dma((2, n_snap - 1)),
        dma((2 * INNER, chunks)), dma((2 * INNER, chunks)),
        dma((INNER, chunks, n_x - 1)), dma((INNER, chunks, n_x - 1)),
        dma((INNER + 1, n_dev - 1)), dma((INNER + 1, n_dev - 1)),
        dma((2, n_snap - 1)), dma((2, n_snap - 1)),
    ]
    modes, coefs = pl.pallas_call(
        functools.partial(kernel, n_pts, n_snap),
        out_shape=(jax.ShapeDtypeStruct((rows, rank), F32), jax.ShapeDtypeStruct((rank, width), F32)),
        in_specs=[pl.BlockSpec(memory_space=pl.ANY)] * 3,
        out_specs=(pl.BlockSpec(memory_space=vmem), pl.BlockSpec(memory_space=vmem)),
        scratch_shapes=scratch,
        compiler_params=pltpu.CompilerParams(collective_id=0, has_side_effects=True, vmem_limit_bytes=60 * 1024 * 1024),
    )(snapshots, modes_init, coefs_init)
    return modes, coefs * jnp.sqrt(jnp.float32(points))


def solution(mesh):
    in_specs = (P("pts", "snap"), P("pts", None), P(None, "snap"))
    out_specs = (P("pts", None), P(None, "snap"))
    body = functools.partial(shards, mesh.shape["pts"], mesh.shape["snap"])
    return jax.shard_map(body, mesh=mesh, in_specs=in_specs, out_specs=out_specs, check_vma=False)
```

```python
import functools

import jax
import jax.numpy as jnp
from jax import lax
from jax.experimental import pallas as pl
from jax.experimental.pallas import tpu as pltpu
from jax.sharding import PartitionSpec as P

OUTER = 2
INNER = 2
PIVOTS = 16
CHUNK = 128
STEP = 256

HUBER = 1.345
RIDGE = 0.01

F32 = jnp.float32
BF16 = jnp.bfloat16
MESH = pl.DeviceIdType.MESH


def split(x):
    hi = x.astype(BF16)
    lo = (x - hi.astype(F32)).astype(BF16)
    return hi, lo


def split3(x):
    hi = x.astype(BF16)
    rest = x - hi.astype(F32)
    mid = rest.astype(BF16)
    lo = (rest - mid.astype(F32)).astype(BF16)
    return hi, mid, lo


def dot(a, b):
    return jnp.dot(a, b, preferred_element_type=F32)


def quads(x):
    r, c = x.shape[0] // 2, x.shape[1] // 2
    return (x[:r, :c] + x[:r, c:]) + (x[r:, :c] + x[r:, c:])


def pts_peer(me, j, n):
    if n % 2:
        return lax.rem(me + j, n)
    x, c = me // 2, lax.rem(me, 2)
    return lax.rem(x + j // 2, n // 2) * 2 + lax.rem(c + lax.rem(j, 2), 2)


def snap_peer(me, j, n):
    return lax.rem(me + j, n)


def kernel(n_pts, n_snap, s_hbm, m_hbm, c_hbm, m_out, c_out,
           s, e, mcat, mtcat, ccat, ctcat, sq,
           gpart, gslots, gred, gfull, hpart, hslots, hred, hfull,
           lslots, cpart, cslots, xslots, ypart, yslots, zpart, zslots,
           load_sem, p_send, p_recv, s_send, s_recv, c_send, c_recv, x_send, x_recv,
           l_send, l_recv, y_send, y_recv, z_send, z_recv):
    rows, width = s.shape
    rank = m_out.shape[1]
    pme = lax.axis_index("pts")
    sme = lax.axis_index("snap")
    n_dev = n_pts * n_snap
    me = pme * n_snap + sme
    rw = rows // n_snap
    half = width // 2
    chunks = half // CHUNK
    n_x, n_z = n_pts // 2, n_snap // 2
    px, core = pme // 2, lax.rem(pme, 2)
    sz, sy = sme // 2, lax.rem(sme, 2)
    gw = rank // n_pts
    hw = rank // n_snap
    count = float(rows * n_pts * width * n_snap)
    loads = width // STEP

    def offset(d):
        dx, dc, dz, dy = d
        return {"pts": lax.rem(px + dx, n_x) * 2 + lax.rem(core + dc, 2),
                "snap": lax.rem(sz + dz, n_z) * 2 + lax.rem(sy + dy, 2)}

    def hops(d):
        dx, dc, dz, dy = d
        return min(dx, n_x - dx) + dy + min(dz, n_z - dz) + 0.1 * dc
    others = [(dx, dc, dz, dy) for dx in range(n_x) for dc in range(2) for dz in range(n_z) for dy in range(2)][1:]
    others.sort(key=lambda d: -hops(d))

    barrier = pltpu.get_barrier_semaphore()
    for d in others:
        pl.semaphore_signal(barrier, inc=1, device_id=offset(d), device_id_type=MESH)

    def load_cols(j):
        cols = pl.ds(j * STEP, STEP)
        return pltpu.make_async_copy(s_hbm.at[:, cols], s.at[:, cols], load_sem.at[2 + j])
    load_m = pltpu.make_async_copy(m_hbm, m_out, load_sem.at[0])
    load_c = pltpu.make_async_copy(c_hbm, c_out, load_sem.at[1])
    load_m.start()
    load_c.start()
    for j in range(loads):
        load_cols(j).start()

    def pcopy(site, j, src, dst):
        return pltpu.make_async_remote_copy(
            src_ref=src, dst_ref=dst, send_sem=p_send.at[site, j - 1], recv_sem=p_recv.at[site, j - 1],
            device_id={"pts": pts_peer(pme, j, n_pts)}, device_id_type=MESH)

    def scopy(site, j, src, dst):
        return pltpu.make_async_remote_copy(
            src_ref=src, dst_ref=dst, send_sem=s_send.at[site, j - 1], recv_sem=s_recv.at[site, j - 1],
            device_id={"snap": snap_peer(sme, j, n_snap)}, device_id_type=MESH)

    def ccopy(site, k, src, dst):
        return pltpu.make_async_remote_copy(
            src_ref=src, dst_ref=dst, send_sem=c_send.at[site, k], recv_sem=c_recv.at[site, k],
            device_id={"pts": px * 2 + 1 - core}, device_id_type=MESH)

    def xcopy(site, k, d):
        ref = xslots.at[site, px, k]
        return pltpu.make_async_remote_copy(
            src_ref=ref, dst_ref=ref, send_sem=x_send.at[site, k, d - 1], recv_sem=x_recv.at[site, k, d - 1],
            device_id={"pts": lax.rem(px + d, n_x) * 2 + core}, device_id_type=MESH)

    def lcopy(use, i):
        ref = lslots.at[use, pl.ds(me, 1)]
        return pltpu.make_async_remote_copy(
            src_ref=ref, dst_ref=ref, send_sem=l_send.at[use, i], recv_sem=l_recv.at[use, i],
            device_id=offset(others[i]), device_id_type=MESH)

    def ycopy(site, d, src, dst):
        return pltpu.make_async_remote_copy(
            src_ref=src, dst_ref=dst, send_sem=y_send.at[site, d], recv_sem=y_recv.at[site, d],
            device_id={"snap": sz * 2 + 1 - sy}, device_id_type=MESH)

    def zcopy(site, d, src, dst):
        return pltpu.make_async_remote_copy(
            src_ref=src, dst_ref=dst, send_sem=z_send.at[site, d - 1], recv_sem=z_recv.at[site, d - 1],
            device_id={"snap": lax.rem(sz + d, n_z) * 2 + sy}, device_id_type=MESH)

    def row_block(d, which):
        return pl.ds(pl.multiple_of((lax.rem(sz + d, n_z) * 2 + which) * rw, rw), rw)

    def far(t):
        return n_z // 2 + ((t + 1) // 2) * (1 - 2 * (t % 2))

    def col_chunk(which, k):
        return pl.ds(pl.multiple_of(which * half + k * CHUNK, CHUNK), CHUNK)

    def start(copies):
        for copy in copies:
            copy.start()

    def finish(copies):
        for copy in copies:
            copy.wait_recv()
        for copy in copies:
            copy.wait_send()

    def prepare_rows(part):
        hi, lo = split(m_out[part, :])
        mcat[part, :rank] = hi
        mcat[part, rank:] = lo

    def prepare_mt():
        hi, lo = split(m_out[...].T)
        mtcat[:rank, :] = hi
        mtcat[rank:, :] = lo

    def prepare_cols(cols, value):
        hi, lo = split(value)
        ccat[:rank, cols] = hi
        ccat[rank:, cols] = lo

    def prepare_ct(cols, value):
        hi, lo = split(value.T)
        ctcat[cols, :rank] = hi
        ctcat[cols, rank:] = lo

    def sweep(ref, base, steps):
        sub = lax.broadcasted_iota(jnp.int32, (PIVOTS, rank), 0)
        lane = lax.broadcasted_iota(jnp.int32, (PIVOTS, rank), 1)
        wide = lax.broadcasted_iota(jnp.int32, (rank, rank), 1)
        side = sub[:, :1]

        def body(t, carry):
            k = (base + t) * PIVOTS
            rws = pl.ds(pl.multiple_of(k, PIVOTS), PIVOTS)
            before = ref[rws, :]
            after = before
            cols = [jnp.sum(jnp.where(lane == k + p, before, 0.0), axis=1, keepdims=True) for p in range(PIVOTS)]
            for p in range(PIVOTS):
                col = cols[p]
                inv = 1.0 / col[p:p + 1, :]
                row = after[p:p + 1, :] * inv
                for q in range(p + 1, PIVOTS):
                    f = cols[q][p:p + 1, :] * inv
                    cols[q] = jnp.where(side == p, f, cols[q] - col * f)
                after = jnp.where(lane == k + p, col * inv, after - col * row)
                after = jnp.where(sub == p, jnp.where(lane == k + p, -inv, row), after)
            h, m, l = split3(before)
            a, b, c = split3(after)
            change = lax.dot_general(
                jnp.concatenate([h, h, m, h, m, l], 0), jnp.concatenate([a, b, a, c, b, a], 0),
                (((0,), (0,)), ((), ())), preferred_element_type=F32)
            ref[...] = jnp.where((wide >= k) & (wide < k + PIVOTS), 0.0, ref[...]) - change
            ref[rws, :] = after
            return carry
        with jax.named_scope("sweep"):
            lax.fori_loop(0, steps, body, 0)

    def errors(part, n_rows, cols):
        hi, lo = mcat[part, :rank], mcat[part, rank:]
        c = ccat[:, cols]
        fit = dot(jnp.concatenate([hi, hi], 1), c) + dot(jnp.concatenate([lo, lo], 1), c)
        err = s[part, cols] - fit
        e[part, cols] = err
        sq[...] += jnp.sum((err * err).reshape(n_rows // 8, 8, STEP), axis=0)

    def step_cols(j):
        return pl.ds(pl.multiple_of(j * STEP, STEP), STEP)

    def error_rows(part):
        hi, lo = mcat[part, :rank], mcat[part, rank:]
        both = jnp.concatenate([jnp.concatenate([hi, hi], 1), jnp.concatenate([lo, lo], 1)], 0)
        for j in range(loads):
            cols = pl.ds(j * STEP, STEP)
            fit = dot(both, ccat[:, cols])
            err = s[part, cols] - (fit[:rw] + fit[rw:])
            e[part, cols] = err
            sq[...] += jnp.sum((err * err).reshape(rw // 8, 8, STEP), axis=0)

    def send_limit(use):
        acc = sq[:, :128]
        for k in range(1, STEP // 128):
            acc = acc + sq[:, k * 128:(k + 1) * 128]
        lslots[use, pl.ds(me, 1), :] = jnp.sum(acc, axis=0, keepdims=True)
        start([lcopy(use, i) for i in range(n_dev - 1)])
        sq[...] = jnp.zeros_like(sq)

    def get_limit(use):
        with jax.named_scope("limit"):
            for i in reversed(range(n_dev - 1)):
                lcopy(use, i).wait_recv()
        total = jnp.sum(jnp.sum(lslots[use], axis=0, keepdims=True), axis=1, keepdims=True)
        for i in range(n_dev - 1):
            lcopy(use, i).wait_send()
        return HUBER * jnp.sqrt(total / count + 1e-06)

    eye = (lax.broadcasted_iota(jnp.int32, (rank, rank), 0)
           == lax.broadcasted_iota(jnp.int32, (rank, rank), 1)).astype(F32) * RIDGE

    grs = [pcopy(0, j, gpart.at[pl.ds(pts_peer(pme, j, n_pts) * gw, gw)], gslots.at[j - 1]) for j in range(1, n_pts)]
    gag = [pcopy(1, j, gred, gfull.at[pl.ds(pme * gw, gw)]) for j in range(1, n_pts)]
    hrs = [scopy(0, j, hpart.at[pl.ds(snap_peer(sme, j, n_snap) * hw, hw)], hslots.at[j - 1]) for j in range(1, n_snap)]
    hag = [scopy(1, j, hred, hfull.at[pl.ds(sme * hw, hw)]) for j in range(1, n_snap)]
    own_rows = pl.ds(pl.multiple_of(sme * rw, rw), rw)

    def gram_part():
        prepare_mt()
        gpart[...] = quads(dot(mtcat[...], mcat[...]))

    sq[...] = jnp.zeros_like(sq)
    load_m.wait()
    prepare_rows(pl.ds(0, rows))
    gram_part()
    load_c.wait()
    prepare_cols(pl.ds(0, width), c_out[...])
    with jax.named_scope("barrier"):
        pl.semaphore_wait(barrier, n_dev - 1)
    start(grs)
    for j in range(loads):
        load_cols(j).wait()
    with jax.named_scope("err0"):
        def first(j, carry):
            errors(pl.ds(0, rows), rows, step_cols(j))
            return carry
        lax.fori_loop(0, loads, first, 0)
    send_limit(0)

    def outer(o, carry):
        more = o < OUTER - 1
        finish(grs)
        own = gpart[pl.ds(pme * gw, gw), :]
        for j in range(1, n_pts):
            own = own + gslots[j - 1]
        gred[...] = own
        gfull[pl.ds(pme * gw, gw), :] = own
        start(gag)

        for inner in range(INNER):
            if inner == 0:
                @pl.when(o == 0)
                def _():
                    finish(gag)
                    gfull[...] = gfull[...] + eye
                    sweep(gfull, 0, rank // PIVOTS // 2)
            limit = get_limit(inner)

            def give(k):
                return ccopy(inner, k, cpart.at[k], cslots.at[inner, k])

            def spread(k):
                ref = c_out.at[:, col_chunk(core, k)]
                return ccopy(INNER + inner, k, ref, ref)

            def products(t, carry):
                last = t == 2 * chunks - 1
                theirs = (t == 0) | ((lax.rem(t, 2) == 1) & (t < 2 * chunks - 1))
                k = jnp.where(theirs, (t + 1) // 2, jnp.where(last, chunks - 1, t // 2 - 1))
                which = jnp.where(theirs, 1 - core, core)
                hi, lo = split(jnp.clip(e[:, col_chunk(which, k)], -limit, limit))
                value = quads(dot(mtcat[...], jnp.concatenate([hi, lo], 1)))

                @pl.when(theirs)
                def _():
                    cpart[k] = value
                    give(k).start()

                @pl.when(jnp.logical_not(theirs))
                def _():
                    give(k).wait_recv()
                    xslots[inner, px, k] = value + cslots[inner, k]
                    for d in range(1, n_x):
                        xcopy(inner, k, d).start()
                return carry
            with jax.named_scope("products"):
                lax.fori_loop(0, 2 * chunks, products, 0)
            if inner == 0:
                @pl.when(o > 0)
                def _():
                    finish(gag)
                    gfull[...] = gfull[...] + eye
                    sweep(gfull, 0, rank // PIVOTS // 2)
                sweep(gfull, rank // PIVOTS // 2, rank // PIVOTS // 2)

            def update(t, carry):
                j = t // 2
                mine = lax.rem(t, 2) == 0
                per = STEP // CHUNK

                def own_cols(i, carry):
                    k = j * per + i
                    for d in range(1, n_x):
                        xcopy(inner, k, d).wait_recv()
                    share = xslots[inner, 0, k]
                    for x in range(1, n_x):
                        share = share + xslots[inner, x, k]
                    step = jnp.dot(gfull[...], share, preferred_element_type=F32, precision=lax.Precision.HIGHEST)
                    cols = col_chunk(core, k)
                    value = c_out[:, cols] - step
                    c_out[:, cols] = value
                    spread(k).start()
                    prepare_cols(cols, value)
                    if inner == INNER - 1:
                        prepare_ct(cols, value)
                    return carry

                def their_cols(i, carry):
                    k = j * per + i
                    spread(k).wait_recv()
                    cols = col_chunk(1 - core, k)
                    value = c_out[:, cols]
                    prepare_cols(cols, value)
                    if inner == INNER - 1:
                        prepare_ct(cols, value)
                    return carry

                @pl.when(mine)
                def _():
                    lax.fori_loop(0, per, own_cols, 0)

                @pl.when(jnp.logical_not(mine))
                def _():
                    lax.fori_loop(0, per, their_cols, 0)
                which = jnp.where(mine, core, 1 - core)
                with jax.named_scope("errchunk"):
                    errors(pl.ds(0, rows), rows, pl.ds(pl.multiple_of(which * half + j * STEP, STEP), STEP))
                return carry
            with jax.named_scope("update"):
                lax.fori_loop(0, loads, update, 0)
            send_limit(inner + 1)

            def settle(k, carry):
                spread(k).wait_send()
                give(k).wait_send()
                for d in range(1, n_x):
                    xcopy(inner, k, d).wait_send()
                return carry
            lax.fori_loop(0, chunks, settle, 0)

        with jax.named_scope("hpart"):
            hpart[...] = quads(dot(ccat[...], ctcat[...]))
            start(hrs)
        limit = get_limit(INNER)

        def moment(part):
            hi, lo = split(jnp.clip(e[part, :], -limit, limit))
            return quads(dot(jnp.concatenate([hi, lo], 0), ctcat[...]))

        def over_y(d):
            return ycopy(0, d, ypart.at[d], yslots.at[d])

        def over_z(d):
            return zcopy(0, d, zpart.at[d], zslots.at[d - 1])

        def moments(t, carry):
            theirs = t < n_z
            d = far(t % n_z)
            value = moment(row_block(d, jnp.where(theirs, 1 - sy, sy)))

            @pl.when(theirs)
            def _():
                ypart[d] = value
                over_y(d).start()

            @pl.when(jnp.logical_not(theirs))
            def _():
                zpart[d] = value

            @pl.when(t == 0)
            def _():
                finish(hrs)
                own = hpart[pl.ds(sme * hw, hw), :]
                for j in range(1, n_snap):
                    own = own + hslots[j - 1]
                hred[...] = own
                hfull[pl.ds(sme * hw, hw), :] = own
                start(hag)
            return carry
        with jax.named_scope("moments"):
            lax.fori_loop(0, 2 * n_z, moments, 0)
        steps = rank // PIVOTS

        def forward(t, carry):
            d = far(t)
            with jax.named_scope("ywait"):
                over_y(d).wait_recv()
            zpart[d] = zpart[d] + yslots[d]

            @pl.when(t < n_z - 1)
            def _():
                over_z(d).start()

            @pl.when(t == 0)
            def _():
                with jax.named_scope("hag"):
                    finish(hag)
                hfull[...] = hfull[...] + eye
            sweep(hfull, t * (steps // n_z), steps // n_z)
            return carry
        lax.fori_loop(0, n_z, forward, 0)
        sweep(hfull, steps // n_z * n_z, steps - steps // n_z * n_z)
        with jax.named_scope("zwait"):
            for d in range(1, n_z):
                over_z(d).wait_recv()
        share = zpart[0]
        for d in range(1, n_z):
            share = share + zslots[d - 1]
        step = jnp.dot(share, hfull[...], preferred_element_type=F32, precision=lax.Precision.HIGHEST)
        m_out[own_rows, :] = m_out[own_rows, :] - step
        own_ref = m_out.at[own_rows]
        order = [far(t) for t in range(n_z - 1)]
        start([zcopy(1, d, own_ref, own_ref) for d in order])
        ycopy(1, 0, own_ref, own_ref).start()

        def pass_on(d):
            ref = m_out.at[row_block(n_z - d, sy)]
            return ycopy(1, d, ref, ref)

        def take(part):
            @pl.when(more)
            def _():
                prepare_rows(part)
                error_rows(part)
        take(own_rows)
        with jax.named_scope("gatherz"):
            for d in order[::-1]:
                zcopy(1, d, own_ref, own_ref).wait_recv()
                pass_on(d).start()

        def near(u, carry):
            take(row_block(u, sy))
            return carry
        with jax.named_scope("near"):
            lax.fori_loop(1, n_z, near, 0)

        def other(u, carry):
            d = jnp.where(u == 0, 0, far(n_z - 1 - u))
            with jax.named_scope("gathery"):
                pass_on(d).wait_recv()
            take(row_block(n_z - d, 1 - sy))
            return carry
        with jax.named_scope("other"):
            lax.fori_loop(0, n_z, other, 0)

        @pl.when(more)
        def _():
            send_limit(0)
            gram_part()
            start(grs)
        ycopy(1, 0, own_ref, own_ref).wait_send()
        over_y(0).wait_send()
        for d in range(1, n_z):
            pass_on(d).wait_send()
            over_y(d).wait_send()
            over_z(d).wait_send()
            zcopy(1, d, own_ref, own_ref).wait_send()
        return carry
    lax.fori_loop(0, OUTER, outer, 0)


def shards(n_pts, n_snap, snapshots, modes_init, coefs_init):
    rows, width = snapshots.shape
    rank = modes_init.shape[1]
    rw, gw, hw = rows // n_snap, rank // n_pts, rank // n_snap
    chunks, n_x, n_z, n_dev = width // 2 // CHUNK, n_pts // 2, n_snap // 2, n_pts * n_snap
    points = float(rows * n_pts)
    vmem, dma = pltpu.VMEM, pltpu.SemaphoreType.DMA
    scratch = [
        vmem((rows, width), F32), vmem((rows, width), F32),
        vmem((rows, 2 * rank), BF16), vmem((2 * rank, rows), BF16),
        vmem((2 * rank, width), BF16), vmem((width, 2 * rank), BF16),
        vmem((8, STEP), F32),
        vmem((rank, rank), F32), vmem((n_pts - 1, gw, rank), F32), vmem((gw, rank), F32), vmem((rank, rank), F32),
        vmem((rank, rank), F32), vmem((n_snap - 1, hw, rank), F32), vmem((hw, rank), F32), vmem((rank, rank), F32),
        vmem((INNER + 1, n_dev, 128), F32),
        vmem((chunks, rank, CHUNK), F32), vmem((INNER, chunks, rank, CHUNK), F32),
        vmem((INNER, n_x, chunks, rank, CHUNK), F32),
        vmem((n_z, rw, rank), F32), vmem((n_z, rw, rank), F32),
        vmem((n_z, rw, rank), F32), vmem((n_z - 1, rw, rank), F32),
        dma((2 + width // STEP,)),
        dma((2, n_pts - 1)), dma((2, n_pts - 1)),
        dma((2, n_snap - 1)), dma((2, n_snap - 1)),
        dma((2 * INNER, chunks)), dma((2 * INNER, chunks)),
        dma((INNER, chunks, n_x - 1)), dma((INNER, chunks, n_x - 1)),
        dma((INNER + 1, n_dev - 1)), dma((INNER + 1, n_dev - 1)),
        dma((2, n_z)), dma((2, n_z)),
        dma((2, n_z - 1)), dma((2, n_z - 1)),
    ]
    modes, coefs = pl.pallas_call(
        functools.partial(kernel, n_pts, n_snap),
        out_shape=(jax.ShapeDtypeStruct((rows, rank), F32), jax.ShapeDtypeStruct((rank, width), F32)),
        in_specs=[pl.BlockSpec(memory_space=pl.ANY)] * 3,
        out_specs=(pl.BlockSpec(memory_space=vmem), pl.BlockSpec(memory_space=vmem)),
        scratch_shapes=scratch,
        compiler_params=pltpu.CompilerParams(collective_id=0, has_side_effects=True, vmem_limit_bytes=60 * 1024 * 1024),
    )(snapshots, modes_init, coefs_init)
    return modes, coefs * jnp.sqrt(jnp.float32(points))


def solution(mesh):
    in_specs = (P("pts", "snap"), P("pts", None), P(None, "snap"))
    out_specs = (P("pts", None), P(None, "snap"))
    body = functools.partial(shards, mesh.shape["pts"], mesh.shape["snap"])
    return jax.shard_map(body, mesh=mesh, in_specs=in_specs, out_specs=out_specs, check_vma=False)
```

```python
import functools

import jax
import jax.numpy as jnp
from jax import lax
from jax.experimental import pallas as pl
from jax.experimental.pallas import tpu as pltpu
from jax.sharding import PartitionSpec as P

OUTER = 2
INNER = 2
PIVOTS = 16
CHUNK = 128
STEP = 256

HUBER = 1.345
RIDGE = 0.01

F32 = jnp.float32
BF16 = jnp.bfloat16
MESH = pl.DeviceIdType.MESH


def split(x):
    hi = x.astype(BF16)
    lo = (x - hi.astype(F32)).astype(BF16)
    return hi, lo


def split3(x):
    hi = x.astype(BF16)
    rest = x - hi.astype(F32)
    mid = rest.astype(BF16)
    lo = (rest - mid.astype(F32)).astype(BF16)
    return hi, mid, lo


def dot(a, b):
    return jnp.dot(a, b, preferred_element_type=F32)


def quads(x):
    r, c = x.shape[0] // 2, x.shape[1] // 2
    return (x[:r, :c] + x[:r, c:]) + (x[r:, :c] + x[r:, c:])


def pts_peer(me, j, n):
    if n % 2:
        return lax.rem(me + j, n)
    x, c = me // 2, lax.rem(me, 2)
    return lax.rem(x + j // 2, n // 2) * 2 + lax.rem(c + lax.rem(j, 2), 2)


def snap_peer(me, j, n):
    return lax.rem(me + j, n)


def kernel(n_pts, n_snap, s_hbm, m_hbm, c_hbm, m_out, c_out,
           s, e, mcat, mtcat, ccat, ctcat, sq,
           gpart, gslots, gred, gfull, hpart, hslots, hred, hfull,
           lslots, cpart, cslots, xslots, ypart, yslots, zpart, zslots,
           load_sem, p_send, p_recv, s_send, s_recv, c_send, c_recv, x_send, x_recv,
           l_send, l_recv, y_send, y_recv, z_send, z_recv):
    rows, width = s.shape
    rank = m_out.shape[1]
    pme = lax.axis_index("pts")
    sme = lax.axis_index("snap")
    n_dev = n_pts * n_snap
    me = pme * n_snap + sme
    rw = rows // n_snap
    half = width // 2
    chunks = half // CHUNK
    n_x, n_z = n_pts // 2, n_snap // 2
    px, core = pme // 2, lax.rem(pme, 2)
    sz, sy = sme // 2, lax.rem(sme, 2)
    gw = rank // n_pts
    hw = rank // n_snap
    count = float(rows * n_pts * width * n_snap)
    loads = width // STEP

    def offset(d):
        dx, dc, dz, dy = d
        return {"pts": lax.rem(px + dx, n_x) * 2 + lax.rem(core + dc, 2),
                "snap": lax.rem(sz + dz, n_z) * 2 + lax.rem(sy + dy, 2)}

    def hops(d):
        dx, dc, dz, dy = d
        return min(dx, n_x - dx) + dy + min(dz, n_z - dz) + 0.1 * dc
    others = [(dx, dc, dz, dy) for dx in range(n_x) for dc in range(2) for dz in range(n_z) for dy in range(2)][1:]
    others.sort(key=lambda d: -hops(d))

    barrier = pltpu.get_barrier_semaphore()
    for d in others:
        pl.semaphore_signal(barrier, inc=1, device_id=offset(d), device_id_type=MESH)

    def step_cols(j):
        return pl.ds(pl.multiple_of(j * STEP, STEP), STEP)

    def load_cols(j):
        cols = step_cols(j)
        return pltpu.make_async_copy(s_hbm.at[:, cols], s.at[:, cols], load_sem.at[2 + j])
    load_m = pltpu.make_async_copy(m_hbm, m_out, load_sem.at[0])
    load_c = pltpu.make_async_copy(c_hbm, c_out, load_sem.at[1])
    load_m.start()
    load_c.start()
    for j in range(loads):
        load_cols(j).start()

    def pcopy(site, j, src, dst):
        return pltpu.make_async_remote_copy(
            src_ref=src, dst_ref=dst, send_sem=p_send.at[site, j - 1], recv_sem=p_recv.at[site, j - 1],
            device_id={"pts": pts_peer(pme, j, n_pts)}, device_id_type=MESH)

    def scopy(site, j, src, dst):
        return pltpu.make_async_remote_copy(
            src_ref=src, dst_ref=dst, send_sem=s_send.at[site, j - 1], recv_sem=s_recv.at[site, j - 1],
            device_id={"snap": snap_peer(sme, j, n_snap)}, device_id_type=MESH)

    def ccopy(site, k, src, dst):
        return pltpu.make_async_remote_copy(
            src_ref=src, dst_ref=dst, send_sem=c_send.at[site, k], recv_sem=c_recv.at[site, k],
            device_id={"pts": px * 2 + 1 - core}, device_id_type=MESH)

    def xcopy(site, k, d):
        ref = xslots.at[site, px, k]
        return pltpu.make_async_remote_copy(
            src_ref=ref, dst_ref=ref, send_sem=x_send.at[k, d - 1], recv_sem=x_recv.at[k, d - 1],
            device_id={"pts": lax.rem(px + d, n_x) * 2 + core}, device_id_type=MESH)

    def lcopy(use, i):
        ref = lslots.at[use, pl.ds(me, 1)]
        return pltpu.make_async_remote_copy(
            src_ref=ref, dst_ref=ref, send_sem=l_send.at[use], recv_sem=l_recv.at[use],
            device_id=offset(others[i]), device_id_type=MESH)

    def lwait(use):
        ref = lslots.at[use, pl.ds(0, n_dev - 1)]
        return pltpu.make_async_remote_copy(
            src_ref=ref, dst_ref=ref, send_sem=l_send.at[use], recv_sem=l_recv.at[use],
            device_id=offset(others[0]), device_id_type=MESH)

    def ycopy(site, d, src, dst):
        return pltpu.make_async_remote_copy(
            src_ref=src, dst_ref=dst, send_sem=y_send.at[site, d], recv_sem=y_recv.at[site, d],
            device_id={"snap": sz * 2 + 1 - sy}, device_id_type=MESH)

    def zcopy(site, d, src, dst):
        return pltpu.make_async_remote_copy(
            src_ref=src, dst_ref=dst, send_sem=z_send.at[site, d - 1], recv_sem=z_recv.at[site, d - 1],
            device_id={"snap": lax.rem(sz + d, n_z) * 2 + sy}, device_id_type=MESH)

    def row_block(d, which):
        return pl.ds(pl.multiple_of((lax.rem(sz + d, n_z) * 2 + which) * rw, rw), rw)

    def far(t):
        return n_z // 2 + ((t + 1) // 2) * (1 - 2 * (t % 2))

    def col_chunk(which, k):
        return pl.ds(pl.multiple_of(which * half + k * CHUNK, CHUNK), CHUNK)

    def start(copies):
        for copy in copies:
            copy.start()

    def finish(copies):
        for copy in copies:
            copy.wait_recv()
        for copy in copies:
            copy.wait_send()

    def prepare_rows(part):
        hi, lo = split(m_out[part, :])
        mcat[part, :rank] = hi
        mcat[part, rank:] = lo

    def prepare_mt():
        hi, lo = split(m_out[...].T)
        mtcat[:rank, :] = hi
        mtcat[rank:, :] = lo

    def prepare_cols(cols, value):
        hi, lo = split(value)
        ccat[:rank, cols] = hi
        ccat[rank:, cols] = lo

    def prepare_ct(cols, value):
        hi, lo = split(value.T)
        ctcat[cols, :rank] = hi
        ctcat[cols, rank:] = lo

    def sweep(ref, base, steps):
        sub = lax.broadcasted_iota(jnp.int32, (PIVOTS, rank), 0)
        lane = lax.broadcasted_iota(jnp.int32, (PIVOTS, rank), 1)
        wide = lax.broadcasted_iota(jnp.int32, (rank, rank), 1)
        side = sub[:, :1]

        def body(t, carry):
            k = (base + t) * PIVOTS
            rws = pl.ds(pl.multiple_of(k, PIVOTS), PIVOTS)
            before = ref[rws, :]
            after = before
            cols = [jnp.sum(jnp.where(lane == k + p, before, 0.0), axis=1, keepdims=True) for p in range(PIVOTS)]
            for p in range(PIVOTS):
                col = cols[p]
                inv = 1.0 / col[p:p + 1, :]
                row = after[p:p + 1, :] * inv
                for q in range(p + 1, PIVOTS):
                    f = cols[q][p:p + 1, :] * inv
                    cols[q] = jnp.where(side == p, f, cols[q] - col * f)
                after = jnp.where(lane == k + p, col * inv, after - col * row)
                after = jnp.where(sub == p, jnp.where(lane == k + p, -inv, row), after)
            h, m, l = split3(before)
            a, b, c = split3(after)
            change = lax.dot_general(
                jnp.concatenate([h, h, m, h, m, l], 0), jnp.concatenate([a, b, a, c, b, a], 0),
                (((0,), (0,)), ((), ())), preferred_element_type=F32)
            ref[...] = jnp.where((wide >= k) & (wide < k + PIVOTS), 0.0, ref[...]) - change
            ref[rws, :] = after
            return carry
        with jax.named_scope("sweep"):
            lax.fori_loop(0, steps, body, 0)

    def errors(part, n_rows, cols):
        hi, lo = mcat[part, :rank], mcat[part, rank:]
        c = ccat[:, cols]
        fit = dot(jnp.concatenate([hi, hi], 1), c) + dot(jnp.concatenate([lo, lo], 1), c)
        err = s[part, cols] - fit
        e[part, cols] = err
        sq[...] += jnp.sum((err * err).reshape(n_rows // 8, 8, STEP), axis=0)

    def error_rows(part):
        hi, lo = mcat[part, :rank], mcat[part, rank:]
        both = jnp.concatenate([jnp.concatenate([hi, hi], 1), jnp.concatenate([lo, lo], 1)], 0)
        for j in range(loads):
            cols = pl.ds(j * STEP, STEP)
            fit = dot(both, ccat[:, cols])
            err = s[part, cols] - (fit[:rw] + fit[rw:])
            e[part, cols] = err
            sq[...] += jnp.sum((err * err).reshape(rw // 8, 8, STEP), axis=0)

    def send_limit(use):
        acc = sq[:, :128]
        for k in range(1, STEP // 128):
            acc = acc + sq[:, k * 128:(k + 1) * 128]
        lslots[use, pl.ds(me, 1), :] = jnp.sum(acc, axis=0, keepdims=True)
        start([lcopy(use, i) for i in range(n_dev - 1)])
        sq[...] = jnp.zeros_like(sq)

    def get_limit(use):
        with jax.named_scope("limit"):
            lwait(use).wait_recv()
        total = jnp.sum(jnp.sum(lslots[use], axis=0, keepdims=True), axis=1, keepdims=True)
        lwait(use).wait_send()
        return HUBER * jnp.sqrt(total / count + 1e-06)

    eye = (lax.broadcasted_iota(jnp.int32, (rank, rank), 0)
           == lax.broadcasted_iota(jnp.int32, (rank, rank), 1)).astype(F32) * RIDGE

    grs = [pcopy(0, j, gpart.at[pl.ds(pts_peer(pme, j, n_pts) * gw, gw)], gslots.at[j - 1]) for j in range(1, n_pts)]
    gag = [pcopy(1, j, gred, gfull.at[pl.ds(pme * gw, gw)]) for j in range(1, n_pts)]
    hrs = [scopy(0, j, hpart.at[pl.ds(snap_peer(sme, j, n_snap) * hw, hw)], hslots.at[j - 1]) for j in range(1, n_snap)]
    hag = [scopy(1, j, hred, hfull.at[pl.ds(sme * hw, hw)]) for j in range(1, n_snap)]
    own_rows = pl.ds(pl.multiple_of(sme * rw, rw), rw)

    def gram_part():
        prepare_mt()
        gpart[...] = quads(dot(mtcat[...], mcat[...]))

    sq[...] = jnp.zeros_like(sq)
    load_m.wait()
    prepare_rows(pl.ds(0, rows))
    load_c.wait()
    prepare_cols(pl.ds(0, width), c_out[...])
    with jax.named_scope("err0"):
        def first(j, carry):
            load_cols(j).wait()
            errors(pl.ds(0, rows), rows, step_cols(j))
            return carry
        lax.fori_loop(0, loads, first, 0)
    with jax.named_scope("barrier"):
        pl.semaphore_wait(barrier, n_dev - 1)
    send_limit(0)
    gram_part()
    start(grs)

    def outer(o, carry):
        more = o < OUTER - 1
        with jax.named_scope("grs"):
            finish(grs)
        own = gpart[pl.ds(pme * gw, gw), :]
        for j in range(1, n_pts):
            own = own + gslots[j - 1]
        gred[...] = own
        gfull[pl.ds(pme * gw, gw), :] = own
        start(gag)

        for inner in range(INNER):
            limit = get_limit(inner)

            def give(k):
                return ccopy(0, k, cpart.at[k], cslots.at[inner, k])

            def spread(k):
                ref = c_out.at[:, col_chunk(core, k)]
                return ccopy(1, k, ref, ref)

            def products(t, carry):
                last = t == 2 * chunks - 1
                theirs = (t == 0) | ((lax.rem(t, 2) == 1) & (t < 2 * chunks - 1))
                k = jnp.where(theirs, (t + 1) // 2, jnp.where(last, chunks - 1, t // 2 - 1))
                which = jnp.where(theirs, 1 - core, core)
                hi, lo = split(jnp.clip(e[:, col_chunk(which, k)], -limit, limit))
                value = quads(dot(mtcat[...], jnp.concatenate([hi, lo], 1)))

                @pl.when(theirs)
                def _():
                    cpart[k] = value
                    give(k).start()

                @pl.when(jnp.logical_not(theirs))
                def _():
                    give(k).wait_recv()
                    xslots[inner, px, k] = value + cslots[inner, k]
                    for d in range(1, n_x):
                        xcopy(inner, k, d).start()
                return carry
            with jax.named_scope("products"):
                lax.fori_loop(0, 2 * chunks, products, 0)
            if inner == 0:
                with jax.named_scope("gag"):
                    finish(gag)
                gfull[...] = gfull[...] + eye
                sweep(gfull, 0, rank // PIVOTS)

            def update(t, carry):
                j = t // 2
                mine = lax.rem(t, 2) == 0
                per = STEP // CHUNK

                def own_cols(i, carry):
                    k = j * per + i
                    for d in range(1, n_x):
                        xcopy(inner, k, d).wait_recv()
                    share = xslots[inner, 0, k]
                    for x in range(1, n_x):
                        share = share + xslots[inner, x, k]
                    step = jnp.dot(gfull[...], share, preferred_element_type=F32, precision=lax.Precision.HIGHEST)
                    cols = col_chunk(core, k)
                    value = c_out[:, cols] - step
                    c_out[:, cols] = value
                    spread(k).start()
                    prepare_cols(cols, value)
                    if inner == INNER - 1:
                        prepare_ct(cols, value)
                    return carry

                def their_cols(i, carry):
                    k = j * per + i
                    spread(k).wait_recv()
                    cols = col_chunk(1 - core, k)
                    value = c_out[:, cols]
                    prepare_cols(cols, value)
                    if inner == INNER - 1:
                        prepare_ct(cols, value)
                    return carry

                @pl.when(mine)
                def _():
                    lax.fori_loop(0, per, own_cols, 0)

                @pl.when(jnp.logical_not(mine))
                def _():
                    lax.fori_loop(0, per, their_cols, 0)
                which = jnp.where(mine, core, 1 - core)
                with jax.named_scope("errchunk"):
                    errors(pl.ds(0, rows), rows, pl.ds(pl.multiple_of(which * half + j * STEP, STEP), STEP))
                return carry
            with jax.named_scope("update"):
                lax.fori_loop(0, loads, update, 0)
            send_limit(inner + 1)

            def settle(k, carry):
                spread(k).wait_send()
                give(k).wait_send()
                for d in range(1, n_x):
                    xcopy(inner, k, d).wait_send()
                return carry
            lax.fori_loop(0, chunks, settle, 0)

        @pl.when(jnp.logical_not(more))
        def _():
            c_out[...] = c_out[...] * jnp.sqrt(jnp.float32(rows * n_pts))
        with jax.named_scope("hpart"):
            hpart[...] = quads(dot(ccat[...], ctcat[...]))
            start(hrs)
        limit = get_limit(INNER)

        def moment(part):
            hi, lo = split(jnp.clip(e[part, :], -limit, limit))
            return quads(dot(jnp.concatenate([hi, lo], 0), ctcat[...]))

        def over_y(d):
            return ycopy(0, d, ypart.at[d], yslots.at[d])

        def over_z(d):
            return zcopy(0, d, zpart.at[d], zslots.at[d - 1])

        def moments(t, carry):
            theirs = t < n_z
            d = far(t % n_z)
            value = moment(row_block(d, jnp.where(theirs, 1 - sy, sy)))

            @pl.when(theirs)
            def _():
                ypart[d] = value
                over_y(d).start()

            @pl.when(jnp.logical_not(theirs))
            def _():
                zpart[d] = value

            @pl.when(t == 0)
            def _():
                finish(hrs)
                own = hpart[pl.ds(sme * hw, hw), :]
                for j in range(1, n_snap):
                    own = own + hslots[j - 1]
                hred[...] = own
                hfull[pl.ds(sme * hw, hw), :] = own
                start(hag)
            return carry
        with jax.named_scope("moments"):
            lax.fori_loop(0, 2 * n_z, moments, 0)
        steps = rank // PIVOTS

        def forward(t, carry):
            d = far(t)
            with jax.named_scope("ywait"):
                over_y(d).wait_recv()
            zpart[d] = zpart[d] + yslots[d]

            @pl.when(t < n_z - 1)
            def _():
                over_z(d).start()

            @pl.when(t == 0)
            def _():
                with jax.named_scope("hag"):
                    finish(hag)
                hfull[...] = hfull[...] + eye
            sweep(hfull, t * (steps // n_z), steps // n_z)
            return carry
        lax.fori_loop(0, n_z, forward, 0)
        sweep(hfull, steps // n_z * n_z, steps - steps // n_z * n_z)
        with jax.named_scope("zwait"):
            for d in range(1, n_z):
                over_z(d).wait_recv()
        share = zpart[0]
        for d in range(1, n_z):
            share = share + zslots[d - 1]
        step = jnp.dot(share, hfull[...], preferred_element_type=F32, precision=lax.Precision.HIGHEST)
        m_out[own_rows, :] = m_out[own_rows, :] - step
        own_ref = m_out.at[own_rows]
        order = [far(t) for t in range(n_z - 1)]
        start([zcopy(1, d, own_ref, own_ref) for d in order])
        ycopy(1, 0, own_ref, own_ref).start()

        def pass_on(d):
            ref = m_out.at[row_block(n_z - d, sy)]
            return ycopy(1, d, ref, ref)

        def take(part):
            @pl.when(more)
            def _():
                prepare_rows(part)
                error_rows(part)
        take(own_rows)
        with jax.named_scope("gatherz"):
            for d in order[::-1]:
                zcopy(1, d, own_ref, own_ref).wait_recv()
                pass_on(d).start()

        def near(u, carry):
            take(row_block(u, sy))
            return carry
        with jax.named_scope("near"):
            lax.fori_loop(1, n_z, near, 0)

        def other(u, carry):
            d = jnp.where(u == 0, 0, far(n_z - 1 - u))
            with jax.named_scope("gathery"):
                pass_on(d).wait_recv()
            take(row_block(n_z - d, 1 - sy))
            return carry
        with jax.named_scope("other"):
            lax.fori_loop(0, n_z, other, 0)

        @pl.when(more)
        def _():
            send_limit(0)
            gram_part()
            start(grs)
        with jax.named_scope("sends"):
            ycopy(1, 0, own_ref, own_ref).wait_send()
            over_y(0).wait_send()
            for d in range(1, n_z):
                pass_on(d).wait_send()
                over_y(d).wait_send()
                over_z(d).wait_send()
                zcopy(1, d, own_ref, own_ref).wait_send()
        return carry
    lax.fori_loop(0, OUTER, outer, 0)


def write_out(modes, amplitudes, m_hbm, a_hbm, sem):
    copies = [pltpu.make_async_copy(modes, m_hbm, sem.at[0]), pltpu.make_async_copy(amplitudes, a_hbm, sem.at[1])]
    for copy in copies:
        copy.start()
    for copy in copies:
        copy.wait()


def shards(n_pts, n_snap, snapshots, modes_init, coefs_init):
    rows, width = snapshots.shape
    rank = modes_init.shape[1]
    rw, gw, hw = rows // n_snap, rank // n_pts, rank // n_snap
    chunks, n_x, n_z, n_dev = width // 2 // CHUNK, n_pts // 2, n_snap // 2, n_pts * n_snap
    vmem, dma = pltpu.VMEM, pltpu.SemaphoreType.DMA
    scratch = [
        vmem((rows, width), F32), vmem((rows, width), F32),
        vmem((rows, 2 * rank), BF16), vmem((2 * rank, rows), BF16),
        vmem((2 * rank, width), BF16), vmem((width, 2 * rank), BF16),
        vmem((8, STEP), F32),
        vmem((rank, rank), F32), vmem((n_pts - 1, gw, rank), F32), vmem((gw, rank), F32), vmem((rank, rank), F32),
        vmem((rank, rank), F32), vmem((n_snap - 1, hw, rank), F32), vmem((hw, rank), F32), vmem((rank, rank), F32),
        vmem((INNER + 1, n_dev, 128), F32),
        vmem((chunks, rank, CHUNK), F32), vmem((INNER, chunks, rank, CHUNK), F32),
        vmem((INNER, n_x, chunks, rank, CHUNK), F32),
        vmem((n_z, rw, rank), F32), vmem((n_z, rw, rank), F32),
        vmem((n_z, rw, rank), F32), vmem((n_z - 1, rw, rank), F32),
        dma((2 + width // STEP,)),
        dma((2, n_pts - 1)), dma((2, n_pts - 1)),
        dma((2, n_snap - 1)), dma((2, n_snap - 1)),
        dma((2, chunks)), dma((2, chunks)),
        dma((chunks, n_x - 1)), dma((chunks, n_x - 1)),
        dma((INNER + 1,)), dma((INNER + 1,)),
        dma((2, n_z)), dma((2, n_z)),
        dma((2, n_z - 1)), dma((2, n_z - 1)),
    ]
    modes, coefs = pl.pallas_call(
        functools.partial(kernel, n_pts, n_snap),
        out_shape=(vmem((rows, rank), F32), vmem((rank, width), F32)),
        in_specs=[pl.BlockSpec(memory_space=pltpu.HBM)] * 3,
        out_specs=(pl.BlockSpec(memory_space=vmem), pl.BlockSpec(memory_space=vmem)),
        scratch_shapes=scratch,
        compiler_params=pltpu.CompilerParams(collective_id=0, has_side_effects=True, vmem_limit_bytes=67043328 - 5 * 256 * 1024),
    )(snapshots, modes_init, coefs_init)
    return pl.pallas_call(
        write_out,
        out_shape=(jax.ShapeDtypeStruct((rows, rank), F32), jax.ShapeDtypeStruct((rank, width), F32)),
        in_specs=[pl.BlockSpec(memory_space=pl.ANY)] * 2,
        out_specs=(pl.BlockSpec(memory_space=pltpu.HBM), pl.BlockSpec(memory_space=pltpu.HBM)),
        scratch_shapes=[dma((2,))],
    )(pltpu.with_memory_space_constraint(modes, vmem), pltpu.with_memory_space_constraint(coefs, vmem))


def solution(mesh):
    in_specs = (P("pts", "snap"), P("pts", None), P(None, "snap"))
    out_specs = (P("pts", None), P(None, "snap"))
    body = functools.partial(shards, mesh.shape["pts"], mesh.shape["snap"])
    return jax.shard_map(body, mesh=mesh, in_specs=in_specs, out_specs=out_specs, check_vma=False)
```

```python
import functools

import jax
import jax.numpy as jnp
from jax import lax
from jax.experimental import pallas as pl
from jax.experimental.pallas import tpu as pltpu
from jax.sharding import PartitionSpec as P

OUTER = 2
INNER = 2
PIVOTS = 16
CHUNK = 128
STEP = 256

HUBER = 1.345
RIDGE = 0.01

F32 = jnp.float32
BF16 = jnp.bfloat16
MESH = pl.DeviceIdType.MESH


def split(x):
    hi = x.astype(BF16)
    lo = (x - hi.astype(F32)).astype(BF16)
    return hi, lo


def split3(x):
    hi = x.astype(BF16)
    rest = x - hi.astype(F32)
    mid = rest.astype(BF16)
    lo = (rest - mid.astype(F32)).astype(BF16)
    return hi, mid, lo


def dot(a, b):
    return jnp.dot(a, b, preferred_element_type=F32)


def quads(x):
    r, c = x.shape[0] // 2, x.shape[1] // 2
    return (x[:r, :c] + x[:r, c:]) + (x[r:, :c] + x[r:, c:])


def pts_peer(me, j, n):
    if n % 2:
        return lax.rem(me + j, n)
    x, c = me // 2, lax.rem(me, 2)
    return lax.rem(x + j // 2, n // 2) * 2 + lax.rem(c + lax.rem(j, 2), 2)


def snap_peer(me, j, n):
    return lax.rem(me + j, n)


def kernel(n_pts, n_snap, s_hbm, m_hbm, c_hbm, m_out, c_out,
           s, e, mcat, mtcat, ccat, ctcat, sq,
           gpart, gslots, gred, gfull, hpart, hslots, hred, hfull,
           lslots, cpart, cslots, xslots, ypart, yslots, zpart, zslots,
           load_sem, p_send, p_recv, s_send, s_recv, c_send, c_recv, x_send, x_recv,
           l_send, l_recv, y_send, y_recv, z_send, z_recv):
    rows, width = s.shape
    rank = m_out.shape[1]
    pme = lax.axis_index("pts")
    sme = lax.axis_index("snap")
    n_dev = n_pts * n_snap
    me = pme * n_snap + sme
    rw = rows // n_snap
    half = width // 2
    chunks = half // CHUNK
    n_x, n_z = n_pts // 2, n_snap // 2
    px, core = pme // 2, lax.rem(pme, 2)
    sz, sy = sme // 2, lax.rem(sme, 2)
    gw = rank // n_pts
    hw = rank // n_snap
    count = float(rows * n_pts * width * n_snap)
    loads = width // STEP

    def offset(d):
        dx, dc, dz, dy = d
        return {"pts": lax.rem(px + dx, n_x) * 2 + lax.rem(core + dc, 2),
                "snap": lax.rem(sz + dz, n_z) * 2 + lax.rem(sy + dy, 2)}

    def hops(d):
        dx, dc, dz, dy = d
        return min(dx, n_x - dx) + dy + min(dz, n_z - dz) + 0.1 * dc
    others = [(dx, dc, dz, dy) for dx in range(n_x) for dc in range(2) for dz in range(n_z) for dy in range(2)][1:]
    others.sort(key=lambda d: -hops(d))

    barrier = pltpu.get_barrier_semaphore()
    for d in others:
        pl.semaphore_signal(barrier, inc=1, device_id=offset(d), device_id_type=MESH)

    def step_cols(j):
        return pl.ds(pl.multiple_of(j * STEP, STEP), STEP)

    def load_cols(j):
        cols = step_cols(j)
        return pltpu.make_async_copy(s_hbm.at[:, cols], s.at[:, cols], load_sem.at[2 + j])
    load_m = pltpu.make_async_copy(m_hbm, m_out, load_sem.at[0])
    load_c = pltpu.make_async_copy(c_hbm, c_out, load_sem.at[1])
    load_m.start()
    load_c.start()
    for j in range(loads):
        load_cols(j).start()

    def pcopy(site, j, src, dst):
        return pltpu.make_async_remote_copy(
            src_ref=src, dst_ref=dst, send_sem=p_send.at[site], recv_sem=p_recv.at[site],
            device_id={"pts": pts_peer(pme, j, n_pts)}, device_id_type=MESH)

    def scopy(site, j, src, dst):
        return pltpu.make_async_remote_copy(
            src_ref=src, dst_ref=dst, send_sem=s_send.at[site], recv_sem=s_recv.at[site],
            device_id={"snap": snap_peer(sme, j, n_snap)}, device_id_type=MESH)

    def ccopy(site, k, src, dst):
        return pltpu.make_async_remote_copy(
            src_ref=src, dst_ref=dst, send_sem=c_send.at[site], recv_sem=c_recv.at[site, k],
            device_id={"pts": px * 2 + 1 - core}, device_id_type=MESH)

    def xcopy(site, k, d):
        ref = xslots.at[site, px, k]
        return pltpu.make_async_remote_copy(
            src_ref=ref, dst_ref=ref, send_sem=x_send, recv_sem=x_recv.at[k, d - 1],
            device_id={"pts": lax.rem(px + d, n_x) * 2 + core}, device_id_type=MESH)

    def lcopy(use, i):
        ref = lslots.at[use, pl.ds(me, 1)]
        return pltpu.make_async_remote_copy(
            src_ref=ref, dst_ref=ref, send_sem=l_send.at[use], recv_sem=l_recv.at[use],
            device_id=offset(others[i]), device_id_type=MESH)

    def lwait(use):
        ref = lslots.at[use, pl.ds(0, n_dev - 1)]
        return pltpu.make_async_remote_copy(
            src_ref=ref, dst_ref=ref, send_sem=l_send.at[use], recv_sem=l_recv.at[use],
            device_id=offset(others[0]), device_id_type=MESH)

    def ycopy(site, d, src, dst):
        return pltpu.make_async_remote_copy(
            src_ref=src, dst_ref=dst, send_sem=y_send.at[site], recv_sem=y_recv.at[site, d],
            device_id={"snap": sz * 2 + 1 - sy}, device_id_type=MESH)

    def zcopy(site, d, src, dst):
        return pltpu.make_async_remote_copy(
            src_ref=src, dst_ref=dst, send_sem=z_send.at[site], recv_sem=z_recv.at[site, d - 1],
            device_id={"snap": lax.rem(sz + d, n_z) * 2 + sy}, device_id_type=MESH)

    def row_block(d, which):
        return pl.ds(pl.multiple_of((lax.rem(sz + d, n_z) * 2 + which) * rw, rw), rw)

    def far(t):
        return n_z // 2 + ((t + 1) // 2) * (1 - 2 * (t % 2))

    def col_chunk(which, k):
        return pl.ds(pl.multiple_of(which * half + k * CHUNK, CHUNK), CHUNK)

    def start(copies):
        for copy in copies:
            copy.start()

    def all_of(ref, send_sem, recv_sem):
        return pltpu.make_async_remote_copy(
            src_ref=ref, dst_ref=ref, send_sem=send_sem, recv_sem=recv_sem,
            device_id={"pts": px * 2 + 1 - core}, device_id_type=MESH)

    def finish(ref, send_sem, recv_sem):
        all_of(ref, send_sem, recv_sem).wait_recv()
        all_of(ref, send_sem, recv_sem).wait_send()

    def sent(ref, send_sem, recv_sem):
        all_of(ref, send_sem, recv_sem).wait_send()

    def prepare_rows(part):
        hi, lo = split(m_out[part, :])
        mcat[part, :rank] = hi
        mcat[part, rank:] = lo

    def prepare_mt():
        hi, lo = split(m_out[...].T)
        mtcat[:rank, :] = hi
        mtcat[rank:, :] = lo

    def prepare_cols(cols, value):
        hi, lo = split(value)
        ccat[:rank, cols] = hi
        ccat[rank:, cols] = lo

    def prepare_ct(cols, value):
        hi, lo = split(value.T)
        ctcat[cols, :rank] = hi
        ctcat[cols, rank:] = lo

    def sweep(ref, base, steps):
        sub = lax.broadcasted_iota(jnp.int32, (PIVOTS, rank), 0)
        lane = lax.broadcasted_iota(jnp.int32, (PIVOTS, rank), 1)
        wide = lax.broadcasted_iota(jnp.int32, (rank, rank), 1)
        side = sub[:, :1]

        def body(t, carry):
            k = (base + t) * PIVOTS
            rws = pl.ds(pl.multiple_of(k, PIVOTS), PIVOTS)
            before = ref[rws, :]
            after = before
            cols = [jnp.sum(jnp.where(lane == k + p, before, 0.0), axis=1, keepdims=True) for p in range(PIVOTS)]
            for p in range(PIVOTS):
                col = cols[p]
                inv = 1.0 / col[p:p + 1, :]
                row = after[p:p + 1, :] * inv
                for q in range(p + 1, PIVOTS):
                    f = cols[q][p:p + 1, :] * inv
                    cols[q] = jnp.where(side == p, f, cols[q] - col * f)
                after = jnp.where(lane == k + p, col * inv, after - col * row)
                after = jnp.where(sub == p, jnp.where(lane == k + p, -inv, row), after)
            h, m, l = split3(before)
            a, b, c = split3(after)
            change = lax.dot_general(
                jnp.concatenate([h, h, m, h, m, l], 0), jnp.concatenate([a, b, a, c, b, a], 0),
                (((0,), (0,)), ((), ())), preferred_element_type=F32)
            ref[...] = jnp.where((wide >= k) & (wide < k + PIVOTS), 0.0, ref[...]) - change
            ref[rws, :] = after
            return carry
        with jax.named_scope("sweep"):
            lax.fori_loop(0, steps, body, 0)

    def errors(part, n_rows, cols):
        hi, lo = mcat[part, :rank], mcat[part, rank:]
        c = ccat[:, cols]
        fit = dot(jnp.concatenate([hi, hi], 1), c) + dot(jnp.concatenate([lo, lo], 1), c)
        err = s[part, cols] - fit
        e[part, cols] = err
        sq[...] += jnp.sum((err * err).reshape(n_rows // 8, 8, STEP), axis=0)

    def error_rows(part):
        hi, lo = mcat[part, :rank], mcat[part, rank:]
        both = jnp.concatenate([jnp.concatenate([hi, hi], 1), jnp.concatenate([lo, lo], 1)], 0)
        for j in range(loads):
            cols = pl.ds(j * STEP, STEP)
            fit = dot(both, ccat[:, cols])
            err = s[part, cols] - (fit[:rw] + fit[rw:])
            e[part, cols] = err
            sq[...] += jnp.sum((err * err).reshape(rw // 8, 8, STEP), axis=0)

    def send_limit(use):
        acc = sq[:, :128]
        for k in range(1, STEP // 128):
            acc = acc + sq[:, k * 128:(k + 1) * 128]
        lslots[use, pl.ds(me, 1), :] = jnp.sum(acc, axis=0, keepdims=True)
        start([lcopy(use, i) for i in range(n_dev - 1)])
        sq[...] = jnp.zeros_like(sq)

    def get_limit(use):
        with jax.named_scope("limit"):
            lwait(use).wait_recv()
        total = jnp.sum(jnp.sum(lslots[use], axis=0, keepdims=True), axis=1, keepdims=True)
        lwait(use).wait_send()
        return HUBER * jnp.sqrt(total / count + 1e-06)

    eye = (lax.broadcasted_iota(jnp.int32, (rank, rank), 0)
           == lax.broadcasted_iota(jnp.int32, (rank, rank), 1)).astype(F32) * RIDGE

    grs = [pcopy(0, j, gpart.at[pl.ds(pts_peer(pme, j, n_pts) * gw, gw)], gslots.at[j - 1]) for j in range(1, n_pts)]
    gag = [pcopy(1, j, gred, gfull.at[pl.ds(pme * gw, gw)]) for j in range(1, n_pts)]
    hrs = [scopy(0, j, hpart.at[pl.ds(snap_peer(sme, j, n_snap) * hw, hw)], hslots.at[j - 1]) for j in range(1, n_snap)]
    hag = [scopy(1, j, hred, hfull.at[pl.ds(sme * hw, hw)]) for j in range(1, n_snap)]
    own_rows = pl.ds(pl.multiple_of(sme * rw, rw), rw)

    def gram_part():
        prepare_mt()
        gpart[...] = quads(dot(mtcat[...], mcat[...]))

    sq[...] = jnp.zeros_like(sq)
    load_m.wait()
    prepare_rows(pl.ds(0, rows))
    load_c.wait()
    prepare_cols(pl.ds(0, width), c_out[...])
    with jax.named_scope("err0"):
        def first(j, carry):
            load_cols(j).wait()
            errors(pl.ds(0, rows), rows, step_cols(j))
            return carry
        lax.fori_loop(0, loads, first, 0)
    with jax.named_scope("barrier"):
        pl.semaphore_wait(barrier, n_dev - 1)
    send_limit(0)
    gram_part()
    start(grs)

    def outer(o, carry):
        more = o < OUTER - 1
        with jax.named_scope("grs"):
            finish(gslots, p_send.at[0], p_recv.at[0])
        own = gpart[pl.ds(pme * gw, gw), :]
        for j in range(1, n_pts):
            own = own + gslots[j - 1]
        gred[...] = own
        gfull[pl.ds(pme * gw, gw), :] = own
        start(gag)

        for inner in range(INNER):
            limit = get_limit(inner)

            def give(k):
                return ccopy(0, k, cpart.at[k], cslots.at[inner, k])

            def spread(k):
                ref = c_out.at[:, col_chunk(core, k)]
                return ccopy(1, k, ref, ref)

            def products(t, carry):
                last = t == 2 * chunks - 1
                theirs = (t == 0) | ((lax.rem(t, 2) == 1) & (t < 2 * chunks - 1))
                k = jnp.where(theirs, (t + 1) // 2, jnp.where(last, chunks - 1, t // 2 - 1))
                which = jnp.where(theirs, 1 - core, core)
                hi, lo = split(jnp.clip(e[:, col_chunk(which, k)], -limit, limit))
                value = quads(dot(mtcat[...], jnp.concatenate([hi, lo], 1)))

                @pl.when(theirs)
                def _():
                    cpart[k] = value
                    give(k).start()

                @pl.when(jnp.logical_not(theirs))
                def _():
                    give(k).wait_recv()
                    xslots[inner, px, k] = value + cslots[inner, k]
                    for d in range(1, n_x):
                        xcopy(inner, k, d).start()
                return carry
            with jax.named_scope("products"):
                lax.fori_loop(0, 2 * chunks, products, 0)
            if inner == 0:
                with jax.named_scope("gag"):
                    finish(gfull.at[pl.ds(0, rank - gw)], p_send.at[1], p_recv.at[1])
                gfull[...] = gfull[...] + eye
                sweep(gfull, 0, rank // PIVOTS)

            def update(t, carry):
                j = t // 2
                mine = lax.rem(t, 2) == 0
                per = STEP // CHUNK

                def own_cols(i, carry):
                    k = j * per + i
                    for d in range(1, n_x):
                        xcopy(inner, k, d).wait_recv()
                    share = xslots[inner, 0, k]
                    for x in range(1, n_x):
                        share = share + xslots[inner, x, k]
                    step = jnp.dot(gfull[...], share, preferred_element_type=F32, precision=lax.Precision.HIGHEST)
                    cols = col_chunk(core, k)
                    value = c_out[:, cols] - step
                    c_out[:, cols] = value
                    spread(k).start()
                    prepare_cols(cols, value)
                    if inner == INNER - 1:
                        prepare_ct(cols, value)
                    return carry

                def their_cols(i, carry):
                    k = j * per + i
                    spread(k).wait_recv()
                    cols = col_chunk(1 - core, k)
                    value = c_out[:, cols]
                    prepare_cols(cols, value)
                    if inner == INNER - 1:
                        prepare_ct(cols, value)
                    return carry

                @pl.when(mine)
                def _():
                    lax.fori_loop(0, per, own_cols, 0)

                @pl.when(jnp.logical_not(mine))
                def _():
                    lax.fori_loop(0, per, their_cols, 0)
                which = jnp.where(mine, core, 1 - core)
                with jax.named_scope("errchunk"):
                    errors(pl.ds(0, rows), rows, pl.ds(pl.multiple_of(which * half + j * STEP, STEP), STEP))
                return carry
            with jax.named_scope("update"):
                lax.fori_loop(0, loads, update, 0)
            send_limit(inner + 1)

            sent(cpart, c_send.at[0], c_recv.at[0, 0])
            sent(c_out.at[:, pl.ds(0, half)], c_send.at[1], c_recv.at[1, 0])
            sent(xslots.at[0, pl.ds(0, n_x - 1)], x_send, x_recv.at[0, 0])

        @pl.when(jnp.logical_not(more))
        def _():
            c_out[...] = c_out[...] * jnp.sqrt(jnp.float32(rows * n_pts))
        with jax.named_scope("hpart"):
            hpart[...] = quads(dot(ccat[...], ctcat[...]))
            start(hrs)
        limit = get_limit(INNER)

        def moment(part):
            hi, lo = split(jnp.clip(e[part, :], -limit, limit))
            return quads(dot(jnp.concatenate([hi, lo], 0), ctcat[...]))

        def over_y(d):
            return ycopy(0, d, ypart.at[d], yslots.at[d])

        def over_z(d):
            return zcopy(0, d, zpart.at[d], zslots.at[d - 1])

        def moments(t, carry):
            theirs = t < n_z
            d = far(t % n_z)
            value = moment(row_block(d, jnp.where(theirs, 1 - sy, sy)))

            @pl.when(theirs)
            def _():
                ypart[d] = value
                over_y(d).start()

            @pl.when(jnp.logical_not(theirs))
            def _():
                zpart[d] = value

            @pl.when(t == 0)
            def _():
                finish(hslots, s_send.at[0], s_recv.at[0])
                own = hpart[pl.ds(sme * hw, hw), :]
                for j in range(1, n_snap):
                    own = own + hslots[j - 1]
                hred[...] = own
                hfull[pl.ds(sme * hw, hw), :] = own
                start(hag)
            return carry
        with jax.named_scope("moments"):
            lax.fori_loop(0, 2 * n_z, moments, 0)
        def forward(t, carry):
            d = far(t)
            with jax.named_scope("ywait"):
                over_y(d).wait_recv()
            zpart[d] = zpart[d] + yslots[d]

            @pl.when(t < n_z - 1)
            def _():
                over_z(d).start()
            return carry
        lax.fori_loop(0, n_z - 2, forward, 0)
        with jax.named_scope("hag"):
            finish(hfull.at[pl.ds(0, rank - hw)], s_send.at[1], s_recv.at[1])
        hfull[...] = hfull[...] + eye
        early = rank // PIVOTS * 3 // 8
        sweep(hfull, 0, early)
        forward(n_z - 2, 0)
        sweep(hfull, early, rank // PIVOTS - early)
        forward(n_z - 1, 0)
        with jax.named_scope("zwait"):
            for d in range(1, n_z):
                over_z(d).wait_recv()
        share = zpart[0]
        for d in range(1, n_z):
            share = share + zslots[d - 1]
        step = jnp.dot(share, hfull[...], preferred_element_type=F32, precision=lax.Precision.HIGHEST)
        m_out[own_rows, :] = m_out[own_rows, :] - step
        own_ref = m_out.at[own_rows]
        order = [far(t) for t in range(n_z - 1)]
        start([zcopy(1, d, own_ref, own_ref) for d in order[1:] + order[:1]])
        ycopy(1, 0, own_ref, own_ref).start()

        def pass_on(d):
            ref = m_out.at[row_block(n_z - d, sy)]
            return ycopy(1, d, ref, ref)

        def take(part):
            @pl.when(more)
            def _():
                prepare_rows(part)
                error_rows(part)
        take(own_rows)
        with jax.named_scope("gatherz"):
            for d in order[:0:-1] + order[:1]:
                zcopy(1, d, own_ref, own_ref).wait_recv()
                pass_on(d).start()

        def near(u, carry):
            take(row_block(u, sy))
            return carry
        with jax.named_scope("near"):
            lax.fori_loop(1, n_z, near, 0)

        def other(u, carry):
            d = jnp.where(u == 0, 0, far(n_z - 1 - u))
            with jax.named_scope("gathery"):
                pass_on(d).wait_recv()
            take(row_block(n_z - d, 1 - sy))
            return carry
        with jax.named_scope("other"):
            lax.fori_loop(0, n_z, other, 0)

        @pl.when(more)
        def _():
            send_limit(0)
            gram_part()
            start(grs)
        with jax.named_scope("sends"):
            sent(ypart, y_send.at[0], y_recv.at[0, 0])
            sent(m_out.at[pl.ds(0, n_z * rw)], y_send.at[1], y_recv.at[1, 0])
            sent(zslots, z_send.at[0], z_recv.at[0, 0])
            sent(m_out.at[pl.ds(0, (n_z - 1) * rw)], z_send.at[1], z_recv.at[1, 0])
        return carry
    lax.fori_loop(0, OUTER, outer, 0)


def write_out(modes, amplitudes, m_hbm, a_hbm, sem):
    copies = [pltpu.make_async_copy(modes, m_hbm, sem.at[0]), pltpu.make_async_copy(amplitudes, a_hbm, sem.at[1])]
    for copy in copies:
        copy.start()
    for copy in copies:
        copy.wait()


def shards(n_pts, n_snap, snapshots, modes_init, coefs_init):
    rows, width = snapshots.shape
    rank = modes_init.shape[1]
    rw, gw, hw = rows // n_snap, rank // n_pts, rank // n_snap
    chunks, n_x, n_z, n_dev = width // 2 // CHUNK, n_pts // 2, n_snap // 2, n_pts * n_snap
    vmem, dma = pltpu.VMEM, pltpu.SemaphoreType.DMA
    scratch = [
        vmem((rows, width), F32), vmem((rows, width), F32),
        vmem((rows, 2 * rank), BF16), vmem((2 * rank, rows), BF16),
        vmem((2 * rank, width), BF16), vmem((width, 2 * rank), BF16),
        vmem((8, STEP), F32),
        vmem((rank, rank), F32), vmem((n_pts - 1, gw, rank), F32), vmem((gw, rank), F32), vmem((rank, rank), F32),
        vmem((rank, rank), F32), vmem((n_snap - 1, hw, rank), F32), vmem((hw, rank), F32), vmem((rank, rank), F32),
        vmem((INNER + 1, n_dev, 128), F32),
        vmem((chunks, rank, CHUNK), F32), vmem((INNER, chunks, rank, CHUNK), F32),
        vmem((INNER, n_x, chunks, rank, CHUNK), F32),
        vmem((n_z, rw, rank), F32), vmem((n_z, rw, rank), F32),
        vmem((n_z, rw, rank), F32), vmem((n_z - 1, rw, rank), F32),
        dma((2 + width // STEP,)),
        dma((2,)), dma((2,)),
        dma((2,)), dma((2,)),
        dma((2,)), dma((2, chunks)),
        dma, dma((chunks, n_x - 1)),
        dma((INNER + 1,)), dma((INNER + 1,)),
        dma((2,)), dma((2, n_z)),
        dma((2,)), dma((2, n_z - 1)),
    ]
    modes, coefs = pl.pallas_call(
        functools.partial(kernel, n_pts, n_snap),
        out_shape=(vmem((rows, rank), F32), vmem((rank, width), F32)),
        in_specs=[pl.BlockSpec(memory_space=pltpu.HBM)] * 3,
        out_specs=(pl.BlockSpec(memory_space=vmem), pl.BlockSpec(memory_space=vmem)),
        scratch_shapes=scratch,
        compiler_params=pltpu.CompilerParams(collective_id=0, has_side_effects=True, vmem_limit_bytes=67043328 - 5 * 256 * 1024),
    )(snapshots, modes_init, coefs_init)
    return pl.pallas_call(
        write_out,
        out_shape=(jax.ShapeDtypeStruct((rows, rank), F32), jax.ShapeDtypeStruct((rank, width), F32)),
        in_specs=[pl.BlockSpec(memory_space=pl.ANY)] * 2,
        out_specs=(pl.BlockSpec(memory_space=pltpu.HBM), pl.BlockSpec(memory_space=pltpu.HBM)),
        scratch_shapes=[dma((2,))],
    )(pltpu.with_memory_space_constraint(modes, vmem), pltpu.with_memory_space_constraint(coefs, vmem))


def solution(mesh):
    in_specs = (P("pts", "snap"), P("pts", None), P(None, "snap"))
    out_specs = (P("pts", None), P(None, "snap"))
    body = functools.partial(shards, mesh.shape["pts"], mesh.shape["snap"])
    return jax.shard_map(body, mesh=mesh, in_specs=in_specs, out_specs=out_specs, check_vma=False)
```

```python
import functools

import jax
import jax.numpy as jnp
from jax import lax
from jax.experimental import pallas as pl
from jax.experimental.pallas import tpu as pltpu
from jax.sharding import PartitionSpec as P

OUTER = 2
INNER = 2
PIVOTS = 16
CHUNK = 128
STEP = 256

HUBER = 1.345
RIDGE = 0.01

F32 = jnp.float32
BF16 = jnp.bfloat16
MESH = pl.DeviceIdType.MESH


def split(x):
    hi = x.astype(BF16)
    lo = (x - hi.astype(F32)).astype(BF16)
    return hi, lo


def split3(x):
    hi = x.astype(BF16)
    rest = x - hi.astype(F32)
    mid = rest.astype(BF16)
    lo = (rest - mid.astype(F32)).astype(BF16)
    return hi, mid, lo


def dot(a, b):
    return jnp.dot(a, b, preferred_element_type=F32)


def quads(x):
    r, c = x.shape[0] // 2, x.shape[1] // 2
    return (x[:r, :c] + x[:r, c:]) + (x[r:, :c] + x[r:, c:])


def pts_peer(me, j, n):
    if n % 2:
        return lax.rem(me + j, n)
    x, c = me // 2, lax.rem(me, 2)
    return lax.rem(x + j // 2, n // 2) * 2 + lax.rem(c + lax.rem(j, 2), 2)


def snap_peer(me, j, n):
    return lax.rem(me + j, n)


def kernel(n_pts, n_snap, s_hbm, m_hbm, c_hbm, m_out, c_out,
           s, e, mcat, mtcat, ccat, ctcat, sq,
           gpart, gslots, gred, gfull, hpart, hslots, hred, hfull,
           lslots, cpart, cslots, xslots, ypart, yslots, zpart, zslots,
           load_sem, p_send, p_recv, s_send, s_recv, c_send, c_recv, x_send, x_recv,
           l_send, l_recv, y_send, y_recv, z_send, z_recv):
    rows, width = s.shape
    rank = m_out.shape[1]
    pme = lax.axis_index("pts")
    sme = lax.axis_index("snap")
    n_dev = n_pts * n_snap
    me = pme * n_snap + sme
    rw = rows // n_snap
    rh = rw // 2
    half = width // 2
    chunks = half // CHUNK
    n_x, n_z = n_pts // 2, n_snap // 2
    px, core = pme // 2, lax.rem(pme, 2)
    sz, sy = sme // 2, lax.rem(sme, 2)
    gw = rank // n_pts
    hw = rank // n_snap
    count = float(rows * n_pts * width * n_snap)
    loads = width // STEP

    def offset(d):
        dx, dc, dz, dy = d
        return {"pts": lax.rem(px + dx, n_x) * 2 + lax.rem(core + dc, 2),
                "snap": lax.rem(sz + dz, n_z) * 2 + lax.rem(sy + dy, 2)}

    def hops(d):
        dx, dc, dz, dy = d
        return min(dx, n_x - dx) + dy + min(dz, n_z - dz) + 0.1 * dc
    others = [(dx, dc, dz, dy) for dx in range(n_x) for dc in range(2) for dz in range(n_z) for dy in range(2)][1:]
    others.sort(key=lambda d: -hops(d))

    barrier = pltpu.get_barrier_semaphore()
    for d in others:
        pl.semaphore_signal(barrier, inc=1, device_id=offset(d), device_id_type=MESH)

    def step_cols(j):
        return pl.ds(pl.multiple_of(j * STEP, STEP), STEP)

    def load_cols(j):
        cols = step_cols(j)
        return pltpu.make_async_copy(s_hbm.at[:, cols], s.at[:, cols], load_sem.at[2 + j])
    load_m = pltpu.make_async_copy(m_hbm, m_out, load_sem.at[0])
    load_c = pltpu.make_async_copy(c_hbm, c_out, load_sem.at[1])
    load_m.start()
    load_c.start()
    for j in range(loads):
        load_cols(j).start()

    def pcopy(site, j, src, dst):
        return pltpu.make_async_remote_copy(
            src_ref=src, dst_ref=dst, send_sem=p_send.at[site], recv_sem=p_recv.at[site],
            device_id={"pts": pts_peer(pme, j, n_pts)}, device_id_type=MESH)

    def scopy(site, j, src, dst):
        return pltpu.make_async_remote_copy(
            src_ref=src, dst_ref=dst, send_sem=s_send.at[site], recv_sem=s_recv.at[site],
            device_id={"snap": snap_peer(sme, j, n_snap)}, device_id_type=MESH)

    def ccopy(site, k, src, dst):
        return pltpu.make_async_remote_copy(
            src_ref=src, dst_ref=dst, send_sem=c_send.at[site], recv_sem=c_recv.at[site, k],
            device_id={"pts": px * 2 + 1 - core}, device_id_type=MESH)

    def xcopy(site, k, d):
        ref = xslots.at[site, px, k]
        return pltpu.make_async_remote_copy(
            src_ref=ref, dst_ref=ref, send_sem=x_send, recv_sem=x_recv.at[k, d - 1],
            device_id={"pts": lax.rem(px + d, n_x) * 2 + core}, device_id_type=MESH)

    def lcopy(use, i):
        ref = lslots.at[use, pl.ds(me, 1)]
        return pltpu.make_async_remote_copy(
            src_ref=ref, dst_ref=ref, send_sem=l_send.at[use], recv_sem=l_recv.at[use],
            device_id=offset(others[i]), device_id_type=MESH)

    def lwait(use):
        ref = lslots.at[use, pl.ds(0, n_dev - 1)]
        return pltpu.make_async_remote_copy(
            src_ref=ref, dst_ref=ref, send_sem=l_send.at[use], recv_sem=l_recv.at[use],
            device_id=offset(others[0]), device_id_type=MESH)

    def half_of(ref, h):
        return ref.at[pl.ds(pl.multiple_of(h * rh, rh), rh)]

    def ycopy(site, d, h, src, dst):
        return pltpu.make_async_remote_copy(
            src_ref=src, dst_ref=dst, send_sem=y_send.at[site], recv_sem=y_recv.at[site, d, h],
            device_id={"snap": sz * 2 + 1 - sy}, device_id_type=MESH)

    def zcopy(site, d, h, src, dst):
        return pltpu.make_async_remote_copy(
            src_ref=src, dst_ref=dst, send_sem=z_send.at[site], recv_sem=z_recv.at[site, d - 1, h],
            device_id={"snap": z_peer(d) * 2 + sy}, device_id_type=MESH)

    def z_peer(d):
        return (sz // 2 + d // 2) % (n_z // 2) * 2 + (sz + d) % 2

    def z_from(d):
        return (sz // 2 + n_z // 2 - d // 2) % (n_z // 2) * 2 + (sz + d) % 2

    def row_block(z, which):
        return pl.ds(pl.multiple_of((z * 2 + which) * rw, rw), rw)

    def far(t):
        return n_z - 1 - t

    def col_chunk(which, k):
        return pl.ds(pl.multiple_of(which * half + k * CHUNK, CHUNK), CHUNK)

    def start(copies):
        for copy in copies:
            copy.start()

    def all_of(ref, send_sem, recv_sem):
        return pltpu.make_async_remote_copy(
            src_ref=ref, dst_ref=ref, send_sem=send_sem, recv_sem=recv_sem,
            device_id={"pts": px * 2 + 1 - core}, device_id_type=MESH)

    def finish(ref, send_sem, recv_sem):
        all_of(ref, send_sem, recv_sem).wait_recv()
        all_of(ref, send_sem, recv_sem).wait_send()

    def sent(ref, send_sem, recv_sem):
        all_of(ref, send_sem, recv_sem).wait_send()

    def prepare_rows(part):
        hi, lo = split(m_out[part, :])
        mcat[part, :rank] = hi
        mcat[part, rank:] = lo

    def prepare_mt():
        hi, lo = split(m_out[...].T)
        mtcat[:rank, :] = hi
        mtcat[rank:, :] = lo

    def prepare_cols(cols, value):
        hi, lo = split(value)
        ccat[:rank, cols] = hi
        ccat[rank:, cols] = lo

    def prepare_ct(cols, value):
        hi, lo = split(value.T)
        ctcat[cols, :rank] = hi
        ctcat[cols, rank:] = lo

    def sweep(ref, base, steps):
        sub = lax.broadcasted_iota(jnp.int32, (PIVOTS, rank), 0)
        lane = lax.broadcasted_iota(jnp.int32, (PIVOTS, rank), 1)
        wide = lax.broadcasted_iota(jnp.int32, (rank, rank), 1)
        side = sub[:, :1]

        def body(t, carry):
            k = (base + t) * PIVOTS
            rws = pl.ds(pl.multiple_of(k, PIVOTS), PIVOTS)
            before = ref[rws, :]
            after = before
            cols = [jnp.sum(jnp.where(lane == k + p, before, 0.0), axis=1, keepdims=True) for p in range(PIVOTS)]
            for p in range(PIVOTS):
                col = cols[p]
                inv = 1.0 / col[p:p + 1, :]
                row = after[p:p + 1, :] * inv
                for q in range(p + 1, PIVOTS):
                    f = cols[q][p:p + 1, :] * inv
                    cols[q] = jnp.where(side == p, f, cols[q] - col * f)
                after = jnp.where(lane == k + p, col * inv, after - col * row)
                after = jnp.where(sub == p, jnp.where(lane == k + p, -inv, row), after)
            h, m, l = split3(before)
            a, b, c = split3(after)
            change = lax.dot_general(
                jnp.concatenate([h, h, m, h, m, l], 0), jnp.concatenate([a, b, a, c, b, a], 0),
                (((0,), (0,)), ((), ())), preferred_element_type=F32)
            ref[...] = jnp.where((wide >= k) & (wide < k + PIVOTS), 0.0, ref[...]) - change
            ref[rws, :] = after
            return carry
        with jax.named_scope("sweep"):
            lax.fori_loop(0, steps, body, 0)

    def errors(part, n_rows, cols):
        hi, lo = mcat[part, :rank], mcat[part, rank:]
        c = ccat[:, cols]
        fit = dot(jnp.concatenate([hi, hi], 1), c) + dot(jnp.concatenate([lo, lo], 1), c)
        err = s[part, cols] - fit
        e[part, cols] = err
        sq[...] += jnp.sum((err * err).reshape(n_rows // 8, 8, STEP), axis=0)

    def error_rows(part):
        hi, lo = mcat[part, :rank], mcat[part, rank:]
        both = jnp.concatenate([jnp.concatenate([hi, hi], 1), jnp.concatenate([lo, lo], 1)], 0)
        for j in range(loads):
            cols = pl.ds(j * STEP, STEP)
            fit = dot(both, ccat[:, cols])
            err = s[part, cols] - (fit[:rw] + fit[rw:])
            e[part, cols] = err
            sq[...] += jnp.sum((err * err).reshape(rw // 8, 8, STEP), axis=0)

    def send_limit(use):
        acc = sq[:, :128]
        for k in range(1, STEP // 128):
            acc = acc + sq[:, k * 128:(k + 1) * 128]
        lslots[use, pl.ds(me, 1), :] = jnp.sum(acc, axis=0, keepdims=True)
        start([lcopy(use, i) for i in range(n_dev - 1)])
        sq[...] = jnp.zeros_like(sq)

    def get_limit(use):
        with jax.named_scope("limit"):
            lwait(use).wait_recv()
        total = jnp.sum(jnp.sum(lslots[use], axis=0, keepdims=True), axis=1, keepdims=True)
        lwait(use).wait_send()
        return HUBER * jnp.sqrt(total / count + 1e-06)

    eye = (lax.broadcasted_iota(jnp.int32, (rank, rank), 0)
           == lax.broadcasted_iota(jnp.int32, (rank, rank), 1)).astype(F32) * RIDGE

    grs = [pcopy(0, j, gpart.at[pl.ds(pts_peer(pme, j, n_pts) * gw, gw)], gslots.at[j - 1]) for j in range(1, n_pts)]
    gag = [pcopy(1, j, gred, gfull.at[pl.ds(pme * gw, gw)]) for j in range(1, n_pts)]
    hrs = [scopy(0, j, hpart.at[pl.ds(snap_peer(sme, j, n_snap) * hw, hw)], hslots.at[j - 1]) for j in range(1, n_snap)]
    hag = [scopy(1, j, hred, hfull.at[pl.ds(sme * hw, hw)]) for j in range(1, n_snap)]
    own_rows = pl.ds(pl.multiple_of(sme * rw, rw), rw)

    def gram_part():
        prepare_mt()
        gpart[...] = quads(dot(mtcat[...], mcat[...]))

    sq[...] = jnp.zeros_like(sq)
    load_m.wait()
    prepare_rows(pl.ds(0, rows))
    load_c.wait()
    prepare_cols(pl.ds(0, width), c_out[...])
    with jax.named_scope("err0"):
        def first(j, carry):
            load_cols(j).wait()
            errors(pl.ds(0, rows), rows, step_cols(j))
            return carry
        lax.fori_loop(0, loads, first, 0)
    with jax.named_scope("barrier"):
        pl.semaphore_wait(barrier, n_dev - 1)
    send_limit(0)
    gram_part()
    start(grs)

    def outer(o, carry):
        more = o < OUTER - 1
        with jax.named_scope("grs"):
            finish(gslots, p_send.at[0], p_recv.at[0])
        own = gpart[pl.ds(pme * gw, gw), :]
        for j in range(1, n_pts):
            own = own + gslots[j - 1]
        gred[...] = own
        gfull[pl.ds(pme * gw, gw), :] = own
        start(gag)

        for inner in range(INNER):
            limit = get_limit(inner)

            def give(k):
                return ccopy(0, k, cpart.at[k], cslots.at[inner, k])

            def spread(k):
                ref = c_out.at[:, col_chunk(core, k)]
                return ccopy(1, k, ref, ref)

            def products(t, carry):
                last = t == 2 * chunks - 1
                theirs = (t == 0) | ((lax.rem(t, 2) == 1) & (t < 2 * chunks - 1))
                k = jnp.where(theirs, (t + 1) // 2, jnp.where(last, chunks - 1, t // 2 - 1))
                which = jnp.where(theirs, 1 - core, core)
                hi, lo = split(jnp.clip(e[:, col_chunk(which, k)], -limit, limit))
                value = quads(dot(mtcat[...], jnp.concatenate([hi, lo], 1)))

                @pl.when(theirs)
                def _():
                    cpart[k] = value
                    give(k).start()

                @pl.when(jnp.logical_not(theirs))
                def _():
                    give(k).wait_recv()
                    xslots[inner, px, k] = value + cslots[inner, k]
                    for d in range(1, n_x):
                        xcopy(inner, k, d).start()
                return carry
            with jax.named_scope("products"):
                lax.fori_loop(0, 2 * chunks, products, 0)
            if inner == 0:
                with jax.named_scope("gag"):
                    finish(gfull.at[pl.ds(0, rank - gw)], p_send.at[1], p_recv.at[1])
                gfull[...] = gfull[...] + eye
                sweep(gfull, 0, rank // PIVOTS)

            def update(t, carry):
                j = t // 2
                mine = lax.rem(t, 2) == 0
                per = STEP // CHUNK

                def own_cols(i, carry):
                    k = j * per + i
                    for d in range(1, n_x):
                        xcopy(inner, k, d).wait_recv()
                    share = xslots[inner, 0, k]
                    for x in range(1, n_x):
                        share = share + xslots[inner, x, k]
                    step = jnp.dot(gfull[...], share, preferred_element_type=F32, precision=lax.Precision.HIGHEST)
                    cols = col_chunk(core, k)
                    value = c_out[:, cols] - step
                    c_out[:, cols] = value
                    spread(k).start()
                    prepare_cols(cols, value)
                    if inner == INNER - 1:
                        prepare_ct(cols, value)
                    return carry

                def their_cols(i, carry):
                    k = j * per + i
                    spread(k).wait_recv()
                    cols = col_chunk(1 - core, k)
                    value = c_out[:, cols]
                    prepare_cols(cols, value)
                    if inner == INNER - 1:
                        prepare_ct(cols, value)
                    return carry

                @pl.when(mine)
                def _():
                    lax.fori_loop(0, per, own_cols, 0)

                @pl.when(jnp.logical_not(mine))
                def _():
                    lax.fori_loop(0, per, their_cols, 0)
                which = jnp.where(mine, core, 1 - core)
                with jax.named_scope("errchunk"):
                    errors(pl.ds(0, rows), rows, pl.ds(pl.multiple_of(which * half + j * STEP, STEP), STEP))
                return carry
            with jax.named_scope("update"):
                lax.fori_loop(0, loads, update, 0)
            send_limit(inner + 1)

            sent(cpart, c_send.at[0], c_recv.at[0, 0])
            sent(c_out.at[:, pl.ds(0, half)], c_send.at[1], c_recv.at[1, 0])
            sent(xslots.at[0, pl.ds(0, n_x - 1)], x_send, x_recv.at[0, 0])

        @pl.when(jnp.logical_not(more))
        def _():
            c_out[...] = c_out[...] * jnp.sqrt(jnp.float32(rows * n_pts))
        with jax.named_scope("hpart"):
            hpart[...] = quads(dot(ccat[...], ctcat[...]))
            start(hrs)
        limit = get_limit(INNER)

        def moment(part):
            hi, lo = split(jnp.clip(e[part, :], -limit, limit))
            return quads(dot(jnp.concatenate([hi, lo], 0), ctcat[...]))

        def over_y(d, h):
            return ycopy(0, d, h, half_of(ypart.at[d], h), half_of(yslots.at[d], h))

        def over_z(d, h):
            return zcopy(0, d, h, half_of(zpart.at[d], h), half_of(zslots.at[d - 1], h))

        def moments(t, carry):
            theirs = t < n_z
            d = far(t % n_z)
            value = moment(row_block(z_peer(d), jnp.where(theirs, 1 - sy, sy)))

            @pl.when(theirs)
            def _():
                ypart[d] = value
                over_y(d, 0).start()

            @pl.when(jnp.logical_not(theirs))
            def _():
                zpart[d] = value

            @pl.when(t == n_z - 1)
            def _():
                start([over_y(far(u), 1) for u in range(n_z)])

            @pl.when(t == 0)
            def _():
                finish(hslots, s_send.at[0], s_recv.at[0])
                own = hpart[pl.ds(sme * hw, hw), :]
                for j in range(1, n_snap):
                    own = own + hslots[j - 1]
                hred[...] = own
                hfull[pl.ds(sme * hw, hw), :] = own
                start(hag)
            return carry
        with jax.named_scope("moments"):
            lax.fori_loop(0, 2 * n_z, moments, 0)
        def forward(t, carry):
            d, h = far(t % n_z), t // n_z
            part = pl.ds(pl.multiple_of(h * rh, rh), rh)
            with jax.named_scope("ywait"):
                over_y(d, h).wait_recv()
            zpart[d, part, :] = zpart[d, part, :] + yslots[d, part, :]

            @pl.when(d > 0)
            def _():
                over_z(d, h).start()
            return carry
        lax.fori_loop(0, n_z, forward, 0)
        with jax.named_scope("hag"):
            finish(hfull.at[pl.ds(0, rank - hw)], s_send.at[1], s_recv.at[1])
        hfull[...] = hfull[...] + eye
        steps = rank // PIVOTS
        per = steps // n_z

        def sweep_forward(t, carry):
            sweep(hfull, t * per, per)
            return forward(n_z + t, carry)
        lax.fori_loop(0, n_z, sweep_forward, 0)
        sweep(hfull, per * n_z, steps - per * n_z)

        def modes_half(z, which, h):
            return m_out.at[pl.ds(pl.multiple_of((z * 2 + which) * rw + h * rh, rh), rh)]

        def gather(d, h):
            ref = modes_half(sz, sy, h)
            return zcopy(1, d, h, ref, ref)

        def pass_on(d, h):
            ref = modes_half(z_from(d), sy, h)
            return ycopy(1, d, h, ref, ref)

        def solve(h, carry):
            with jax.named_scope("zwait"):
                for d in range(1, n_z):
                    over_z(d, h).wait_recv()
            part = pl.ds(pl.multiple_of(h * rh, rh), rh)
            share = zpart[0, part, :]
            for d in range(1, n_z):
                share = share + zslots[d - 1, part, :]
            step = jnp.dot(share, hfull[...], preferred_element_type=F32, precision=lax.Precision.HIGHEST)
            mine = pl.ds(pl.multiple_of(sme * rw + h * rh, rh), rh)
            m_out[mine, :] = m_out[mine, :] - step
            start([gather(far(t), h) for t in range(n_z - 1)])
            pass_on(0, h).start()
            return carry
        lax.fori_loop(0, 2, solve, 0)

        def take(part):
            @pl.when(more)
            def _():
                prepare_rows(part)
                error_rows(part)
        take(own_rows)

        def near(u):
            return jnp.where(u == 0, 1, n_z - u)

        def first_half(u, carry):
            with jax.named_scope("gatherz"):
                gather(near(u), 0).wait_recv()
            pass_on(near(u), 0).start()
            return carry
        lax.fori_loop(0, n_z - 1, first_half, 0)

        def second_half(u, carry):
            with jax.named_scope("gatherz"):
                gather(near(u), 1).wait_recv()
            pass_on(near(u), 1).start()
            take(row_block(z_from(near(u)), sy))
            return carry
        lax.fori_loop(0, n_z - 1, second_half, 0)

        def other(u, carry):
            d = jnp.where(u == 0, 0, near(u - 1))
            with jax.named_scope("gathery"):
                pass_on(d, 0).wait_recv()
                pass_on(d, 1).wait_recv()
            take(row_block(z_from(d), 1 - sy))
            return carry
        with jax.named_scope("other"):
            lax.fori_loop(0, n_z, other, 0)

        @pl.when(more)
        def _():
            send_limit(0)
            gram_part()
            start(grs)
        with jax.named_scope("sends"):
            sent(ypart, y_send.at[0], y_recv.at[0, 0, 0])
            sent(m_out.at[pl.ds(0, n_z * rw)], y_send.at[1], y_recv.at[1, 0, 0])
            sent(zslots, z_send.at[0], z_recv.at[0, 0, 0])
            sent(m_out.at[pl.ds(0, (n_z - 1) * rw)], z_send.at[1], z_recv.at[1, 0, 0])
        return carry
    lax.fori_loop(0, OUTER, outer, 0)


def write_out(modes, amplitudes, m_hbm, a_hbm, sem):
    copies = [pltpu.make_async_copy(modes, m_hbm, sem.at[0]), pltpu.make_async_copy(amplitudes, a_hbm, sem.at[1])]
    for copy in copies:
        copy.start()
    for copy in copies:
        copy.wait()


def shards(n_pts, n_snap, snapshots, modes_init, coefs_init):
    rows, width = snapshots.shape
    rank = modes_init.shape[1]
    rw, gw, hw = rows // n_snap, rank // n_pts, rank // n_snap
    chunks, n_x, n_z, n_dev = width // 2 // CHUNK, n_pts // 2, n_snap // 2, n_pts * n_snap
    vmem, dma = pltpu.VMEM, pltpu.SemaphoreType.DMA
    scratch = [
        vmem((rows, width), F32), vmem((rows, width), F32),
        vmem((rows, 2 * rank), BF16), vmem((2 * rank, rows), BF16),
        vmem((2 * rank, width), BF16), vmem((width, 2 * rank), BF16),
        vmem((8, STEP), F32),
        vmem((rank, rank), F32), vmem((n_pts - 1, gw, rank), F32), vmem((gw, rank), F32), vmem((rank, rank), F32),
        vmem((rank, rank), F32), vmem((n_snap - 1, hw, rank), F32), vmem((hw, rank), F32), vmem((rank, rank), F32),
        vmem((INNER + 1, n_dev, 128), F32),
        vmem((chunks, rank, CHUNK), F32), vmem((INNER, chunks, rank, CHUNK), F32),
        vmem((INNER, n_x, chunks, rank, CHUNK), F32),
        vmem((n_z, rw, rank), F32), vmem((n_z, rw, rank), F32),
        vmem((n_z, rw, rank), F32), vmem((n_z - 1, rw, rank), F32),
        dma((2 + width // STEP,)),
        dma((2,)), dma((2,)),
        dma((2,)), dma((2,)),
        dma((2,)), dma((2, chunks)),
        dma, dma((chunks, n_x - 1)),
        dma((INNER + 1,)), dma((INNER + 1,)),
        dma((2,)), dma((2, n_z, 2)),
        dma((2,)), dma((2, n_z - 1, 2)),
    ]
    modes, coefs = pl.pallas_call(
        functools.partial(kernel, n_pts, n_snap),
        out_shape=(vmem((rows, rank), F32), vmem((rank, width), F32)),
        in_specs=[pl.BlockSpec(memory_space=pltpu.HBM)] * 3,
        out_specs=(pl.BlockSpec(memory_space=vmem), pl.BlockSpec(memory_space=vmem)),
        scratch_shapes=scratch,
        compiler_params=pltpu.CompilerParams(collective_id=0, has_side_effects=True, vmem_limit_bytes=67043328 - 5 * 256 * 1024),
    )(snapshots, modes_init, coefs_init)
    return pl.pallas_call(
        write_out,
        out_shape=(jax.ShapeDtypeStruct((rows, rank), F32), jax.ShapeDtypeStruct((rank, width), F32)),
        in_specs=[pl.BlockSpec(memory_space=pl.ANY)] * 2,
        out_specs=(pl.BlockSpec(memory_space=pltpu.HBM), pl.BlockSpec(memory_space=pltpu.HBM)),
        scratch_shapes=[dma((2,))],
    )(pltpu.with_memory_space_constraint(modes, vmem), pltpu.with_memory_space_constraint(coefs, vmem))


def solution(mesh):
    in_specs = (P("pts", "snap"), P("pts", None), P(None, "snap"))
    out_specs = (P("pts", None), P(None, "snap"))
    body = functools.partial(shards, mesh.shape["pts"], mesh.shape["snap"])
    return jax.shard_map(body, mesh=mesh, in_specs=in_specs, out_specs=out_specs, check_vma=False)
```

```python
import functools

import jax
import jax.numpy as jnp
from jax import lax
from jax.experimental import pallas as pl
from jax.experimental.pallas import tpu as pltpu
from jax.sharding import PartitionSpec as P

OUTER = 2
INNER = 2
PIVOTS = 16
CHUNK = 128
STEP = 256

HUBER = 1.345
RIDGE = 0.01

F32 = jnp.float32
BF16 = jnp.bfloat16
MESH = pl.DeviceIdType.MESH


def split(x):
    hi = x.astype(BF16)
    lo = (x - hi.astype(F32)).astype(BF16)
    return hi, lo


def split3(x):
    hi = x.astype(BF16)
    rest = x - hi.astype(F32)
    mid = rest.astype(BF16)
    lo = (rest - mid.astype(F32)).astype(BF16)
    return hi, mid, lo


def dot(a, b):
    return jnp.dot(a, b, preferred_element_type=F32)


def quads(x):
    r, c = x.shape[0] // 2, x.shape[1] // 2
    return (x[:r, :c] + x[:r, c:]) + (x[r:, :c] + x[r:, c:])


def pts_peer(me, j, n):
    if n % 2:
        return lax.rem(me + j, n)
    x, c = me // 2, lax.rem(me, 2)
    return lax.rem(x + j // 2, n // 2) * 2 + lax.rem(c + lax.rem(j, 2), 2)


def snap_peer(me, j, n):
    return lax.rem(me + j, n)


def kernel(n_pts, n_snap, s_hbm, m_hbm, c_hbm, m_out, c_out,
           s, e, mcat, mtcat, ccat, ctcat, sq,
           gpart, gslots, gred, gfull, hpart, hslots, hred, hfull,
           lslots, cpart, cslots, xslots, ypart, yslots, zpart, zslots,
           load_sem, p_send, p_recv, s_send, s_recv, c_send, c_recv, x_send, x_recv,
           l_send, l_recv, y_send, y_recv, z_send, z_recv):
    rows, width = s.shape
    rank = m_out.shape[1]
    pme = lax.axis_index("pts")
    sme = lax.axis_index("snap")
    n_dev = n_pts * n_snap
    me = pme * n_snap + sme
    rw = rows // n_snap
    rh = rw // 2
    half = width // 2
    chunks = half // CHUNK
    n_x, n_z = n_pts // 2, n_snap // 2
    px, core = pme // 2, lax.rem(pme, 2)
    sz, sy = sme // 2, lax.rem(sme, 2)
    gw = rank // n_pts
    hw = rank // n_snap
    count = float(rows * n_pts * width * n_snap)
    loads = width // STEP

    def offset(d):
        dx, dc, dz, dy = d
        return {"pts": lax.rem(px + dx, n_x) * 2 + lax.rem(core + dc, 2),
                "snap": lax.rem(sz + dz, n_z) * 2 + lax.rem(sy + dy, 2)}

    def hops(d):
        dx, dc, dz, dy = d
        return min(dx, n_x - dx) + dy + min(dz, n_z - dz) + 0.1 * dc
    others = [(dx, dc, dz, dy) for dx in range(n_x) for dc in range(2) for dz in range(n_z) for dy in range(2)][1:]
    others.sort(key=lambda d: -hops(d))

    barrier = pltpu.get_barrier_semaphore()
    for d in others:
        pl.semaphore_signal(barrier, inc=1, device_id=offset(d), device_id_type=MESH)

    def step_cols(j):
        return pl.ds(pl.multiple_of(j * STEP, STEP), STEP)

    def load_cols(j):
        cols = step_cols(j)
        return pltpu.make_async_copy(s_hbm.at[:, cols], s.at[:, cols], load_sem.at[2 + j])
    load_m = pltpu.make_async_copy(m_hbm, m_out, load_sem.at[0])
    load_c = pltpu.make_async_copy(c_hbm, c_out, load_sem.at[1])
    load_m.start()
    load_c.start()
    for j in range(loads):
        load_cols(j).start()

    def pcopy(site, j, src, dst):
        return pltpu.make_async_remote_copy(
            src_ref=src, dst_ref=dst, send_sem=p_send.at[site], recv_sem=p_recv.at[site],
            device_id={"pts": pts_peer(pme, j, n_pts)}, device_id_type=MESH)

    def scopy(site, j, src, dst):
        return pltpu.make_async_remote_copy(
            src_ref=src, dst_ref=dst, send_sem=s_send.at[site], recv_sem=s_recv.at[site],
            device_id={"snap": snap_peer(sme, j, n_snap)}, device_id_type=MESH)

    def ccopy(site, k, src, dst):
        return pltpu.make_async_remote_copy(
            src_ref=src, dst_ref=dst, send_sem=c_send.at[site], recv_sem=c_recv.at[site, k],
            device_id={"pts": px * 2 + 1 - core}, device_id_type=MESH)

    def xcopy(site, k, d):
        ref = xslots.at[site, px, k]
        return pltpu.make_async_remote_copy(
            src_ref=ref, dst_ref=ref, send_sem=x_send, recv_sem=x_recv.at[k, d - 1],
            device_id={"pts": lax.rem(px + d, n_x) * 2 + core}, device_id_type=MESH)

    def lcopy(use, i):
        ref = lslots.at[use, pl.ds(me, 1)]
        return pltpu.make_async_remote_copy(
            src_ref=ref, dst_ref=ref, send_sem=l_send.at[use], recv_sem=l_recv.at[use],
            device_id=offset(others[i]), device_id_type=MESH)

    def lwait(use):
        ref = lslots.at[use, pl.ds(0, n_dev - 1)]
        return pltpu.make_async_remote_copy(
            src_ref=ref, dst_ref=ref, send_sem=l_send.at[use], recv_sem=l_recv.at[use],
            device_id=offset(others[0]), device_id_type=MESH)

    def half_of(ref, h):
        return ref.at[pl.ds(pl.multiple_of(h * rh, rh), rh)]

    def ycopy(site, d, h, src, dst):
        return pltpu.make_async_remote_copy(
            src_ref=src, dst_ref=dst, send_sem=y_send.at[site], recv_sem=y_recv.at[site, d, h],
            device_id={"snap": sz * 2 + 1 - sy}, device_id_type=MESH)

    def zcopy(site, d, h, src, dst):
        return pltpu.make_async_remote_copy(
            src_ref=src, dst_ref=dst, send_sem=z_send.at[site], recv_sem=z_recv.at[site, d - 1, h],
            device_id={"snap": z_peer(d) * 2 + sy}, device_id_type=MESH)

    def z_peer(d):
        return (sz // 2 + d // 2) % (n_z // 2) * 2 + (sz + d) % 2

    def z_from(d):
        return (sz // 2 + n_z // 2 - d // 2) % (n_z // 2) * 2 + (sz + d) % 2

    def row_block(z, which):
        return pl.ds(pl.multiple_of((z * 2 + which) * rw, rw), rw)

    def far(t):
        return n_z - 1 - t

    def col_chunk(which, k):
        return pl.ds(pl.multiple_of(which * half + k * CHUNK, CHUNK), CHUNK)

    def start(copies):
        for copy in copies:
            copy.start()

    def all_of(ref, send_sem, recv_sem):
        return pltpu.make_async_remote_copy(
            src_ref=ref, dst_ref=ref, send_sem=send_sem, recv_sem=recv_sem,
            device_id={"pts": px * 2 + 1 - core}, device_id_type=MESH)

    def finish(ref, send_sem, recv_sem):
        all_of(ref, send_sem, recv_sem).wait_recv()
        all_of(ref, send_sem, recv_sem).wait_send()

    def sent(ref, send_sem, recv_sem):
        all_of(ref, send_sem, recv_sem).wait_send()

    def prepare_rows(part):
        hi, lo = split(m_out[part, :])
        mcat[part, :rank] = hi
        mcat[part, rank:] = lo

    def prepare_mt():
        hi, lo = split(m_out[...].T)
        mtcat[:rank, :] = hi
        mtcat[rank:, :] = lo

    def prepare_cols(cols, value):
        hi, lo = split(value)
        ccat[:rank, cols] = hi
        ccat[rank:, cols] = lo

    def sweep(ref, base, steps):
        sub = lax.broadcasted_iota(jnp.int32, (PIVOTS, rank), 0)
        lane = lax.broadcasted_iota(jnp.int32, (PIVOTS, rank), 1)
        wide = lax.broadcasted_iota(jnp.int32, (rank, rank), 1)
        side = sub[:, :1]

        def body(t, carry):
            k = (base + t) * PIVOTS
            rws = pl.ds(pl.multiple_of(k, PIVOTS), PIVOTS)
            before = ref[rws, :]
            after = before
            cols = [jnp.sum(jnp.where(lane == k + p, before, 0.0), axis=1, keepdims=True) for p in range(PIVOTS)]
            for p in range(PIVOTS):
                col = cols[p]
                inv = 1.0 / col[p:p + 1, :]
                row = after[p:p + 1, :] * inv
                for q in range(p + 1, PIVOTS):
                    f = cols[q][p:p + 1, :] * inv
                    cols[q] = jnp.where(side == p, f, cols[q] - col * f)
                after = jnp.where(lane == k + p, col * inv, after - col * row)
                after = jnp.where(sub == p, jnp.where(lane == k + p, -inv, row), after)
            h, m, l = split3(before)
            a, b, c = split3(after)
            change = lax.dot_general(
                jnp.concatenate([h, h, m, h, m, l], 0), jnp.concatenate([a, b, a, c, b, a], 0),
                (((0,), (0,)), ((), ())), preferred_element_type=F32)
            ref[...] = jnp.where((wide >= k) & (wide < k + PIVOTS), 0.0, ref[...]) - change
            ref[rws, :] = after
            return carry
        with jax.named_scope("sweep"):
            lax.fori_loop(0, steps, body, 0)

    def errors(part, n_rows, cols, n_cols=STEP):
        hi, lo = mcat[part, :rank], mcat[part, rank:]
        c = ccat[:, cols]
        fit = dot(jnp.concatenate([hi, hi], 1), c) + dot(jnp.concatenate([lo, lo], 1), c)
        err = s[part, cols] - fit
        e[part, cols] = err
        sq[:, :n_cols] += jnp.sum((err * err).reshape(n_rows // 8, 8, n_cols), axis=0)

    def error_rows(part):
        hi, lo = mcat[part, :rank], mcat[part, rank:]
        both = jnp.concatenate([jnp.concatenate([hi, hi], 1), jnp.concatenate([lo, lo], 1)], 0)
        for j in range(loads):
            cols = pl.ds(j * STEP, STEP)
            fit = dot(both, ccat[:, cols])
            err = s[part, cols] - (fit[:rw] + fit[rw:])
            e[part, cols] = err
            sq[...] += jnp.sum((err * err).reshape(rw // 8, 8, STEP), axis=0)

    def send_limit(use):
        acc = sq[:, :128]
        for k in range(1, STEP // 128):
            acc = acc + sq[:, k * 128:(k + 1) * 128]
        lslots[use, pl.ds(me, 1), :] = jnp.sum(acc, axis=0, keepdims=True)
        start([lcopy(use, i) for i in range(n_dev - 1)])
        sq[...] = jnp.zeros_like(sq)

    def get_limit(use):
        with jax.named_scope("limit"):
            lwait(use).wait_recv()
        total = jnp.sum(jnp.sum(lslots[use], axis=0, keepdims=True), axis=1, keepdims=True)
        lwait(use).wait_send()
        return HUBER * jnp.sqrt(total / count + 1e-06)

    eye = (lax.broadcasted_iota(jnp.int32, (rank, rank), 0)
           == lax.broadcasted_iota(jnp.int32, (rank, rank), 1)).astype(F32) * RIDGE

    grs = [pcopy(0, j, gpart.at[pl.ds(pts_peer(pme, j, n_pts) * gw, gw)], gslots.at[j - 1]) for j in range(1, n_pts)]
    gag = [pcopy(1, j, gred, gfull.at[pl.ds(pme * gw, gw)]) for j in range(1, n_pts)]
    hrs = [scopy(0, j, hpart.at[pl.ds(snap_peer(sme, j, n_snap) * hw, hw)], hslots.at[j - 1]) for j in range(1, n_snap)]
    hag = [scopy(1, j, hred, hfull.at[pl.ds(sme * hw, hw)]) for j in range(1, n_snap)]
    own_rows = pl.ds(pl.multiple_of(sme * rw, rw), rw)

    def gram_part():
        prepare_mt()
        gpart[...] = quads(dot(mtcat[...], mcat[...]))

    sq[...] = jnp.zeros_like(sq)
    load_m.wait()
    prepare_rows(pl.ds(0, rows))
    load_c.wait()
    prepare_cols(pl.ds(0, width), c_out[...])
    with jax.named_scope("err0"):
        def first(j, carry):
            load_cols(j).wait()
            errors(pl.ds(0, rows), rows, step_cols(j))
            return carry
        lax.fori_loop(0, loads, first, 0)
    with jax.named_scope("barrier"):
        pl.semaphore_wait(barrier, n_dev - 1)
    send_limit(0)
    gram_part()
    start(grs)

    def outer(o, carry):
        more = o < OUTER - 1
        with jax.named_scope("grs"):
            finish(gslots, p_send.at[0], p_recv.at[0])
        own = gpart[pl.ds(pme * gw, gw), :]
        for j in range(1, n_pts):
            own = own + gslots[j - 1]
        gred[...] = own
        gfull[pl.ds(pme * gw, gw), :] = own
        start(gag)

        for inner in range(INNER):
            limit = get_limit(inner)

            def give(k):
                return ccopy(0, k, cpart.at[k], cslots.at[inner, k])

            def spread(k):
                ref = c_out.at[:, col_chunk(core, k)]
                return ccopy(1, k, ref, ref)

            def products(t, carry):
                last = t == 2 * chunks - 1
                theirs = (t == 0) | ((lax.rem(t, 2) == 1) & (t < 2 * chunks - 1))
                k = jnp.where(theirs, (t + 1) // 2, jnp.where(last, chunks - 1, t // 2 - 1))
                which = jnp.where(theirs, 1 - core, core)
                hi, lo = split(jnp.clip(e[:, col_chunk(which, k)], -limit, limit))
                value = quads(dot(mtcat[...], jnp.concatenate([hi, lo], 1)))

                @pl.when(theirs)
                def _():
                    cpart[k] = value
                    give(k).start()

                @pl.when(jnp.logical_not(theirs))
                def _():
                    give(k).wait_recv()
                    xslots[inner, px, k] = value + cslots[inner, k]
                    for d in range(1, n_x):
                        xcopy(inner, k, d).start()
                return carry
            with jax.named_scope("products"):
                lax.fori_loop(0, 2 * chunks, products, 0)
            if inner == 0:
                with jax.named_scope("gag"):
                    finish(gfull.at[pl.ds(0, rank - gw)], p_send.at[1], p_recv.at[1])
                gfull[...] = gfull[...] + eye
                sweep(gfull, 0, rank // PIVOTS)

            def update(t, carry):
                j = t // 2
                mine = lax.rem(t, 2) == 0
                per = STEP // CHUNK

                def own_cols(i, carry):
                    k = j * per + i
                    for d in range(1, n_x):
                        xcopy(inner, k, d).wait_recv()
                    share = xslots[inner, 0, k]
                    for x in range(1, n_x):
                        share = share + xslots[inner, x, k]
                    step = jnp.dot(gfull[...], share, preferred_element_type=F32, precision=lax.Precision.HIGHEST)
                    cols = col_chunk(core, k)
                    value = c_out[:, cols] - step
                    c_out[:, cols] = value
                    spread(k).start()
                    prepare_cols(cols, value)
                    return carry

                def their_cols(i, carry):
                    k = j * per + i
                    spread(k).wait_recv()
                    cols = col_chunk(1 - core, k)
                    prepare_cols(cols, c_out[:, cols])
                    if inner:
                        errors(pl.ds(0, rows), rows, cols, CHUNK)
                    return carry

                @pl.when(mine)
                def _():
                    lax.fori_loop(0, per, own_cols, 0)

                @pl.when(jnp.logical_not(mine))
                def _():
                    lax.fori_loop(0, per, their_cols, 0)
                which = jnp.where(mine, core, 1 - core)

                @pl.when(mine | (inner == 0))
                def _():
                    errors(pl.ds(0, rows), rows, pl.ds(pl.multiple_of(which * half + j * STEP, STEP), STEP))
                return carry
            with jax.named_scope("update"):
                lax.fori_loop(0, loads, update, 0)
            send_limit(inner + 1)

            sent(cpart, c_send.at[0], c_recv.at[0, 0])
            sent(c_out.at[:, pl.ds(0, half)], c_send.at[1], c_recv.at[1, 0])
            sent(xslots.at[0, pl.ds(0, n_x - 1)], x_send, x_recv.at[0, 0])

        with jax.named_scope("hpart"):
            hi, lo = split(c_out[...].T)
            ctcat[:, :rank] = hi
            ctcat[:, rank:] = lo
            hpart[...] = quads(dot(ccat[...], ctcat[...]))
            start(hrs)

        @pl.when(jnp.logical_not(more))
        def _():
            c_out[...] = c_out[...] * jnp.sqrt(jnp.float32(rows * n_pts))
        limit = get_limit(INNER)

        def moment(part):
            hi, lo = split(jnp.clip(e[part, :], -limit, limit))
            return quads(dot(jnp.concatenate([hi, lo], 0), ctcat[...]))

        def over_y(d, h):
            return ycopy(0, d, h, half_of(ypart.at[d], h), half_of(yslots.at[d], h))

        def over_z(d, h):
            return zcopy(0, d, h, half_of(zpart.at[d], h), half_of(zslots.at[d - 1], h))

        def moments(t, carry):
            theirs = t < n_z
            d = far(t % n_z)
            value = moment(row_block(z_peer(d), jnp.where(theirs, 1 - sy, sy)))

            @pl.when(theirs)
            def _():
                ypart[d] = value
                over_y(d, 0).start()

            @pl.when(jnp.logical_not(theirs))
            def _():
                zpart[d] = value

            @pl.when(t == n_z - 1)
            def _():
                start([over_y(far(u), 1) for u in range(n_z)])

            @pl.when(t == 0)
            def _():
                finish(hslots, s_send.at[0], s_recv.at[0])
                own = hpart[pl.ds(sme * hw, hw), :]
                for j in range(1, n_snap):
                    own = own + hslots[j - 1]
                hred[...] = own
                hfull[pl.ds(sme * hw, hw), :] = own
                start(hag)
            return carry
        with jax.named_scope("moments"):
            lax.fori_loop(0, 2 * n_z, moments, 0)
        def forward(t, carry):
            d, h = far(t % n_z), t // n_z
            part = pl.ds(pl.multiple_of(h * rh, rh), rh)
            with jax.named_scope("ywait"):
                over_y(d, h).wait_recv()
            zpart[d, part, :] = zpart[d, part, :] + yslots[d, part, :]

            @pl.when(d > 0)
            def _():
                over_z(d, h).start()
            return carry
        lax.fori_loop(0, n_z, forward, 0)
        with jax.named_scope("hag"):
            finish(hfull.at[pl.ds(0, rank - hw)], s_send.at[1], s_recv.at[1])
        hfull[...] = hfull[...] + eye
        steps = rank // PIVOTS
        per = steps // n_z

        def sweep_forward(t, carry):
            sweep(hfull, t * per, per)
            return forward(n_z + t, carry)
        lax.fori_loop(0, n_z, sweep_forward, 0)
        sweep(hfull, per * n_z, steps - per * n_z)

        def modes_half(z, which, h):
            return m_out.at[pl.ds(pl.multiple_of((z * 2 + which) * rw + h * rh, rh), rh)]

        def gather(d, h):
            ref = modes_half(sz, sy, h)
            return zcopy(1, d, h, ref, ref)

        def pass_on(d, h):
            ref = modes_half(z_from(d), sy, h)
            return ycopy(1, d, h, ref, ref)

        def solve(h, carry):
            with jax.named_scope("zwait"):
                for d in range(1, n_z):
                    over_z(d, h).wait_recv()
            part = pl.ds(pl.multiple_of(h * rh, rh), rh)
            share = zpart[0, part, :]
            for d in range(1, n_z):
                share = share + zslots[d - 1, part, :]
            step = jnp.dot(share, hfull[...], preferred_element_type=F32, precision=lax.Precision.HIGHEST)
            mine = pl.ds(pl.multiple_of(sme * rw + h * rh, rh), rh)
            m_out[mine, :] = m_out[mine, :] - step
            start([gather(far(t), h) for t in range(n_z - 1)])
            pass_on(0, h).start()
            return carry
        lax.fori_loop(0, 2, solve, 0)

        def take(part):
            @pl.when(more)
            def _():
                prepare_rows(part)
                error_rows(part)
        take(own_rows)

        def near(u):
            return jnp.where(u == 0, 1, n_z - u)

        def first_half(u, carry):
            with jax.named_scope("gatherz"):
                gather(near(u), 0).wait_recv()
            pass_on(near(u), 0).start()
            return carry
        lax.fori_loop(0, n_z - 1, first_half, 0)

        def second_half(u, carry):
            with jax.named_scope("gatherz"):
                gather(near(u), 1).wait_recv()
            pass_on(near(u), 1).start()
            take(row_block(z_from(near(u)), sy))
            return carry
        lax.fori_loop(0, n_z - 1, second_half, 0)

        def other(u, carry):
            d = jnp.where(u == 0, 0, near(u - 1))
            with jax.named_scope("gathery"):
                pass_on(d, 0).wait_recv()
                pass_on(d, 1).wait_recv()
            take(row_block(z_from(d), 1 - sy))
            return carry
        with jax.named_scope("other"):
            lax.fori_loop(0, n_z, other, 0)

        @pl.when(more)
        def _():
            send_limit(0)
            gram_part()
            start(grs)
        with jax.named_scope("sends"):
            sent(ypart, y_send.at[0], y_recv.at[0, 0, 0])
            sent(m_out.at[pl.ds(0, n_z * rw)], y_send.at[1], y_recv.at[1, 0, 0])
            sent(zslots, z_send.at[0], z_recv.at[0, 0, 0])
            sent(m_out.at[pl.ds(0, (n_z - 1) * rw)], z_send.at[1], z_recv.at[1, 0, 0])
        return carry
    lax.fori_loop(0, OUTER, outer, 0)


def write_out(modes, amplitudes, m_hbm, a_hbm, sem):
    copies = [pltpu.make_async_copy(modes, m_hbm, sem.at[0]), pltpu.make_async_copy(amplitudes, a_hbm, sem.at[1])]
    for copy in copies:
        copy.start()
    for copy in copies:
        copy.wait()


def shards(n_pts, n_snap, snapshots, modes_init, coefs_init):
    rows, width = snapshots.shape
    rank = modes_init.shape[1]
    rw, gw, hw = rows // n_snap, rank // n_pts, rank // n_snap
    chunks, n_x, n_z, n_dev = width // 2 // CHUNK, n_pts // 2, n_snap // 2, n_pts * n_snap
    vmem, dma = pltpu.VMEM, pltpu.SemaphoreType.DMA
    scratch = [
        vmem((rows, width), F32), vmem((rows, width), F32),
        vmem((rows, 2 * rank), BF16), vmem((2 * rank, rows), BF16),
        vmem((2 * rank, width), BF16), vmem((width, 2 * rank), BF16),
        vmem((8, STEP), F32),
        vmem((rank, rank), F32), vmem((n_pts - 1, gw, rank), F32), vmem((gw, rank), F32), vmem((rank, rank), F32),
        vmem((rank, rank), F32), vmem((n_snap - 1, hw, rank), F32), vmem((hw, rank), F32), vmem((rank, rank), F32),
        vmem((INNER + 1, n_dev, 128), F32),
        vmem((chunks, rank, CHUNK), F32), vmem((INNER, chunks, rank, CHUNK), F32),
        vmem((INNER, n_x, chunks, rank, CHUNK), F32),
        vmem((n_z, rw, rank), F32), vmem((n_z, rw, rank), F32),
        vmem((n_z, rw, rank), F32), vmem((n_z - 1, rw, rank), F32),
        dma((2 + width // STEP,)),
        dma((2,)), dma((2,)),
        dma((2,)), dma((2,)),
        dma((2,)), dma((2, chunks)),
        dma, dma((chunks, n_x - 1)),
        dma((INNER + 1,)), dma((INNER + 1,)),
        dma((2,)), dma((2, n_z, 2)),
        dma((2,)), dma((2, n_z - 1, 2)),
    ]
    modes, coefs = pl.pallas_call(
        functools.partial(kernel, n_pts, n_snap),
        out_shape=(vmem((rows, rank), F32), vmem((rank, width), F32)),
        in_specs=[pl.BlockSpec(memory_space=pltpu.HBM)] * 3,
        out_specs=(pl.BlockSpec(memory_space=vmem), pl.BlockSpec(memory_space=vmem)),
        scratch_shapes=scratch,
        compiler_params=pltpu.CompilerParams(collective_id=0, has_side_effects=True, vmem_limit_bytes=67043328 - 5 * 256 * 1024),
    )(snapshots, modes_init, coefs_init)
    return pl.pallas_call(
        write_out,
        out_shape=(jax.ShapeDtypeStruct((rows, rank), F32), jax.ShapeDtypeStruct((rank, width), F32)),
        in_specs=[pl.BlockSpec(memory_space=pl.ANY)] * 2,
        out_specs=(pl.BlockSpec(memory_space=pltpu.HBM), pl.BlockSpec(memory_space=pltpu.HBM)),
        scratch_shapes=[dma((2,))],
    )(pltpu.with_memory_space_constraint(modes, vmem), pltpu.with_memory_space_constraint(coefs, vmem))


def solution(mesh):
    in_specs = (P("pts", "snap"), P("pts", None), P(None, "snap"))
    out_specs = (P("pts", None), P(None, "snap"))
    body = functools.partial(shards, mesh.shape["pts"], mesh.shape["snap"])
    return jax.shard_map(body, mesh=mesh, in_specs=in_specs, out_specs=out_specs, check_vma=False)
```

```python
import functools

import jax
import jax.numpy as jnp
from jax import lax
from jax.experimental import pallas as pl
from jax.experimental.pallas import tpu as pltpu
from jax.sharding import PartitionSpec as P

OUTER = 2
INNER = 2
PIVOTS = 16
CHUNK = 128
STEP = 256
LAG = 2

HUBER = 1.345
RIDGE = 0.01

F32 = jnp.float32
BF16 = jnp.bfloat16
MESH = pl.DeviceIdType.MESH


def split(x):
    hi = x.astype(BF16)
    lo = (x - hi.astype(F32)).astype(BF16)
    return hi, lo


def split3(x):
    hi = x.astype(BF16)
    rest = x - hi.astype(F32)
    mid = rest.astype(BF16)
    lo = (rest - mid.astype(F32)).astype(BF16)
    return hi, mid, lo


def dot(a, b):
    return jnp.dot(a, b, preferred_element_type=F32)


def quads(x):
    r, c = x.shape[0] // 2, x.shape[1] // 2
    return (x[:r, :c] + x[:r, c:]) + (x[r:, :c] + x[r:, c:])


def kernel(n_pts, n_snap, s_hbm, m_hbm, c_hbm, m_out, c_out,
           s, e, s_far, e_far, m_far, c_now, c_far, mcat, mtcat, ccat, ccat_far, ctcat, sq,
           gslots, gfull, hpart, hslots, hred, hfull,
           lslots, xslots, opart, oslots, ypart, yslots, zpart, zslots,
           load_sem, g_send, g_recv, h_send, h_recv, c_send, c_recv, x_send, x_recv,
           l_send, l_recv, y_send, y_recv, z_send, z_recv):
    rows, rank = m_out.shape
    width = c_out.shape[1]
    pme = lax.axis_index("pts")
    sme = lax.axis_index("snap")
    n_dev = n_pts * n_snap
    me = pme * n_snap + sme
    rw = rows // n_snap
    rh = rw // 2
    half = width // 2
    chunks = half // CHUNK
    n_x, n_z = n_pts // 2, n_snap // 2
    px, core = pme // 2, lax.rem(pme, 2)
    sz, sy = sme // 2, lax.rem(sme, 2)
    group = 2 * n_snap
    gme = core * n_snap + sme
    hw = rank // group
    count = float(rows * n_pts * width * n_snap)
    loads = half // STEP
    whole = pl.ds(0, 2 * rows)
    own_points = pl.ds(pl.multiple_of(core * rows, rows), rows)
    far_points = pl.ds(pl.multiple_of((1 - core) * rows, rows), rows)

    def offset(d):
        dx, dc, dz, dy = d
        return {"pts": lax.rem(px + dx, n_x) * 2 + lax.rem(core + dc, 2),
                "snap": lax.rem(sz + dz, n_z) * 2 + lax.rem(sy + dy, 2)}

    def hops(d):
        dx, dc, dz, dy = d
        return min(dx, n_x - dx) + dy + min(dz, n_z - dz) + 0.1 * dc
    others = [(dx, dc, dz, dy) for dx in range(n_x) for dc in range(2) for dz in range(n_z) for dy in range(2)][1:]
    others.sort(key=lambda d: -hops(d))

    barrier = pltpu.get_barrier_semaphore()
    for d in others:
        pl.semaphore_signal(barrier, inc=1, device_id=offset(d), device_id_type=MESH)

    def step_cols(j):
        return pl.ds(pl.multiple_of(j * STEP, STEP), STEP)

    def snap_cols(which, j):
        return pl.ds(pl.multiple_of(which * half + j * STEP, STEP), STEP)

    def load_own(j):
        return pltpu.make_async_copy(
            s_hbm.at[:, snap_cols(core, j)], s.at[own_points, step_cols(j)], load_sem.at[3 + j])

    def load_far(j):
        return pltpu.make_async_copy(
            s_hbm.at[:, snap_cols(1 - core, j)], s_far.at[:, step_cols(j)], load_sem.at[3 + loads + j])

    def side(which):
        return pl.ds(pl.multiple_of(which * half, half), half)
    load_m = pltpu.make_async_copy(m_hbm, m_out, load_sem.at[0])
    load_c = pltpu.make_async_copy(c_hbm.at[:, side(core)], c_now, load_sem.at[1])
    load_c_far = pltpu.make_async_copy(c_hbm.at[:, side(1 - core)], c_far, load_sem.at[2])
    start_all = [load_m, load_c] + [load_own(j) for j in range(loads)] + [load_c_far] + [load_far(j) for j in range(loads)]
    for copy in start_all:
        copy.start()

    def gcopy(d):
        ref = gslots.at[px]
        return pltpu.make_async_remote_copy(
            src_ref=ref, dst_ref=ref, send_sem=g_send, recv_sem=g_recv.at[d - 1],
            device_id={"pts": lax.rem(px + d, n_x) * 2 + core}, device_id_type=MESH)

    def hcopy(site, j, src, dst):
        peer = lax.rem(gme + j, group)
        return pltpu.make_async_remote_copy(
            src_ref=src, dst_ref=dst, send_sem=h_send.at[site], recv_sem=h_recv.at[site],
            device_id={"pts": px * 2 + peer // n_snap, "snap": lax.rem(peer, n_snap)}, device_id_type=MESH)

    def h_rows(g):
        return pl.ds(pl.multiple_of(g * hw, hw), hw)

    def ccopy(site, k, src, dst):
        return pltpu.make_async_remote_copy(
            src_ref=src, dst_ref=dst, send_sem=c_send.at[site + k if site == 2 else site], recv_sem=c_recv.at[min(site, 3), k],
            device_id={"pts": px * 2 + 1 - core}, device_id_type=MESH)

    def xcopy(site, k, d):
        ref = xslots.at[site, px, k]
        return pltpu.make_async_remote_copy(
            src_ref=ref, dst_ref=ref, send_sem=x_send, recv_sem=x_recv.at[k, d - 1],
            device_id={"pts": lax.rem(px + d, n_x) * 2 + core}, device_id_type=MESH)

    def lcopy(use, i):
        ref = lslots.at[use, pl.ds(me, 1)]
        return pltpu.make_async_remote_copy(
            src_ref=ref, dst_ref=ref, send_sem=l_send.at[use], recv_sem=l_recv.at[use],
            device_id=offset(others[i]), device_id_type=MESH)

    def lwait(use):
        ref = lslots.at[use, pl.ds(0, n_dev - 1)]
        return pltpu.make_async_remote_copy(
            src_ref=ref, dst_ref=ref, send_sem=l_send.at[use], recv_sem=l_recv.at[use],
            device_id=offset(others[0]), device_id_type=MESH)

    def half_of(ref, h):
        return ref.at[pl.ds(pl.multiple_of(h * rh, rh), rh)]

    def ycopy(site, d, h, src, dst):
        return pltpu.make_async_remote_copy(
            src_ref=src, dst_ref=dst, send_sem=y_send.at[site], recv_sem=y_recv.at[site, d, h],
            device_id={"snap": sz * 2 + 1 - sy}, device_id_type=MESH)

    def zcopy(site, d, h, src, dst):
        return pltpu.make_async_remote_copy(
            src_ref=src, dst_ref=dst, send_sem=z_send.at[site], recv_sem=z_recv.at[site, d - 1, h],
            device_id={"snap": z_peer(d) * 2 + sy}, device_id_type=MESH)

    def z_peer(d):
        return (sz // 2 + d // 2) % (n_z // 2) * 2 + (sz + d) % 2

    def z_from(d):
        return (sz // 2 + n_z // 2 - d // 2) % (n_z // 2) * 2 + (sz + d) % 2

    def row_block(z, which):
        return (z * 2 + which) * rw

    def far(t):
        return n_z - 1 - t

    def start(copies):
        for copy in copies:
            copy.start()

    def all_of(ref, send_sem, recv_sem):
        return pltpu.make_async_remote_copy(
            src_ref=ref, dst_ref=ref, send_sem=send_sem, recv_sem=recv_sem,
            device_id={"pts": px * 2 + 1 - core}, device_id_type=MESH)

    def finish(ref, send_sem, recv_sem):
        all_of(ref, send_sem, recv_sem).wait_recv()
        all_of(ref, send_sem, recv_sem).wait_send()

    def sent(ref, send_sem, recv_sem):
        all_of(ref, send_sem, recv_sem).wait_send()

    def prepare_rows(part, value):
        hi, lo = split(value)
        mcat[part, :rank] = hi
        mcat[part, rank:] = lo

    def prepare_mt():
        for ref, part in ((m_out, own_points), (m_far, far_points)):
            hi, lo = split(ref[...].T)
            mtcat[:rank, part] = hi
            mtcat[rank:, part] = lo

    def prepare_cols(ref, cols, value):
        hi, lo = split(value)
        ref[:rank, cols] = hi
        ref[rank:, cols] = lo

    def sweep(ref, base, steps):
        sub = lax.broadcasted_iota(jnp.int32, (PIVOTS, rank), 0)
        lane = lax.broadcasted_iota(jnp.int32, (PIVOTS, rank), 1)
        wide = lax.broadcasted_iota(jnp.int32, (rank, rank), 1)
        side = sub[:, :1]

        def body(t, carry):
            k = (base + t) * PIVOTS
            rws = pl.ds(pl.multiple_of(k, PIVOTS), PIVOTS)
            before = ref[rws, :]
            after = before
            cols = [jnp.sum(jnp.where(lane == k + p, before, 0.0), axis=1, keepdims=True) for p in range(PIVOTS)]
            for p in range(PIVOTS):
                col = cols[p]
                inv = 1.0 / col[p:p + 1, :]
                row = after[p:p + 1, :] * inv
                for q in range(p + 1, PIVOTS):
                    f = cols[q][p:p + 1, :] * inv
                    cols[q] = jnp.where(side == p, f, cols[q] - col * f)
                after = jnp.where(lane == k + p, col * inv, after - col * row)
                after = jnp.where(sub == p, jnp.where(lane == k + p, -inv, row), after)
            h, m, l = split3(before)
            a, b, c = split3(after)
            change = lax.dot_general(
                jnp.concatenate([h, h, m, h, m, l], 0), jnp.concatenate([a, b, a, c, b, a], 0),
                (((0,), (0,)), ((), ())), preferred_element_type=F32)
            ref[...] = jnp.where((wide >= k) & (wide < k + PIVOTS), 0.0, ref[...]) - change
            ref[rws, :] = after
            return carry
        with jax.named_scope("sweep"):
            lax.fori_loop(0, steps, body, 0)

    def errors(src, dst, part, m_part, n_rows, c_ref, cols, n_cols):
        c = jnp.concatenate([c_ref[:rank, cols], c_ref[rank:, cols]], 1)
        fit = dot(mcat[m_part, :], jnp.concatenate([c, c], 0))
        err = src[part, cols] - (fit[:, :n_cols] + fit[:, n_cols:])
        dst[part, cols] = err
        sq[:, :n_cols] += jnp.sum((err * err).reshape(n_rows // 8, 8, n_cols), axis=0)

    def error_rows(part):
        hi, lo = mcat[part, :rank], mcat[part, rank:]
        both = jnp.concatenate([jnp.concatenate([hi, hi], 1), jnp.concatenate([lo, lo], 1)], 0)
        for j in range(loads):
            cols = pl.ds(j * STEP, STEP)
            fit = dot(both, ccat[:, cols])
            err = s[part, cols] - (fit[:rw] + fit[rw:])
            e[part, cols] = err
            sq[...] += jnp.sum((err * err).reshape(rw // 8, 8, STEP), axis=0)

    def send_limit(use):
        acc = sq[:, :128]
        for k in range(1, STEP // 128):
            acc = acc + sq[:, k * 128:(k + 1) * 128]
        lslots[use, pl.ds(me, 1), :] = jnp.sum(acc, axis=0, keepdims=True)
        start([lcopy(use, i) for i in range(n_dev - 1)])
        sq[...] = jnp.zeros_like(sq)

    def get_limit(use):
        with jax.named_scope("limit"):
            lwait(use).wait_recv()
        total = jnp.sum(jnp.sum(lslots[use], axis=0, keepdims=True), axis=1, keepdims=True)
        lwait(use).wait_send()
        return HUBER * jnp.sqrt(total / count + 1e-06)

    eye = (lax.broadcasted_iota(jnp.int32, (rank, rank), 0)
           == lax.broadcasted_iota(jnp.int32, (rank, rank), 1)).astype(F32) * RIDGE

    hrs = [hcopy(0, j, hpart.at[h_rows(lax.rem(gme + j, group))], hslots.at[j - 1]) for j in range(1, group)]
    hag = [hcopy(1, j, hred, hfull.at[h_rows(gme)]) for j in range(1, group)]

    def gram_part():
        prepare_mt()
        gslots[px] = quads(dot(mtcat[...], mcat[...]))
        start([gcopy(d) for d in range(1, n_x)])

    sq[...] = jnp.zeros_like(sq)
    load_m.wait()
    prepare_rows(own_points, m_out[...])
    load_c.wait()
    prepare_cols(ccat, pl.ds(0, half), c_now[...])
    with jax.named_scope("err0"):
        def first_own(j, carry):
            load_own(j).wait()
            errors(s, e, own_points, own_points, rows, ccat, step_cols(j), STEP)
            return carry
        lax.fori_loop(0, loads, first_own, 0)
        load_c_far.wait()
        prepare_cols(ccat_far, pl.ds(0, half), c_far[...])

        def first_far(j, carry):
            load_far(j).wait()
            errors(s_far, e_far, pl.ds(0, rows), own_points, rows, ccat_far, step_cols(j), STEP)
            return carry
        lax.fori_loop(0, loads, first_far, 0)
    with jax.named_scope("barrier"):
        pl.semaphore_wait(barrier, n_dev - 1)
    send_limit(0)
    swap = [ccopy(2, 0, m_out, m_far), ccopy(2, 1, e_far, e.at[own_points]), ccopy(2, 2, s_far, s.at[own_points])]
    start(swap)
    with jax.named_scope("mswap"):
        swap[0].wait_recv()
    prepare_rows(far_points, m_far[...])
    gram_part()

    amplitudes = ccopy(5, 0, c_out.at[:, side(core)], c_out.at[:, side(core)])

    def outer(o, carry):
        more = o < OUTER - 1

        for inner in range(INNER):
            limit = get_limit(inner)

            if inner == 0:
                @pl.when(o == 0)
                def _():
                    with jax.named_scope("eswap"):
                        swap[1].wait_recv()

            def products(k, carry):
                cols = pl.ds(pl.multiple_of(k * CHUNK, CHUNK), CHUNK)
                hi, lo = split(jnp.clip(e[:, cols], -limit, limit))
                xslots[inner, px, k] = quads(dot(mtcat[...], jnp.concatenate([hi, lo], 1)))
                for d in range(1, n_x):
                    xcopy(inner, k, d).start()
                return carry
            with jax.named_scope("products"):
                lax.fori_loop(0, chunks, products, 0)
            if inner == 0:
                with jax.named_scope("gwait"):
                    for d in range(1, n_x):
                        gcopy(d).wait_recv()
                total = gslots[0]
                for x in range(1, n_x):
                    total = total + gslots[x]
                gfull[...] = total + eye
                sent(gslots.at[pl.ds(0, n_x - 1)], g_send, g_recv.at[0])
                sweep(gfull, 0, rank // PIVOTS)

                @pl.when(o == 0)
                def _():
                    with jax.named_scope("sswap"):
                        swap[2].wait_recv()
                    sent(m_out, c_send.at[2], c_recv.at[2, 0])
                    sent(e_far, c_send.at[3], c_recv.at[2, 1])
                    sent(s_far, c_send.at[4], c_recv.at[2, 2])
            wide = CHUNK

            def update(j, carry):
                def own_cols(i, carry):
                    k = j * (wide // CHUNK) + i
                    with jax.named_scope("xw"):
                        for d in range(1, n_x):
                            xcopy(inner, k, d).wait_recv()
                    share = xslots[inner, 0, k]
                    for x in range(1, n_x):
                        share = share + xslots[inner, x, k]
                    step = jnp.dot(gfull[...], share, preferred_element_type=F32, precision=lax.Precision.HIGHEST)
                    cols = pl.ds(pl.multiple_of(k * CHUNK, CHUNK), CHUNK)
                    value = c_now[:, cols] - step
                    c_now[:, cols] = value
                    prepare_cols(ccat, cols, value)
                    return carry
                lax.fori_loop(0, wide // CHUNK, own_cols, 0)
                errors(s, e, whole, whole, 2 * rows, ccat, pl.ds(pl.multiple_of(j * wide, wide), wide), wide)
                return carry
            with jax.named_scope("update"):
                lax.fori_loop(0, half // wide, update, 0)
            send_limit(inner + 1)

            sent(xslots.at[0, pl.ds(0, n_x - 1)], x_send, x_recv.at[0, 0])

        with jax.named_scope("hpart"):
            hi, lo = split(c_now[...].T)
            ctcat[:, :rank] = hi
            ctcat[:, rank:] = lo
            hpart[...] = quads(dot(ccat[...], ctcat[...]))
            start(hrs)

        @pl.when(jnp.logical_not(more))
        def _():
            c_out[:, side(core)] = c_now[...] * jnp.sqrt(jnp.float32(rows * n_pts))
            amplitudes.start()
        limit = get_limit(INNER)

        def moment(block):
            parts = []
            for q in (1 - core, core):
                part = pl.ds(pl.multiple_of(q * rows + block, rw), rw)
                parts += split(jnp.clip(e[part, :], -limit, limit))
            both = dot(jnp.concatenate(parts, 0), ctcat[...])
            return quads(both[:2 * rw]), quads(both[2 * rw:])

        def over_y(d, h):
            return ycopy(0, d, h, half_of(ypart.at[d], h), half_of(yslots.at[d], h))

        def over_z(d, h):
            return zcopy(0, d, h, half_of(zpart.at[d], h), half_of(zslots.at[d - 1], h))

        def across(t):
            return ccopy(0, t, opart.at[t], oslots.at[t])

        def moments(t, carry):
            @pl.when(t < 2 * n_z)
            def _():
                theirs = t < n_z
                block = row_block(z_peer(far(t % n_z)), jnp.where(theirs, 1 - sy, sy))
                opart[t], value = moment(block)
                across(t).start()

                @pl.when(theirs)
                def _():
                    ypart[far(t % n_z)] = value

                @pl.when(jnp.logical_not(theirs))
                def _():
                    zpart[far(t % n_z)] = value

            @pl.when(t == 1)
            def _():
                finish(hslots, h_send.at[0], h_recv.at[0])
                own = hpart[h_rows(gme), :]
                for j in range(1, group):
                    own = own + hslots[j - 1]
                hred[...] = own
                hfull[h_rows(gme), :] = own
                start(hag)

            @pl.when(t >= LAG)
            def _():
                u = t - LAG
                d = far(u % n_z)
                across(u).wait_recv()

                @pl.when(u < n_z)
                def _():
                    ypart[d] = ypart[d] + oslots[u]
                    over_y(d, 0).start()

                @pl.when(u >= n_z)
                def _():
                    zpart[d] = zpart[d] + oslots[u]

                @pl.when(u == n_z - 1)
                def _():
                    start([over_y(far(v), 1) for v in range(n_z)])
            return carry
        with jax.named_scope("moments"):
            lax.fori_loop(0, 2 * n_z + LAG, moments, 0)

        def forward(t, carry):
            d, h = far(t % n_z), t // n_z
            part = pl.ds(pl.multiple_of(h * rh, rh), rh)
            with jax.named_scope("ywait"):
                over_y(d, h).wait_recv()
            zpart[d, part, :] = zpart[d, part, :] + yslots[d, part, :]

            @pl.when(d > 0)
            def _():
                over_z(d, h).start()
            return carry
        lax.fori_loop(0, n_z, forward, 0)
        with jax.named_scope("hag"):
            finish(hfull.at[pl.ds(0, rank - hw)], h_send.at[1], h_recv.at[1])
        hfull[...] = hfull[...] + eye
        steps = rank // PIVOTS
        per = steps // n_z

        def sweep_forward(t, carry):
            sweep(hfull, t * per, per)
            return forward(n_z + t, carry)
        lax.fori_loop(0, n_z, sweep_forward, 0)
        sweep(hfull, per * n_z, steps - per * n_z)

        def modes_half(z, which, h):
            return m_out.at[pl.ds(pl.multiple_of((z * 2 + which) * rw + h * rh, rh), rh)]

        def gather(d, h):
            ref = modes_half(sz, sy, h)
            return zcopy(1, d, h, ref, ref)

        def pass_on(d, h):
            ref = modes_half(z_from(d), sy, h)
            return ycopy(1, d, h, ref, ref)

        def solve(h, carry):
            with jax.named_scope("zwait"):
                for d in range(1, n_z):
                    over_z(d, h).wait_recv()
            part = pl.ds(pl.multiple_of(h * rh, rh), rh)
            share = zpart[0, part, :]
            for d in range(1, n_z):
                share = share + zslots[d - 1, part, :]
            step = jnp.dot(share, hfull[...], preferred_element_type=F32, precision=lax.Precision.HIGHEST)
            mine = pl.ds(pl.multiple_of(sme * rw + h * rh, rh), rh)
            m_out[mine, :] = m_out[mine, :] - step
            start([gather(far(t), h) for t in range(n_z - 1)])
            pass_on(0, h).start()
            return carry
        lax.fori_loop(0, 2, solve, 0)

        def near(u):
            return jnp.where(u == 0, 1, n_z - u)

        def block_of(i):
            u = i % n_z
            d = jnp.where(u == 0, 0, near(u - 1))
            return d, row_block(z_from(d), jnp.where(i < n_z, sy, 1 - sy))

        def hand_over(i):
            part = pl.ds(pl.multiple_of(block_of(i)[1], rw), rw)
            return ccopy(1, i, m_out.at[part], m_far.at[part])

        def take(ref, which, i):
            block = block_of(i)[1]
            part = pl.ds(pl.multiple_of(which * rows + block, rw), rw)
            prepare_rows(part, ref[pl.ds(pl.multiple_of(block, rw), rw), :])
            error_rows(part)

        def take_own(i):
            @pl.when(more)
            def _():
                hand_over(i).start()
                take(m_out, core, i)

        def take_far(i):
            @pl.when(more)
            def _():
                with jax.named_scope("farwait"):
                    hand_over(i).wait_recv()
                take(m_far, 1 - core, i)
        take_own(0)

        def first_half(u, carry):
            with jax.named_scope("gatherz"):
                gather(near(u), 0).wait_recv()
            pass_on(near(u), 0).start()
            return carry
        lax.fori_loop(0, n_z - 1, first_half, 0)

        def second_half(u, carry):
            with jax.named_scope("gatherz"):
                gather(near(u), 1).wait_recv()
            pass_on(near(u), 1).start()
            take_own(1 + u)
            return carry
        lax.fori_loop(0, n_z - 1, second_half, 0)

        def other(u, carry):
            take_far(u)
            d = block_of(u)[0]
            with jax.named_scope("gathery"):
                pass_on(d, 0).wait_recv()
                pass_on(d, 1).wait_recv()
            take_own(n_z + u)
            return carry
        with jax.named_scope("other"):
            lax.fori_loop(0, n_z, other, 0)

        def last(u, carry):
            take_far(n_z + u)
            return carry
        lax.fori_loop(0, n_z, last, 0)

        @pl.when(more)
        def _():
            send_limit(0)
            gram_part()
            sent(m_out, c_send.at[1], c_recv.at[1, 0])
        with jax.named_scope("sends"):
            sent(opart, c_send.at[0], c_recv.at[0, 0])
            sent(ypart, y_send.at[0], y_recv.at[0, 0, 0])
            sent(m_out.at[pl.ds(0, n_z * rw)], y_send.at[1], y_recv.at[1, 0, 0])
            sent(zslots, z_send.at[0], z_recv.at[0, 0, 0])
            sent(m_out.at[pl.ds(0, (n_z - 1) * rw)], z_send.at[1], z_recv.at[1, 0, 0])
        return carry
    lax.fori_loop(0, OUTER, outer, 0)
    amplitudes.wait_recv()
    amplitudes.wait_send()


def write_out(modes, amplitudes, m_hbm, a_hbm, sem):
    copies = [pltpu.make_async_copy(modes, m_hbm, sem.at[0]), pltpu.make_async_copy(amplitudes, a_hbm, sem.at[1])]
    for copy in copies:
        copy.start()
    for copy in copies:
        copy.wait()


def shards(n_pts, n_snap, snapshots, modes_init, coefs_init):
    rows, width = snapshots.shape
    rank = modes_init.shape[1]
    rw, half, group = rows // n_snap, width // 2, 2 * n_snap
    chunks, n_x, n_z, n_dev = half // CHUNK, n_pts // 2, n_snap // 2, n_pts * n_snap
    hw = rank // group
    vmem, dma = pltpu.VMEM, pltpu.SemaphoreType.DMA
    scratch = [
        vmem((2 * rows, half), F32), vmem((2 * rows, half), F32), vmem((rows, half), F32), vmem((rows, half), F32),
        vmem((rows, rank), F32), vmem((rank, half), F32), vmem((rank, half), F32),
        vmem((2 * rows, 2 * rank), BF16), vmem((2 * rank, 2 * rows), BF16),
        vmem((2 * rank, half), BF16), vmem((2 * rank, half), BF16), vmem((half, 2 * rank), BF16),
        vmem((8, STEP), F32),
        vmem((n_x, rank, rank), F32), vmem((rank, rank), F32),
        vmem((rank, rank), F32), vmem((group - 1, hw, rank), F32), vmem((hw, rank), F32), vmem((rank, rank), F32),
        vmem((INNER + 1, n_dev, 128), F32),
        vmem((INNER, n_x, chunks, rank, CHUNK), F32),
        vmem((n_snap, rw, rank), F32), vmem((n_snap, rw, rank), F32),
        vmem((n_z, rw, rank), F32), vmem((n_z, rw, rank), F32),
        vmem((n_z, rw, rank), F32), vmem((n_z - 1, rw, rank), F32),
        dma((3 + width // STEP,)),
        dma, dma((n_x - 1,)),
        dma((2,)), dma((2,)),
        dma((6,)), dma((4, n_snap)),
        dma, dma((chunks, n_x - 1)),
        dma((INNER + 1,)), dma((INNER + 1,)),
        dma((2,)), dma((2, n_z, 2)),
        dma((2,)), dma((2, n_z - 1, 2)),
    ]
    modes, coefs = pl.pallas_call(
        functools.partial(kernel, n_pts, n_snap),
        out_shape=(vmem((rows, rank), F32), vmem((rank, width), F32)),
        in_specs=[pl.BlockSpec(memory_space=pltpu.HBM)] * 3,
        out_specs=(pl.BlockSpec(memory_space=vmem), pl.BlockSpec(memory_space=vmem)),
        scratch_shapes=scratch,
        compiler_params=pltpu.CompilerParams(collective_id=0, has_side_effects=True, vmem_limit_bytes=67043328 - 5 * 256 * 1024),
    )(snapshots, modes_init, coefs_init)
    return pl.pallas_call(
        write_out,
        out_shape=(jax.ShapeDtypeStruct((rows, rank), F32), jax.ShapeDtypeStruct((rank, width), F32)),
        in_specs=[pl.BlockSpec(memory_space=pl.ANY)] * 2,
        out_specs=(pl.BlockSpec(memory_space=pltpu.HBM), pl.BlockSpec(memory_space=pltpu.HBM)),
        scratch_shapes=[dma((2,))],
    )(pltpu.with_memory_space_constraint(modes, vmem), pltpu.with_memory_space_constraint(coefs, vmem))


def solution(mesh):
    in_specs = (P("pts", "snap"), P("pts", None), P(None, "snap"))
    out_specs = (P("pts", None), P(None, "snap"))
    body = functools.partial(shards, mesh.shape["pts"], mesh.shape["snap"])
    return jax.shard_map(body, mesh=mesh, in_specs=in_specs, out_specs=out_specs, check_vma=False)
```

```python
import functools

import jax
import jax.numpy as jnp
from jax import lax
from jax.experimental import pallas as pl
from jax.experimental.pallas import tpu as pltpu
from jax.sharding import PartitionSpec as P

OUTER = 2
INNER = 2
PIVOTS = 16
CHUNK = 128
STEP = 256
LAG = 3

HUBER = 1.345
RIDGE = 0.01

F32 = jnp.float32
BF16 = jnp.bfloat16
MESH = pl.DeviceIdType.MESH


def split(x):
    hi = x.astype(BF16)
    lo = (x - hi.astype(F32)).astype(BF16)
    return hi, lo


def split3(x):
    hi = x.astype(BF16)
    rest = x - hi.astype(F32)
    mid = rest.astype(BF16)
    lo = (rest - mid.astype(F32)).astype(BF16)
    return hi, mid, lo


def dot(a, b):
    return jnp.dot(a, b, preferred_element_type=F32)


def quads(x):
    r, c = x.shape[0] // 2, x.shape[1] // 2
    return (x[:r, :c] + x[:r, c:]) + (x[r:, :c] + x[r:, c:])


def kernel(n_pts, n_snap, s_hbm, m_hbm, c_hbm, m_out, c_out,
           s, e, s_far, e_far, m_far, c_now, c_far, mcat, mtcat, ccat, ccat_far, ctcat, sq,
           gslots, gfull, hpart, hslots, hred, hfull,
           lslots, xslots, opart, oslots, ypart, yslots, zpart, zslots,
           load_sem, g_send, g_recv, h_send, h_recv, c_send, c_recv, x_send, x_recv,
           l_send, l_recv, y_send, y_recv, z_send, z_recv):
    rows, rank = m_out.shape
    width = c_out.shape[1]
    pme = lax.axis_index("pts")
    sme = lax.axis_index("snap")
    n_dev = n_pts * n_snap
    me = pme * n_snap + sme
    rw = rows // n_snap
    rh = rw // 2
    half = width // 2
    chunks = half // CHUNK
    n_x, n_z = n_pts // 2, n_snap // 2
    px, core = pme // 2, lax.rem(pme, 2)
    sz, sy = sme // 2, lax.rem(sme, 2)
    group = 2 * n_snap
    gme = core * n_snap + sme
    hw = rank // group
    count = float(rows * n_pts * width * n_snap)
    loads = half // STEP
    whole = pl.ds(0, 2 * rows)
    own_points = pl.ds(pl.multiple_of(core * rows, rows), rows)
    far_points = pl.ds(pl.multiple_of((1 - core) * rows, rows), rows)

    def offset(d):
        dx, dc, dz, dy = d
        return {"pts": lax.rem(px + dx, n_x) * 2 + lax.rem(core + dc, 2),
                "snap": lax.rem(sz + dz, n_z) * 2 + lax.rem(sy + dy, 2)}

    def hops(d):
        dx, dc, dz, dy = d
        return min(dx, n_x - dx) + dy + min(dz, n_z - dz) + 0.1 * dc
    others = [(dx, dc, dz, dy) for dx in range(n_x) for dc in range(2) for dz in range(n_z) for dy in range(2)][1:]
    others.sort(key=lambda d: -hops(d))

    barrier = pltpu.get_barrier_semaphore()
    for d in others:
        pl.semaphore_signal(barrier, inc=1, device_id=offset(d), device_id_type=MESH)

    def step_cols(j):
        return pl.ds(pl.multiple_of(j * STEP, STEP), STEP)

    def snap_cols(which, j):
        return pl.ds(pl.multiple_of(which * half + j * STEP, STEP), STEP)

    def load_own(j):
        return pltpu.make_async_copy(
            s_hbm.at[:, snap_cols(core, j)], s.at[own_points, step_cols(j)], load_sem.at[3 + j])

    def load_far(j):
        return pltpu.make_async_copy(
            s_hbm.at[:, snap_cols(1 - core, j)], s_far.at[:, step_cols(j)], load_sem.at[3 + loads + j])

    def side(which):
        return pl.ds(pl.multiple_of(which * half, half), half)
    load_m = pltpu.make_async_copy(m_hbm, m_out, load_sem.at[0])
    load_c = pltpu.make_async_copy(c_hbm.at[:, side(core)], c_now, load_sem.at[1])
    load_c_far = pltpu.make_async_copy(c_hbm.at[:, side(1 - core)], c_far, load_sem.at[2])
    start_all = [load_m, load_c] + [load_own(j) for j in range(loads)] + [load_c_far] + [load_far(j) for j in range(loads)]
    for copy in start_all:
        copy.start()

    def gcopy(d):
        ref = gslots.at[px]
        return pltpu.make_async_remote_copy(
            src_ref=ref, dst_ref=ref, send_sem=g_send, recv_sem=g_recv.at[d - 1],
            device_id={"pts": lax.rem(px + d, n_x) * 2 + core}, device_id_type=MESH)

    def hcopy(site, j, src, dst):
        peer = lax.rem(gme + j, group)
        return pltpu.make_async_remote_copy(
            src_ref=src, dst_ref=dst, send_sem=h_send.at[site], recv_sem=h_recv.at[site],
            device_id={"pts": px * 2 + peer // n_snap, "snap": lax.rem(peer, n_snap)}, device_id_type=MESH)

    def h_rows(g):
        return pl.ds(pl.multiple_of(g * hw, hw), hw)

    def ccopy(site, k, src, dst):
        return pltpu.make_async_remote_copy(
            src_ref=src, dst_ref=dst, send_sem=c_send.at[site + k if site == 2 else site], recv_sem=c_recv.at[min(site, 3), k],
            device_id={"pts": px * 2 + 1 - core}, device_id_type=MESH)

    def xcopy(site, k, d):
        ref = xslots.at[site, px, k]
        return pltpu.make_async_remote_copy(
            src_ref=ref, dst_ref=ref, send_sem=x_send, recv_sem=x_recv.at[k, d - 1],
            device_id={"pts": lax.rem(px + d, n_x) * 2 + core}, device_id_type=MESH)

    def lcopy(use, i):
        ref = lslots.at[use, pl.ds(me, 1)]
        return pltpu.make_async_remote_copy(
            src_ref=ref, dst_ref=ref, send_sem=l_send.at[use], recv_sem=l_recv.at[use],
            device_id=offset(others[i]), device_id_type=MESH)

    def lwait(use):
        ref = lslots.at[use, pl.ds(0, n_dev - 1)]
        return pltpu.make_async_remote_copy(
            src_ref=ref, dst_ref=ref, send_sem=l_send.at[use], recv_sem=l_recv.at[use],
            device_id=offset(others[0]), device_id_type=MESH)

    def half_of(ref, h):
        return ref.at[pl.ds(pl.multiple_of(h * rh, rh), rh)]

    def ycopy(site, d, h, src, dst):
        return pltpu.make_async_remote_copy(
            src_ref=src, dst_ref=dst, send_sem=y_send.at[site], recv_sem=y_recv.at[site, d, h],
            device_id={"snap": sz * 2 + 1 - sy}, device_id_type=MESH)

    def zcopy(site, d, h, src, dst):
        return pltpu.make_async_remote_copy(
            src_ref=src, dst_ref=dst, send_sem=z_send.at[site], recv_sem=z_recv.at[site, d - 1, h],
            device_id={"snap": z_peer(d) * 2 + sy}, device_id_type=MESH)

    def z_peer(d):
        return (sz // 2 + d // 2) % (n_z // 2) * 2 + (sz + d) % 2

    def z_from(d):
        return (sz // 2 + n_z // 2 - d // 2) % (n_z // 2) * 2 + (sz + d) % 2

    def row_block(z, which):
        return (z * 2 + which) * rw

    def far(t):
        return n_z - 1 - t

    def start(copies):
        for copy in copies:
            copy.start()

    def all_of(ref, send_sem, recv_sem):
        return pltpu.make_async_remote_copy(
            src_ref=ref, dst_ref=ref, send_sem=send_sem, recv_sem=recv_sem,
            device_id={"pts": px * 2 + 1 - core}, device_id_type=MESH)

    def finish(ref, send_sem, recv_sem):
        all_of(ref, send_sem, recv_sem).wait_recv()
        all_of(ref, send_sem, recv_sem).wait_send()

    def sent(ref, send_sem, recv_sem):
        all_of(ref, send_sem, recv_sem).wait_send()

    def prepare_rows(part, value):
        hi, lo = split(value)
        mcat[part, :rank] = hi
        mcat[part, rank:] = lo

    def prepare_mt():
        for ref, part in ((m_out, own_points), (m_far, far_points)):
            hi, lo = split(ref[...].T)
            mtcat[:rank, part] = hi
            mtcat[rank:, part] = lo

    def prepare_cols(ref, cols, value):
        hi, lo = split(value)
        ref[:rank, cols] = hi
        ref[rank:, cols] = lo

    def sweep(ref, base, steps):
        sub = lax.broadcasted_iota(jnp.int32, (PIVOTS, rank), 0)
        lane = lax.broadcasted_iota(jnp.int32, (PIVOTS, rank), 1)
        wide = lax.broadcasted_iota(jnp.int32, (rank, rank), 1)
        side = sub[:, :1]

        def body(t, carry):
            k = (base + t) * PIVOTS
            rws = pl.ds(pl.multiple_of(k, PIVOTS), PIVOTS)
            before = ref[rws, :]
            after = before
            cols = [jnp.sum(jnp.where(lane == k + p, before, 0.0), axis=1, keepdims=True) for p in range(PIVOTS)]
            for p in range(PIVOTS):
                col = cols[p]
                inv = 1.0 / col[p:p + 1, :]
                row = after[p:p + 1, :] * inv
                for q in range(p + 1, PIVOTS):
                    f = cols[q][p:p + 1, :] * inv
                    cols[q] = jnp.where(side == p, f, cols[q] - col * f)
                after = jnp.where(lane == k + p, col * inv, after - col * row)
                after = jnp.where(sub == p, jnp.where(lane == k + p, -inv, row), after)
            h, m, l = split3(before)
            a, b, c = split3(after)
            change = lax.dot_general(
                jnp.concatenate([h, h, m, h, m, l], 0), jnp.concatenate([a, b, a, c, b, a], 0),
                (((0,), (0,)), ((), ())), preferred_element_type=F32)
            ref[...] = jnp.where((wide >= k) & (wide < k + PIVOTS), 0.0, ref[...]) - change
            ref[rws, :] = after
            return carry
        with jax.named_scope("sweep"):
            lax.fori_loop(0, steps, body, 0)

    def errors(src, dst, part, m_part, n_rows, c_ref, cols, n_cols):
        c = jnp.concatenate([c_ref[:rank, cols], c_ref[rank:, cols]], 1)
        fit = dot(mcat[m_part, :], jnp.concatenate([c, c], 0))
        err = src[part, cols] - (fit[:, :n_cols] + fit[:, n_cols:])
        dst[part, cols] = err
        sq[:, :n_cols] += jnp.sum((err * err).reshape(n_rows // 8, 8, n_cols), axis=0)

    def error_rows(part):
        hi, lo = mcat[part, :rank], mcat[part, rank:]
        both = jnp.concatenate([jnp.concatenate([hi, hi], 1), jnp.concatenate([lo, lo], 1)], 0)
        for j in range(loads):
            cols = pl.ds(j * STEP, STEP)
            fit = dot(both, ccat[:, cols])
            err = s[part, cols] - (fit[:rw] + fit[rw:])
            e[part, cols] = err
            sq[...] += jnp.sum((err * err).reshape(rw // 8, 8, STEP), axis=0)

    def send_limit(use):
        acc = sq[:, :128]
        for k in range(1, STEP // 128):
            acc = acc + sq[:, k * 128:(k + 1) * 128]
        lslots[use, pl.ds(me, 1), :] = jnp.sum(acc, axis=0, keepdims=True)
        start([lcopy(use, i) for i in range(n_dev - 1)])
        sq[...] = jnp.zeros_like(sq)

    def get_limit(use):
        with jax.named_scope("limit"):
            lwait(use).wait_recv()
        total = jnp.sum(jnp.sum(lslots[use], axis=0, keepdims=True), axis=1, keepdims=True)
        lwait(use).wait_send()
        return HUBER * jnp.sqrt(total / count + 1e-06)

    eye = (lax.broadcasted_iota(jnp.int32, (rank, rank), 0)
           == lax.broadcasted_iota(jnp.int32, (rank, rank), 1)).astype(F32) * RIDGE

    hrs = [hcopy(0, j, hpart.at[h_rows(lax.rem(gme + j, group))], hslots.at[j - 1]) for j in range(1, group)]
    hag = [hcopy(1, j, hred, hfull.at[h_rows(gme)]) for j in range(1, group)]

    def gram_part():
        prepare_mt()
        gslots[px] = quads(dot(mtcat[...], mcat[...]))
        start([gcopy(d) for d in range(1, n_x)])

    sq[...] = jnp.zeros_like(sq)
    load_m.wait()
    prepare_rows(own_points, m_out[...])
    load_c.wait()
    prepare_cols(ccat, pl.ds(0, half), c_now[...])
    with jax.named_scope("err0"):
        def first_own(j, carry):
            load_own(j).wait()
            errors(s, e, own_points, own_points, rows, ccat, step_cols(j), STEP)
            return carry
        lax.fori_loop(0, loads, first_own, 0)
        load_c_far.wait()
        prepare_cols(ccat_far, pl.ds(0, half), c_far[...])

        def first_far(j, carry):
            load_far(j).wait()
            errors(s_far, e_far, pl.ds(0, rows), own_points, rows, ccat_far, step_cols(j), STEP)
            return carry
        lax.fori_loop(0, loads, first_far, 0)
    with jax.named_scope("barrier"):
        pl.semaphore_wait(barrier, n_dev - 1)
    send_limit(0)
    swap = [ccopy(2, 0, m_out, m_far), ccopy(2, 1, e_far, e.at[own_points]), ccopy(2, 2, s_far, s.at[own_points])]
    start(swap)
    with jax.named_scope("mswap"):
        swap[0].wait_recv()
    prepare_rows(far_points, m_far[...])
    gram_part()

    amplitudes = ccopy(5, 0, c_out.at[:, side(core)], c_out.at[:, side(core)])

    def outer(o, carry):
        more = o < OUTER - 1

        for inner in range(INNER):
            limit = get_limit(inner)

            if inner == 0:
                @pl.when(o == 0)
                def _():
                    with jax.named_scope("eswap"):
                        swap[1].wait_recv()

            def products(k, carry):
                cols = pl.ds(pl.multiple_of(k * CHUNK, CHUNK), CHUNK)
                hi, lo = split(jnp.clip(e[:, cols], -limit, limit))
                xslots[inner, px, k] = quads(dot(mtcat[...], jnp.concatenate([hi, lo], 1)))
                for d in range(1, n_x):
                    xcopy(inner, k, d).start()
                return carry
            with jax.named_scope("products"):
                lax.fori_loop(0, chunks, products, 0)
            if inner == 0:
                with jax.named_scope("gwait"):
                    for d in range(1, n_x):
                        gcopy(d).wait_recv()
                total = gslots[0]
                for x in range(1, n_x):
                    total = total + gslots[x]
                gfull[...] = total + eye
                sent(gslots.at[pl.ds(0, n_x - 1)], g_send, g_recv.at[0])
                sweep(gfull, 0, rank // PIVOTS)

                @pl.when(o == 0)
                def _():
                    with jax.named_scope("sswap"):
                        swap[2].wait_recv()
                    sent(m_out, c_send.at[2], c_recv.at[2, 0])
                    sent(e_far, c_send.at[3], c_recv.at[2, 1])
                    sent(s_far, c_send.at[4], c_recv.at[2, 2])
            wide = CHUNK

            def update(j, carry):
                def own_cols(i, carry):
                    k = j * (wide // CHUNK) + i
                    with jax.named_scope("xw"):
                        for d in range(1, n_x):
                            xcopy(inner, k, d).wait_recv()
                    share = xslots[inner, 0, k]
                    for x in range(1, n_x):
                        share = share + xslots[inner, x, k]
                    step = jnp.dot(gfull[...], share, preferred_element_type=F32, precision=lax.Precision.HIGHEST)
                    cols = pl.ds(pl.multiple_of(k * CHUNK, CHUNK), CHUNK)
                    value = c_now[:, cols] - step
                    c_now[:, cols] = value
                    prepare_cols(ccat, cols, value)
                    return carry
                lax.fori_loop(0, wide // CHUNK, own_cols, 0)
                errors(s, e, whole, whole, 2 * rows, ccat, pl.ds(pl.multiple_of(j * wide, wide), wide), wide)
                return carry
            with jax.named_scope("update"):
                lax.fori_loop(0, half // wide, update, 0)
            send_limit(inner + 1)

            sent(xslots.at[0, pl.ds(0, n_x - 1)], x_send, x_recv.at[0, 0])

        with jax.named_scope("hpart"):
            hi, lo = split(c_now[...].T)
            ctcat[:, :rank] = hi
            ctcat[:, rank:] = lo
            hpart[...] = quads(dot(ccat[...], ctcat[...]))
            start(hrs)

        @pl.when(jnp.logical_not(more))
        def _():
            c_out[:, side(core)] = c_now[...] * jnp.sqrt(jnp.float32(rows * n_pts))
            amplitudes.start()
        limit = get_limit(INNER)

        def moment(block):
            parts = []
            for q in (1 - core, core):
                part = pl.ds(pl.multiple_of(q * rows + block, rw), rw)
                parts += split(jnp.clip(e[part, :], -limit, limit))
            both = dot(jnp.concatenate(parts, 0), ctcat[...])
            return quads(both[:2 * rw]), quads(both[2 * rw:])

        def over_y(d, h):
            return ycopy(0, d, h, half_of(ypart.at[d], h), half_of(yslots.at[d], h))

        def over_z(d, h):
            return zcopy(0, d, h, half_of(zpart.at[d], h), half_of(zslots.at[d - 1], h))

        def across(t):
            return ccopy(0, t, opart.at[t], oslots.at[t])

        def moments(t, carry):
            @pl.when(t < 2 * n_z)
            def _():
                theirs = t < n_z
                block = row_block(z_peer(far(t % n_z)), jnp.where(theirs, 1 - sy, sy))
                opart[t], value = moment(block)
                across(t).start()

                @pl.when(theirs)
                def _():
                    ypart[far(t % n_z)] = value

                @pl.when(jnp.logical_not(theirs))
                def _():
                    zpart[far(t % n_z)] = value

            @pl.when(t == 1)
            def _():
                finish(hslots, h_send.at[0], h_recv.at[0])
                own = hpart[h_rows(gme), :]
                for j in range(1, group):
                    own = own + hslots[j - 1]
                hred[...] = own
                hfull[h_rows(gme), :] = own
                start(hag)

            @pl.when(t >= LAG)
            def _():
                u = t - LAG
                d = far(u % n_z)
                across(u).wait_recv()

                @pl.when(u < n_z)
                def _():
                    ypart[d] = ypart[d] + oslots[u]
                    over_y(d, 0).start()

                @pl.when(u >= n_z)
                def _():
                    zpart[d] = zpart[d] + oslots[u]

                @pl.when(u == n_z - 1)
                def _():
                    start([over_y(far(v), 1) for v in range(n_z)])
            return carry
        with jax.named_scope("moments"):
            lax.fori_loop(0, 2 * n_z + LAG, moments, 0)

        def forward(t, carry):
            d, h = far(t % n_z), t // n_z
            part = pl.ds(pl.multiple_of(h * rh, rh), rh)
            with jax.named_scope("ywait"):
                over_y(d, h).wait_recv()
            zpart[d, part, :] = zpart[d, part, :] + yslots[d, part, :]

            @pl.when(d > 0)
            def _():
                over_z(d, h).start()
            return carry
        lax.fori_loop(0, n_z, forward, 0)
        with jax.named_scope("hag"):
            finish(hfull.at[pl.ds(0, rank - hw)], h_send.at[1], h_recv.at[1])
        hfull[...] = hfull[...] + eye
        steps = rank // PIVOTS
        per = steps // n_z

        def sweep_forward(t, carry):
            sweep(hfull, t * per, per)
            return forward(n_z + t, carry)
        lax.fori_loop(0, n_z, sweep_forward, 0)
        sweep(hfull, per * n_z, steps - per * n_z)

        def modes_half(z, which, h):
            return m_out.at[pl.ds(pl.multiple_of((z * 2 + which) * rw + h * rh, rh), rh)]

        def gather(d, h):
            ref = modes_half(sz, sy, h)
            return zcopy(1, d, h, ref, ref)

        def pass_on(d, h):
            ref = modes_half(z_from(d), sy, h)
            return ycopy(1, d, h, ref, ref)

        def solve(h, carry):
            with jax.named_scope("zwait"):
                for d in range(1, n_z):
                    over_z(d, h).wait_recv()
            part = pl.ds(pl.multiple_of(h * rh, rh), rh)
            share = zpart[0, part, :]
            for d in range(1, n_z):
                share = share + zslots[d - 1, part, :]
            step = jnp.dot(share, hfull[...], preferred_element_type=F32, precision=lax.Precision.HIGHEST)
            mine = pl.ds(pl.multiple_of(sme * rw + h * rh, rh), rh)
            m_out[mine, :] = m_out[mine, :] - step
            start([gather(far(t), h) for t in range(n_z - 1)])
            pass_on(0, h).start()
            return carry
        lax.fori_loop(0, 2, solve, 0)

        def near(u):
            return jnp.where(u == 0, 1, n_z - u)

        def block_of(i):
            u = i % n_z
            d = jnp.where(u == 0, 0, near(u - 1))
            return d, row_block(z_from(d), jnp.where(i < n_z, sy, 1 - sy))

        def hand_over(i):
            part = pl.ds(pl.multiple_of(block_of(i)[1], rw), rw)
            return ccopy(1, i, m_out.at[part], m_far.at[part])

        def take(ref, which, i):
            block = block_of(i)[1]
            part = pl.ds(pl.multiple_of(which * rows + block, rw), rw)
            prepare_rows(part, ref[pl.ds(pl.multiple_of(block, rw), rw), :])
            error_rows(part)

        def take_own(i):
            @pl.when(more)
            def _():
                hand_over(i).start()
                take(m_out, core, i)

        def take_far(i):
            @pl.when(more)
            def _():
                with jax.named_scope("farwait"):
                    hand_over(i).wait_recv()
                take(m_far, 1 - core, i)
        take_own(0)

        def first_half(u, carry):
            with jax.named_scope("gatherz"):
                gather(near(u), 0).wait_recv()
            pass_on(near(u), 0).start()
            return carry
        lax.fori_loop(0, n_z - 1, first_half, 0)

        def second_half(u, carry):
            with jax.named_scope("gatherz"):
                gather(near(u), 1).wait_recv()
            pass_on(near(u), 1).start()
            take_own(1 + u)
            take_far(u)
            return carry
        lax.fori_loop(0, n_z - 1, second_half, 0)

        def other(u, carry):
            d = block_of(u)[0]
            with jax.named_scope("gathery"):
                pass_on(d, 0).wait_recv()
                pass_on(d, 1).wait_recv()
            take_own(n_z + u)
            take_far(n_z + u - 1)
            return carry
        with jax.named_scope("other"):
            lax.fori_loop(0, n_z, other, 0)

        take_far(2 * n_z - 1)

        @pl.when(more)
        def _():
            send_limit(0)
            gram_part()
            sent(m_out, c_send.at[1], c_recv.at[1, 0])
        with jax.named_scope("sends"):
            sent(opart, c_send.at[0], c_recv.at[0, 0])
            sent(ypart, y_send.at[0], y_recv.at[0, 0, 0])
            sent(m_out.at[pl.ds(0, n_z * rw)], y_send.at[1], y_recv.at[1, 0, 0])
            sent(zslots, z_send.at[0], z_recv.at[0, 0, 0])
            sent(m_out.at[pl.ds(0, (n_z - 1) * rw)], z_send.at[1], z_recv.at[1, 0, 0])
        return carry
    lax.fori_loop(0, OUTER, outer, 0)
    amplitudes.wait_recv()
    amplitudes.wait_send()


def write_out(modes, amplitudes, m_hbm, a_hbm, sem):
    copies = [pltpu.make_async_copy(modes, m_hbm, sem.at[0]), pltpu.make_async_copy(amplitudes, a_hbm, sem.at[1])]
    for copy in copies:
        copy.start()
    for copy in copies:
        copy.wait()


def shards(n_pts, n_snap, snapshots, modes_init, coefs_init):
    rows, width = snapshots.shape
    rank = modes_init.shape[1]
    rw, half, group = rows // n_snap, width // 2, 2 * n_snap
    chunks, n_x, n_z, n_dev = half // CHUNK, n_pts // 2, n_snap // 2, n_pts * n_snap
    hw = rank // group
    vmem, dma = pltpu.VMEM, pltpu.SemaphoreType.DMA
    scratch = [
        vmem((2 * rows, half), F32), vmem((2 * rows, half), F32), vmem((rows, half), F32), vmem((rows, half), F32),
        vmem((rows, rank), F32), vmem((rank, half), F32), vmem((rank, half), F32),
        vmem((2 * rows, 2 * rank), BF16), vmem((2 * rank, 2 * rows), BF16),
        vmem((2 * rank, half), BF16), vmem((2 * rank, half), BF16), vmem((half, 2 * rank), BF16),
        vmem((8, STEP), F32),
        vmem((n_x, rank, rank), F32), vmem((rank, rank), F32),
        vmem((rank, rank), F32), vmem((group - 1, hw, rank), F32), vmem((hw, rank), F32), vmem((rank, rank), F32),
        vmem((INNER + 1, n_dev, 128), F32),
        vmem((INNER, n_x, chunks, rank, CHUNK), F32),
        vmem((n_snap, rw, rank), F32), vmem((n_snap, rw, rank), F32),
        vmem((n_z, rw, rank), F32), vmem((n_z, rw, rank), F32),
        vmem((n_z, rw, rank), F32), vmem((n_z - 1, rw, rank), F32),
        dma((3 + width // STEP,)),
        dma, dma((n_x - 1,)),
        dma((2,)), dma((2,)),
        dma((6,)), dma((4, n_snap)),
        dma, dma((chunks, n_x - 1)),
        dma((INNER + 1,)), dma((INNER + 1,)),
        dma((2,)), dma((2, n_z, 2)),
        dma((2,)), dma((2, n_z - 1, 2)),
    ]
    modes, coefs = pl.pallas_call(
        functools.partial(kernel, n_pts, n_snap),
        out_shape=(vmem((rows, rank), F32), vmem((rank, width), F32)),
        in_specs=[pl.BlockSpec(memory_space=pltpu.HBM)] * 3,
        out_specs=(pl.BlockSpec(memory_space=vmem), pl.BlockSpec(memory_space=vmem)),
        scratch_shapes=scratch,
        compiler_params=pltpu.CompilerParams(collective_id=0, has_side_effects=True, vmem_limit_bytes=67043328 - 5 * 256 * 1024),
    )(snapshots, modes_init, coefs_init)
    return pl.pallas_call(
        write_out,
        out_shape=(jax.ShapeDtypeStruct((rows, rank), F32), jax.ShapeDtypeStruct((rank, width), F32)),
        in_specs=[pl.BlockSpec(memory_space=pl.ANY)] * 2,
        out_specs=(pl.BlockSpec(memory_space=pltpu.HBM), pl.BlockSpec(memory_space=pltpu.HBM)),
        scratch_shapes=[dma((2,))],
    )(pltpu.with_memory_space_constraint(modes, vmem), pltpu.with_memory_space_constraint(coefs, vmem))


def solution(mesh):
    in_specs = (P("pts", "snap"), P("pts", None), P(None, "snap"))
    out_specs = (P("pts", None), P(None, "snap"))
    body = functools.partial(shards, mesh.shape["pts"], mesh.shape["snap"])
    return jax.shard_map(body, mesh=mesh, in_specs=in_specs, out_specs=out_specs, check_vma=False)
```

```python
import functools

import jax
import jax.numpy as jnp
from jax import lax
from jax.experimental import pallas as pl
from jax.experimental.pallas import tpu as pltpu
from jax.sharding import PartitionSpec as P

OUTER = 2
INNER = 2
PIVOTS = 16
CHUNK = 128
STEP = 256
LAG = 3

HUBER = 1.345
RIDGE = 0.01

F32 = jnp.float32
BF16 = jnp.bfloat16
MESH = pl.DeviceIdType.MESH


def split(x):
    hi = x.astype(BF16)
    lo = (x - hi.astype(F32)).astype(BF16)
    return hi, lo


def split3(x):
    hi = x.astype(BF16)
    rest = x - hi.astype(F32)
    mid = rest.astype(BF16)
    lo = (rest - mid.astype(F32)).astype(BF16)
    return hi, mid, lo


def dot(a, b):
    return jnp.dot(a, b, preferred_element_type=F32)


def quads(x):
    r, c = x.shape[0] // 2, x.shape[1] // 2
    return (x[:r, :c] + x[:r, c:]) + (x[r:, :c] + x[r:, c:])


def kernel(n_pts, n_snap, s_hbm, m_hbm, c_hbm, m_out, c_out,
           s, e, s_far, e_far, m_far, c_now, c_far, mcat, mtcat, ccat, ccat_far, ctcat, sq,
           gslots, gfull, hpart, hslots, hred, hfull,
           lslots, xslots, opart, oslots, ypart, yslots, zpart, zslots,
           load_sem, g_send, g_recv, h_send, h_recv, c_send, c_recv, once, x_send, x_recv,
           l_send, l_recv, y_send, y_recv, z_send, z_recv):
    rows, rank = m_out.shape
    width = c_out.shape[1]
    pme = lax.axis_index("pts")
    sme = lax.axis_index("snap")
    n_dev = n_pts * n_snap
    me = pme * n_snap + sme
    rw = rows // n_snap
    rh = rw // 2
    half = width // 2
    chunks = half // CHUNK
    n_x, n_z = n_pts // 2, n_snap // 2
    px, core = pme // 2, lax.rem(pme, 2)
    sz, sy = sme // 2, lax.rem(sme, 2)
    group = 2 * n_snap
    gme = core * n_snap + sme
    hw = rank // group
    count = float(rows * n_pts * width * n_snap)
    loads = half // STEP
    whole = pl.ds(0, 2 * rows)
    own_points = pl.ds(pl.multiple_of(core * rows, rows), rows)
    far_points = pl.ds(pl.multiple_of((1 - core) * rows, rows), rows)

    def offset(d):
        dx, dc, dz, dy = d
        return {"pts": lax.rem(px + dx, n_x) * 2 + lax.rem(core + dc, 2),
                "snap": lax.rem(sz + dz, n_z) * 2 + lax.rem(sy + dy, 2)}

    def hops(d):
        dx, dc, dz, dy = d
        return min(dx, n_x - dx) + dy + min(dz, n_z - dz) + 0.1 * dc
    others = [(dx, dc, dz, dy) for dx in range(n_x) for dc in range(2) for dz in range(n_z) for dy in range(2)][1:]
    others.sort(key=lambda d: -hops(d))

    barrier = pltpu.get_barrier_semaphore()
    for d in others:
        pl.semaphore_signal(barrier, inc=1, device_id=offset(d), device_id_type=MESH)

    def step_cols(j):
        return pl.ds(pl.multiple_of(j * STEP, STEP), STEP)

    def snap_cols(which, j):
        return pl.ds(pl.multiple_of(which * half + j * STEP, STEP), STEP)

    def load_own(j):
        return pltpu.make_async_copy(
            s_hbm.at[:, snap_cols(core, j)], s.at[own_points, step_cols(j)], load_sem.at[3 + j])

    def load_far(j):
        return pltpu.make_async_copy(
            s_hbm.at[:, snap_cols(1 - core, j)], s_far.at[:, step_cols(j)], load_sem.at[3 + loads + j])

    def side(which):
        return pl.ds(pl.multiple_of(which * half, half), half)
    load_m = pltpu.make_async_copy(m_hbm, m_out, load_sem.at[0])
    load_c = pltpu.make_async_copy(c_hbm.at[:, side(core)], c_now, load_sem.at[1])
    load_c_far = pltpu.make_async_copy(c_hbm.at[:, side(1 - core)], c_far, load_sem.at[2])
    start_all = [load_m, load_c] + [load_own(j) for j in range(loads)] + [load_c_far] + [load_far(j) for j in range(loads)]
    for copy in start_all:
        copy.start()

    def gcopy(d):
        ref = gslots.at[px]
        return pltpu.make_async_remote_copy(
            src_ref=ref, dst_ref=ref, send_sem=g_send, recv_sem=g_recv.at[d - 1],
            device_id={"pts": lax.rem(px + d, n_x) * 2 + core}, device_id_type=MESH)

    def hcopy(site, j, src, dst):
        peer = lax.rem(gme + j, group)
        return pltpu.make_async_remote_copy(
            src_ref=src, dst_ref=dst, send_sem=h_send.at[site], recv_sem=h_recv.at[site],
            device_id={"pts": px * 2 + peer // n_snap, "snap": lax.rem(peer, n_snap)}, device_id_type=MESH)

    def h_rows(g):
        return pl.ds(pl.multiple_of(g * hw, hw), hw)

    def ccopy(site, k, src, dst):
        return pltpu.make_async_remote_copy(
            src_ref=src, dst_ref=dst, send_sem=c_send.at[site + k if site == 2 else site],
            recv_sem=c_recv.at[site, k] if site < 2 else once.at[k + site - 2],
            device_id={"pts": px * 2 + 1 - core}, device_id_type=MESH)

    def xcopy(site, k, d):
        ref = xslots.at[site, px, k]
        return pltpu.make_async_remote_copy(
            src_ref=ref, dst_ref=ref, send_sem=x_send, recv_sem=x_recv.at[k, d - 1],
            device_id={"pts": lax.rem(px + d, n_x) * 2 + core}, device_id_type=MESH)

    def lcopy(use, i):
        ref = lslots.at[use, pl.ds(me, 1)]
        return pltpu.make_async_remote_copy(
            src_ref=ref, dst_ref=ref, send_sem=l_send.at[use], recv_sem=l_recv.at[use],
            device_id=offset(others[i]), device_id_type=MESH)

    def lwait(use):
        ref = lslots.at[use, pl.ds(0, n_dev - 1)]
        return pltpu.make_async_remote_copy(
            src_ref=ref, dst_ref=ref, send_sem=l_send.at[use], recv_sem=l_recv.at[use],
            device_id=offset(others[0]), device_id_type=MESH)

    def half_of(ref, h):
        return ref.at[pl.ds(pl.multiple_of(h * rh, rh), rh)]

    def ycopy(site, d, h, src, dst):
        return pltpu.make_async_remote_copy(
            src_ref=src, dst_ref=dst, send_sem=y_send.at[site], recv_sem=y_recv.at[site, d, h],
            device_id={"snap": sz * 2 + 1 - sy}, device_id_type=MESH)

    def zcopy(site, d, h, src, dst):
        return pltpu.make_async_remote_copy(
            src_ref=src, dst_ref=dst, send_sem=z_send.at[site], recv_sem=z_recv.at[site, d - 1, h],
            device_id={"snap": z_peer(d) * 2 + sy}, device_id_type=MESH)

    def z_peer(d):
        return (sz // 2 + d // 2) % (n_z // 2) * 2 + (sz + d) % 2

    def z_from(d):
        return (sz // 2 + n_z // 2 - d // 2) % (n_z // 2) * 2 + (sz + d) % 2

    def row_block(z, which):
        return (z * 2 + which) * rw

    def far(t):
        return n_z - 1 - t

    def start(copies):
        for copy in copies:
            copy.start()

    def all_of(ref, send_sem, recv_sem):
        return pltpu.make_async_remote_copy(
            src_ref=ref, dst_ref=ref, send_sem=send_sem, recv_sem=recv_sem,
            device_id={"pts": px * 2 + 1 - core}, device_id_type=MESH)

    def finish(ref, send_sem, recv_sem):
        all_of(ref, send_sem, recv_sem).wait_recv()
        all_of(ref, send_sem, recv_sem).wait_send()

    def sent(ref, send_sem, recv_sem):
        all_of(ref, send_sem, recv_sem).wait_send()

    def prepare_rows(part, value):
        hi, lo = split(value)
        mcat[part, :rank] = hi
        mcat[part, rank:] = lo

    def prepare_mt():
        for ref, part in ((m_out, own_points), (m_far, far_points)):
            hi, lo = split(ref[...].T)
            mtcat[:rank, part] = hi
            mtcat[rank:, part] = lo

    def prepare_cols(ref, cols, value):
        hi, lo = split(value)
        ref[:rank, cols] = hi
        ref[rank:, cols] = lo

    def sweep(ref, base, steps):
        sub = lax.broadcasted_iota(jnp.int32, (PIVOTS, rank), 0)
        lane = lax.broadcasted_iota(jnp.int32, (PIVOTS, rank), 1)
        wide = lax.broadcasted_iota(jnp.int32, (rank, rank), 1)
        side = sub[:, :1]

        def body(t, carry):
            k = (base + t) * PIVOTS
            rws = pl.ds(pl.multiple_of(k, PIVOTS), PIVOTS)
            before = ref[rws, :]
            after = before
            cols = [jnp.sum(jnp.where(lane == k + p, before, 0.0), axis=1, keepdims=True) for p in range(PIVOTS)]
            for p in range(PIVOTS):
                col = cols[p]
                inv = 1.0 / col[p:p + 1, :]
                row = after[p:p + 1, :] * inv
                for q in range(p + 1, PIVOTS):
                    f = cols[q][p:p + 1, :] * inv
                    cols[q] = jnp.where(side == p, f, cols[q] - col * f)
                after = jnp.where(lane == k + p, col * inv, after - col * row)
                after = jnp.where(sub == p, jnp.where(lane == k + p, -inv, row), after)
            h, m, l = split3(before)
            a, b, c = split3(after)
            change = lax.dot_general(
                jnp.concatenate([h, h, m, h, m, l], 0), jnp.concatenate([a, b, a, c, b, a], 0),
                (((0,), (0,)), ((), ())), preferred_element_type=F32)
            ref[...] = jnp.where((wide >= k) & (wide < k + PIVOTS), 0.0, ref[...]) - change
            ref[rws, :] = after
            return carry
        with jax.named_scope("sweep"):
            lax.fori_loop(0, steps, body, 0)

    def errors(src, dst, part, m_part, n_rows, c_ref, cols, n_cols):
        c = jnp.concatenate([c_ref[:rank, cols], c_ref[rank:, cols]], 1)
        fit = dot(mcat[m_part, :], jnp.concatenate([c, c], 0))
        err = src[part, cols] - (fit[:, :n_cols] + fit[:, n_cols:])
        dst[part, cols] = err
        sq[:, :n_cols] += jnp.sum((err * err).reshape(n_rows // 8, 8, n_cols), axis=0)

    def error_rows(part):
        hi, lo = mcat[part, :rank], mcat[part, rank:]
        both = jnp.concatenate([jnp.concatenate([hi, hi], 1), jnp.concatenate([lo, lo], 1)], 0)
        for j in range(loads):
            cols = pl.ds(j * STEP, STEP)
            fit = dot(both, ccat[:, cols])
            err = s[part, cols] - (fit[:rw] + fit[rw:])
            e[part, cols] = err
            sq[...] += jnp.sum((err * err).reshape(rw // 8, 8, STEP), axis=0)

    def send_limit(use):
        acc = sq[:, :128]
        for k in range(1, STEP // 128):
            acc = acc + sq[:, k * 128:(k + 1) * 128]
        lslots[use, pl.ds(me, 1), :] = jnp.sum(acc, axis=0, keepdims=True)
        start([lcopy(use, i) for i in range(n_dev - 1)])
        sq[...] = jnp.zeros_like(sq)

    def get_limit(use):
        with jax.named_scope("limit"):
            lwait(use).wait_recv()
        total = jnp.sum(jnp.sum(lslots[use], axis=0, keepdims=True), axis=1, keepdims=True)
        lwait(use).wait_send()
        return HUBER * jnp.sqrt(total / count + 1e-06)

    eye = (lax.broadcasted_iota(jnp.int32, (rank, rank), 0)
           == lax.broadcasted_iota(jnp.int32, (rank, rank), 1)).astype(F32) * RIDGE

    hrs = [hcopy(0, j, hpart.at[h_rows(lax.rem(gme + j, group))], hslots.at[j - 1]) for j in range(1, group)]
    hag = [hcopy(1, j, hred, hfull.at[h_rows(gme)]) for j in range(1, group)]

    def gram_part():
        prepare_mt()
        gslots[px] = quads(dot(mtcat[...], mcat[...]))
        start([gcopy(d) for d in range(1, n_x)])

    sq[...] = jnp.zeros_like(sq)
    load_m.wait()
    prepare_rows(own_points, m_out[...])
    load_c.wait()
    prepare_cols(ccat, pl.ds(0, half), c_now[...])
    with jax.named_scope("err0"):
        def first_own(j, carry):
            load_own(j).wait()
            errors(s, e, own_points, own_points, rows, ccat, step_cols(j), STEP)
            return carry
        lax.fori_loop(0, loads, first_own, 0)
        load_c_far.wait()
        prepare_cols(ccat_far, pl.ds(0, half), c_far[...])

        def first_far(j, carry):
            load_far(j).wait()
            errors(s_far, e_far, pl.ds(0, rows), own_points, rows, ccat_far, step_cols(j), STEP)
            return carry
        lax.fori_loop(0, loads, first_far, 0)
    with jax.named_scope("barrier"):
        pl.semaphore_wait(barrier, n_dev - 1)
    send_limit(0)
    swap = [ccopy(2, 0, m_out, m_far), ccopy(2, 1, e_far, e.at[own_points]), ccopy(2, 2, s_far, s.at[own_points])]
    start(swap)
    with jax.named_scope("mswap"):
        swap[0].wait_recv()
    prepare_rows(far_points, m_far[...])
    gram_part()

    amplitudes = ccopy(5, 0, c_out.at[:, side(core)], c_out.at[:, side(core)])

    def outer(o, carry):
        more = o < OUTER - 1

        for inner in range(INNER):
            limit = get_limit(inner)

            if inner == 0:
                @pl.when(o == 0)
                def _():
                    with jax.named_scope("eswap"):
                        swap[1].wait_recv()

            def products(k, carry):
                cols = pl.ds(pl.multiple_of(k * CHUNK, CHUNK), CHUNK)
                hi, lo = split(jnp.clip(e[:, cols], -limit, limit))
                xslots[inner, px, k] = quads(dot(mtcat[...], jnp.concatenate([hi, lo], 1)))
                for d in range(1, n_x):
                    xcopy(inner, k, d).start()
                return carry
            with jax.named_scope("products"):
                lax.fori_loop(0, chunks, products, 0)
            if inner == 0:
                with jax.named_scope("gwait"):
                    for d in range(1, n_x):
                        gcopy(d).wait_recv()
                total = gslots[0]
                for x in range(1, n_x):
                    total = total + gslots[x]
                gfull[...] = total + eye
                sent(gslots.at[pl.ds(0, n_x - 1)], g_send, g_recv.at[0])
                sweep(gfull, 0, rank // PIVOTS)

                @pl.when(o == 0)
                def _():
                    with jax.named_scope("sswap"):
                        swap[2].wait_recv()
                    sent(m_out, c_send.at[2], once.at[0])
                    sent(e_far, c_send.at[3], once.at[1])
                    sent(s_far, c_send.at[4], once.at[2])
            wide = CHUNK

            def update(j, carry):
                def own_cols(i, carry):
                    k = j * (wide // CHUNK) + i
                    with jax.named_scope("xw"):
                        for d in range(1, n_x):
                            xcopy(inner, k, d).wait_recv()
                    share = xslots[inner, 0, k]
                    for x in range(1, n_x):
                        share = share + xslots[inner, x, k]
                    step = jnp.dot(gfull[...], share, preferred_element_type=F32, precision=lax.Precision.HIGHEST)
                    cols = pl.ds(pl.multiple_of(k * CHUNK, CHUNK), CHUNK)
                    value = c_now[:, cols] - step
                    c_now[:, cols] = value
                    prepare_cols(ccat, cols, value)
                    return carry
                lax.fori_loop(0, wide // CHUNK, own_cols, 0)
                errors(s, e, whole, whole, 2 * rows, ccat, pl.ds(pl.multiple_of(j * wide, wide), wide), wide)
                return carry
            with jax.named_scope("update"):
                lax.fori_loop(0, half // wide, update, 0)
            send_limit(inner + 1)

            sent(xslots.at[0, pl.ds(0, n_x - 1)], x_send, x_recv.at[0, 0])

        with jax.named_scope("hpart"):
            hi, lo = split(c_now[...].T)
            ctcat[:, :rank] = hi
            ctcat[:, rank:] = lo
            hpart[...] = quads(dot(ccat[...], ctcat[...]))
            start(hrs)

        @pl.when(jnp.logical_not(more))
        def _():
            c_out[:, side(core)] = c_now[...] * jnp.sqrt(jnp.float32(rows * n_pts))
            amplitudes.start()
        limit = get_limit(INNER)

        def moment(block):
            parts = []
            for q in (1 - core, core):
                part = pl.ds(pl.multiple_of(q * rows + block, rw), rw)
                parts += split(jnp.clip(e[part, :], -limit, limit))
            both = dot(jnp.concatenate(parts, 0), ctcat[...])
            return quads(both[:2 * rw]), quads(both[2 * rw:])

        def over_y(d, h):
            return ycopy(0, d, h, half_of(ypart.at[d], h), half_of(yslots.at[d], h))

        def over_z(d, h):
            return zcopy(0, d, h, half_of(zpart.at[d], h), half_of(zslots.at[d - 1], h))

        def across(t):
            return ccopy(0, t, opart.at[t], oslots.at[t])

        def moments(t, carry):
            @pl.when(t < 2 * n_z)
            def _():
                theirs = t < n_z
                block = row_block(z_peer(far(t % n_z)), jnp.where(theirs, 1 - sy, sy))
                opart[t], value = moment(block)
                across(t).start()

                @pl.when(theirs)
                def _():
                    ypart[far(t % n_z)] = value

                @pl.when(jnp.logical_not(theirs))
                def _():
                    zpart[far(t % n_z)] = value

            @pl.when(t == 1)
            def _():
                finish(hslots, h_send.at[0], h_recv.at[0])
                own = hpart[h_rows(gme), :]
                for j in range(1, group):
                    own = own + hslots[j - 1]
                hred[...] = own
                hfull[h_rows(gme), :] = own
                start(hag)

            @pl.when(t >= LAG)
            def _():
                u = t - LAG
                d = far(u % n_z)
                across(u).wait_recv()

                @pl.when(u < n_z)
                def _():
                    ypart[d] = ypart[d] + oslots[u]
                    over_y(d, 0).start()

                @pl.when(u >= n_z)
                def _():
                    zpart[d] = zpart[d] + oslots[u]

                @pl.when(u == n_z - 1)
                def _():
                    start([over_y(far(v), 1) for v in range(n_z)])
            return carry
        with jax.named_scope("moments"):
            lax.fori_loop(0, 2 * n_z + LAG, moments, 0)

        def forward(t, carry):
            d, h = far(t % n_z), t // n_z
            part = pl.ds(pl.multiple_of(h * rh, rh), rh)
            with jax.named_scope("ywait"):
                over_y(d, h).wait_recv()
            zpart[d, part, :] = zpart[d, part, :] + yslots[d, part, :]

            @pl.when(d > 0)
            def _():
                over_z(d, h).start()
            return carry
        lax.fori_loop(0, n_z, forward, 0)
        with jax.named_scope("hag"):
            finish(hfull.at[pl.ds(0, rank - hw)], h_send.at[1], h_recv.at[1])
        hfull[...] = hfull[...] + eye
        steps = rank // PIVOTS
        per = steps // n_z

        def sweep_forward(t, carry):
            sweep(hfull, t * per, per)
            return forward(n_z + t, carry)
        lax.fori_loop(0, n_z, sweep_forward, 0)
        sweep(hfull, per * n_z, steps - per * n_z)

        def modes_half(z, which, h):
            return m_out.at[pl.ds(pl.multiple_of((z * 2 + which) * rw + h * rh, rh), rh)]

        def gather(d, h):
            ref = modes_half(sz, sy, h)
            return zcopy(1, d, h, ref, ref)

        def pass_on(d, h):
            ref = modes_half(z_from(d), sy, h)
            return ycopy(1, d, h, ref, ref)

        def solve(h, carry):
            with jax.named_scope("zwait"):
                for d in range(1, n_z):
                    over_z(d, h).wait_recv()
            part = pl.ds(pl.multiple_of(h * rh, rh), rh)
            share = zpart[0, part, :]
            for d in range(1, n_z):
                share = share + zslots[d - 1, part, :]
            step = jnp.dot(share, hfull[...], preferred_element_type=F32, precision=lax.Precision.HIGHEST)
            mine = pl.ds(pl.multiple_of(sme * rw + h * rh, rh), rh)
            m_out[mine, :] = m_out[mine, :] - step
            start([gather(far(t), h) for t in range(n_z - 1)])
            pass_on(0, h).start()
            return carry
        lax.fori_loop(0, 2, solve, 0)

        def near(u):
            return jnp.where(u == 0, 1, n_z - u)

        def block_of(i):
            u = i % n_z
            d = jnp.where(u == 0, 0, near(u - 1))
            return d, row_block(z_from(d), jnp.where(i < n_z, sy, 1 - sy))

        def hand_over(i):
            part = pl.ds(pl.multiple_of(block_of(i)[1], rw), rw)
            return ccopy(1, i, m_out.at[part], m_far.at[part])

        def take(ref, which, i):
            block = block_of(i)[1]
            part = pl.ds(pl.multiple_of(which * rows + block, rw), rw)
            prepare_rows(part, ref[pl.ds(pl.multiple_of(block, rw), rw), :])
            error_rows(part)

        def take_own(i):
            @pl.when(more)
            def _():
                hand_over(i).start()
                take(m_out, core, i)

        def take_far(i):
            @pl.when(more)
            def _():
                with jax.named_scope("farwait"):
                    hand_over(i).wait_recv()
                take(m_far, 1 - core, i)
        take_own(0)

        def first_half(u, carry):
            with jax.named_scope("gatherz"):
                gather(near(u), 0).wait_recv()
            pass_on(near(u), 0).start()
            return carry
        lax.fori_loop(0, n_z - 1, first_half, 0)

        def second_half(u, carry):
            with jax.named_scope("gatherz"):
                gather(near(u), 1).wait_recv()
            pass_on(near(u), 1).start()
            take_own(1 + u)
            take_far(u)
            return carry
        lax.fori_loop(0, n_z - 1, second_half, 0)

        def other(u, carry):
            d = block_of(u)[0]
            with jax.named_scope("gathery"):
                pass_on(d, 0).wait_recv()
                pass_on(d, 1).wait_recv()
            take_own(n_z + u)
            take_far(n_z + u - 1)
            return carry
        with jax.named_scope("other"):
            lax.fori_loop(0, n_z, other, 0)

        take_far(2 * n_z - 1)

        @pl.when(more)
        def _():
            send_limit(0)
            gram_part()
            sent(m_out, c_send.at[1], c_recv.at[1, 0])
        with jax.named_scope("sends"):
            sent(opart, c_send.at[0], c_recv.at[0, 0])
            sent(ypart, y_send.at[0], y_recv.at[0, 0, 0])
            sent(m_out.at[pl.ds(0, n_z * rw)], y_send.at[1], y_recv.at[1, 0, 0])
            sent(zslots, z_send.at[0], z_recv.at[0, 0, 0])
            sent(m_out.at[pl.ds(0, (n_z - 1) * rw)], z_send.at[1], z_recv.at[1, 0, 0])
        return carry
    lax.fori_loop(0, OUTER, outer, 0)
    amplitudes.wait_recv()
    amplitudes.wait_send()


def write_out(modes, amplitudes, m_hbm, a_hbm, sem):
    copies = [pltpu.make_async_copy(modes, m_hbm, sem.at[0]), pltpu.make_async_copy(amplitudes, a_hbm, sem.at[1])]
    for copy in copies:
        copy.start()
    for copy in copies:
        copy.wait()


def shards(n_pts, n_snap, snapshots, modes_init, coefs_init):
    rows, width = snapshots.shape
    rank = modes_init.shape[1]
    rw, half, group = rows // n_snap, width // 2, 2 * n_snap
    chunks, n_x, n_z, n_dev = half // CHUNK, n_pts // 2, n_snap // 2, n_pts * n_snap
    hw = rank // group
    vmem, dma = pltpu.VMEM, pltpu.SemaphoreType.DMA
    scratch = [
        vmem((2 * rows, half), F32), vmem((2 * rows, half), F32), vmem((rows, half), F32), vmem((rows, half), F32),
        vmem((rows, rank), F32), vmem((rank, half), F32), vmem((rank, half), F32),
        vmem((2 * rows, 2 * rank), BF16), vmem((2 * rank, 2 * rows), BF16),
        vmem((2 * rank, half), BF16), vmem((2 * rank, half), BF16), vmem((half, 2 * rank), BF16),
        vmem((8, STEP), F32),
        vmem((n_x, rank, rank), F32), vmem((rank, rank), F32),
        vmem((rank, rank), F32), vmem((group - 1, hw, rank), F32), vmem((hw, rank), F32), vmem((rank, rank), F32),
        vmem((INNER + 1, n_dev, 128), F32),
        vmem((INNER, n_x, chunks, rank, CHUNK), F32),
        vmem((n_snap, rw, rank), F32), vmem((n_snap, rw, rank), F32),
        vmem((n_z, rw, rank), F32), vmem((n_z, rw, rank), F32),
        vmem((n_z, rw, rank), F32), vmem((n_z - 1, rw, rank), F32),
        dma((3 + width // STEP,)),
        dma, dma((n_x - 1,)),
        dma((2,)), dma((2,)),
        dma((6,)), dma((2, n_snap)), dma((4,)),
        dma, dma((chunks, n_x - 1)),
        dma((INNER + 1,)), dma((INNER + 1,)),
        dma((2,)), dma((2, n_z, 2)),
        dma((2,)), dma((2, n_z - 1, 2)),
    ]
    modes, coefs = pl.pallas_call(
        functools.partial(kernel, n_pts, n_snap),
        out_shape=(vmem((rows, rank), F32), vmem((rank, width), F32)),
        in_specs=[pl.BlockSpec(memory_space=pltpu.HBM)] * 3,
        out_specs=(pl.BlockSpec(memory_space=vmem), pl.BlockSpec(memory_space=vmem)),
        scratch_shapes=scratch,
        compiler_params=pltpu.CompilerParams(collective_id=0, has_side_effects=True, vmem_limit_bytes=67043328 - 5 * 256 * 1024),
    )(snapshots, modes_init, coefs_init)
    return pl.pallas_call(
        write_out,
        out_shape=(jax.ShapeDtypeStruct((rows, rank), F32), jax.ShapeDtypeStruct((rank, width), F32)),
        in_specs=[pl.BlockSpec(memory_space=pl.ANY)] * 2,
        out_specs=(pl.BlockSpec(memory_space=pltpu.HBM), pl.BlockSpec(memory_space=pltpu.HBM)),
        scratch_shapes=[dma((2,))],
    )(pltpu.with_memory_space_constraint(modes, vmem), pltpu.with_memory_space_constraint(coefs, vmem))


def solution(mesh):
    in_specs = (P("pts", "snap"), P("pts", None), P(None, "snap"))
    out_specs = (P("pts", None), P(None, "snap"))
    body = functools.partial(shards, mesh.shape["pts"], mesh.shape["snap"])
    return jax.shard_map(body, mesh=mesh, in_specs=in_specs, out_specs=out_specs, check_vma=False)
```

```python
import functools

import jax
import jax.numpy as jnp
from jax import lax
from jax.experimental import pallas as pl
from jax.experimental.pallas import tpu as pltpu
from jax.sharding import PartitionSpec as P

OUTER = 2
INNER = 2
PIVOTS = 16
CHUNK = 128
STEP = 256
LAG = 3

HUBER = 1.345
RIDGE = 0.01

F32 = jnp.float32
BF16 = jnp.bfloat16
MESH = pl.DeviceIdType.MESH


def split(x):
    hi = x.astype(BF16)
    lo = (x - hi.astype(F32)).astype(BF16)
    return hi, lo


def split3(x):
    hi = x.astype(BF16)
    rest = x - hi.astype(F32)
    mid = rest.astype(BF16)
    lo = (rest - mid.astype(F32)).astype(BF16)
    return hi, mid, lo


def dot(a, b):
    return jnp.dot(a, b, preferred_element_type=F32)


def quads(x):
    r, c = x.shape[0] // 2, x.shape[1] // 2
    return (x[:r, :c] + x[:r, c:]) + (x[r:, :c] + x[r:, c:])


def kernel(n_pts, n_snap, s_hbm, m_hbm, c_hbm, m_out, c_out,
           s, e, s_far, e_far, m_far, c_now, c_far, mcat, mtcat, ccat, ccat_far, ctcat, sq,
           gslots, gfull, gcat, hpart, hslots, hred, hfull, hcat,
           lslots, xslots, opart, oslots, ypart, yslots, zpart, zslots,
           load_sem, g_send, g_recv, h_send, h_recv, c_send, c_recv, once, x_send, x_recv,
           l_send, l_recv, y_send, y_recv, z_send, z_recv):
    rows, rank = m_out.shape
    width = c_out.shape[1]
    pme = lax.axis_index("pts")
    sme = lax.axis_index("snap")
    n_dev = n_pts * n_snap
    me = pme * n_snap + sme
    rw = rows // n_snap
    rh = rw // 2
    half = width // 2
    chunks = half // CHUNK
    n_x, n_z = n_pts // 2, n_snap // 2
    px, core = pme // 2, lax.rem(pme, 2)
    sz, sy = sme // 2, lax.rem(sme, 2)
    group = 2 * n_snap
    gme = core * n_snap + sme
    hw = rank // group
    count = float(rows * n_pts * width * n_snap)
    loads = half // STEP
    whole = pl.ds(0, 2 * rows)
    own_points = pl.ds(pl.multiple_of(core * rows, rows), rows)
    far_points = pl.ds(pl.multiple_of((1 - core) * rows, rows), rows)

    def offset(d):
        dx, dc, dz, dy = d
        return {"pts": lax.rem(px + dx, n_x) * 2 + lax.rem(core + dc, 2),
                "snap": lax.rem(sz + dz, n_z) * 2 + lax.rem(sy + dy, 2)}

    def hops(d):
        dx, dc, dz, dy = d
        return min(dx, n_x - dx) + dy + min(dz, n_z - dz) + 0.1 * dc
    others = [(dx, dc, dz, dy) for dx in range(n_x) for dc in range(2) for dz in range(n_z) for dy in range(2)][1:]
    others.sort(key=lambda d: -hops(d))

    barrier = pltpu.get_barrier_semaphore()
    for d in others:
        pl.semaphore_signal(barrier, inc=1, device_id=offset(d), device_id_type=MESH)

    def step_cols(j):
        return pl.ds(pl.multiple_of(j * STEP, STEP), STEP)

    def snap_cols(which, j):
        return pl.ds(pl.multiple_of(which * half + j * STEP, STEP), STEP)

    def load_own(j):
        return pltpu.make_async_copy(
            s_hbm.at[:, snap_cols(core, j)], s.at[own_points, step_cols(j)], load_sem.at[3 + j])

    def load_far(j):
        return pltpu.make_async_copy(
            s_hbm.at[:, snap_cols(1 - core, j)], s_far.at[:, step_cols(j)], load_sem.at[3 + loads + j])

    def side(which):
        return pl.ds(pl.multiple_of(which * half, half), half)
    load_m = pltpu.make_async_copy(m_hbm, m_out, load_sem.at[0])
    load_c = pltpu.make_async_copy(c_hbm.at[:, side(core)], c_now, load_sem.at[1])
    load_c_far = pltpu.make_async_copy(c_hbm.at[:, side(1 - core)], c_far, load_sem.at[2])
    start_all = [load_m, load_c] + [load_own(j) for j in range(loads)] + [load_c_far] + [load_far(j) for j in range(loads)]
    for copy in start_all:
        copy.start()

    def gcopy(d):
        ref = gslots.at[px]
        return pltpu.make_async_remote_copy(
            src_ref=ref, dst_ref=ref, send_sem=g_send, recv_sem=g_recv.at[d - 1],
            device_id={"pts": lax.rem(px + d, n_x) * 2 + core}, device_id_type=MESH)

    def hcopy(site, j, src, dst):
        peer = lax.rem(gme + j, group)
        return pltpu.make_async_remote_copy(
            src_ref=src, dst_ref=dst, send_sem=h_send.at[site], recv_sem=h_recv.at[site],
            device_id={"pts": px * 2 + peer // n_snap, "snap": lax.rem(peer, n_snap)}, device_id_type=MESH)

    def h_rows(g):
        return pl.ds(pl.multiple_of(g * hw, hw), hw)

    def ccopy(site, k, src, dst):
        return pltpu.make_async_remote_copy(
            src_ref=src, dst_ref=dst, send_sem=c_send.at[site + k if site == 2 else site],
            recv_sem=c_recv.at[site, k] if site < 2 else once.at[k + site - 2],
            device_id={"pts": px * 2 + 1 - core}, device_id_type=MESH)

    def xcopy(site, k, d):
        ref = xslots.at[site, px, k]
        return pltpu.make_async_remote_copy(
            src_ref=ref, dst_ref=ref, send_sem=x_send, recv_sem=x_recv.at[k, d - 1],
            device_id={"pts": lax.rem(px + d, n_x) * 2 + core}, device_id_type=MESH)

    def lcopy(use, i):
        ref = lslots.at[use, pl.ds(me, 1)]
        return pltpu.make_async_remote_copy(
            src_ref=ref, dst_ref=ref, send_sem=l_send.at[use], recv_sem=l_recv.at[use],
            device_id=offset(others[i]), device_id_type=MESH)

    def lwait(use):
        ref = lslots.at[use, pl.ds(0, n_dev - 1)]
        return pltpu.make_async_remote_copy(
            src_ref=ref, dst_ref=ref, send_sem=l_send.at[use], recv_sem=l_recv.at[use],
            device_id=offset(others[0]), device_id_type=MESH)

    def half_of(ref, h):
        return ref.at[pl.ds(pl.multiple_of(h * rh, rh), rh)]

    def ycopy(site, d, h, src, dst):
        return pltpu.make_async_remote_copy(
            src_ref=src, dst_ref=dst, send_sem=y_send.at[site], recv_sem=y_recv.at[site, d, h],
            device_id={"snap": sz * 2 + 1 - sy}, device_id_type=MESH)

    def zcopy(site, d, h, src, dst):
        return pltpu.make_async_remote_copy(
            src_ref=src, dst_ref=dst, send_sem=z_send.at[site], recv_sem=z_recv.at[site, d - 1, h],
            device_id={"snap": z_peer(d) * 2 + sy}, device_id_type=MESH)

    def z_peer(d):
        return (sz // 2 + d // 2) % (n_z // 2) * 2 + (sz + d) % 2

    def z_from(d):
        return (sz // 2 + n_z // 2 - d // 2) % (n_z // 2) * 2 + (sz + d) % 2

    def row_block(z, which):
        return (z * 2 + which) * rw

    def far(t):
        return n_z - 1 - t

    def start(copies):
        for copy in copies:
            copy.start()

    def all_of(ref, send_sem, recv_sem):
        return pltpu.make_async_remote_copy(
            src_ref=ref, dst_ref=ref, send_sem=send_sem, recv_sem=recv_sem,
            device_id={"pts": px * 2 + 1 - core}, device_id_type=MESH)

    def finish(ref, send_sem, recv_sem):
        all_of(ref, send_sem, recv_sem).wait_recv()
        all_of(ref, send_sem, recv_sem).wait_send()

    def sent(ref, send_sem, recv_sem):
        all_of(ref, send_sem, recv_sem).wait_send()

    def prepare_rows(part, value):
        hi, lo = split(value)
        mcat[part, :rank] = hi
        mcat[part, rank:] = lo

    def prepare_mt():
        for ref, part in ((m_out, own_points), (m_far, far_points)):
            hi, lo = split(ref[...].T)
            mtcat[:rank, part] = hi
            mtcat[rank:, part] = lo

    def prepare_cols(ref, cols, value):
        hi, lo = split(value)
        ref[:rank, cols] = hi
        ref[rank:, cols] = lo

    def sweep(ref, base, steps):
        sub = lax.broadcasted_iota(jnp.int32, (PIVOTS, rank), 0)
        lane = lax.broadcasted_iota(jnp.int32, (PIVOTS, rank), 1)
        wide = lax.broadcasted_iota(jnp.int32, (rank, rank), 1)
        side = sub[:, :1]

        def body(t, carry):
            k = (base + t) * PIVOTS
            rws = pl.ds(pl.multiple_of(k, PIVOTS), PIVOTS)
            before = ref[rws, :]
            after = before
            cols = [jnp.sum(jnp.where(lane == k + p, before, 0.0), axis=1, keepdims=True) for p in range(PIVOTS)]
            for p in range(PIVOTS):
                col = cols[p]
                inv = 1.0 / col[p:p + 1, :]
                row = after[p:p + 1, :] * inv
                for q in range(p + 1, PIVOTS):
                    f = cols[q][p:p + 1, :] * inv
                    cols[q] = jnp.where(side == p, f, cols[q] - col * f)
                after = jnp.where(lane == k + p, col * inv, after - col * row)
                after = jnp.where(sub == p, jnp.where(lane == k + p, -inv, row), after)
            h, m, l = split3(before)
            a, b, c = split3(after)
            change = lax.dot_general(
                jnp.concatenate([h, h, m, h, m, l], 0), jnp.concatenate([a, b, a, c, b, a], 0),
                (((0,), (0,)), ((), ())), preferred_element_type=F32)
            ref[...] = jnp.where((wide >= k) & (wide < k + PIVOTS), 0.0, ref[...]) - change
            ref[rws, :] = after
            return carry
        with jax.named_scope("sweep"):
            lax.fori_loop(0, steps, body, 0)

    def errors(src, dst, part, m_part, n_rows, c_ref, cols, n_cols):
        c = jnp.concatenate([c_ref[:rank, cols], c_ref[rank:, cols]], 1)
        fit = dot(mcat[m_part, :], jnp.concatenate([c, c], 0))
        err = src[part, cols] - (fit[:, :n_cols] + fit[:, n_cols:])
        dst[part, cols] = err
        sq[:, :n_cols] += jnp.sum((err * err).reshape(n_rows // 8, 8, n_cols), axis=0)

    def error_rows(part):
        hi, lo = mcat[part, :rank], mcat[part, rank:]
        both = jnp.concatenate([jnp.concatenate([hi, hi], 1), jnp.concatenate([lo, lo], 1)], 0)
        for j in range(loads):
            cols = pl.ds(j * STEP, STEP)
            fit = dot(both, ccat[:, cols])
            err = s[part, cols] - (fit[:rw] + fit[rw:])
            e[part, cols] = err
            sq[...] += jnp.sum((err * err).reshape(rw // 8, 8, STEP), axis=0)

    def send_limit(use):
        acc = sq[:, :128]
        for k in range(1, STEP // 128):
            acc = acc + sq[:, k * 128:(k + 1) * 128]
        lslots[use, pl.ds(me, 1), :] = jnp.sum(acc, axis=0, keepdims=True)
        start([lcopy(use, i) for i in range(n_dev - 1)])
        sq[...] = jnp.zeros_like(sq)

    def get_limit(use):
        with jax.named_scope("limit"):
            lwait(use).wait_recv()
        total = jnp.sum(jnp.sum(lslots[use], axis=0, keepdims=True), axis=1, keepdims=True)
        lwait(use).wait_send()
        return HUBER * jnp.sqrt(total / count + 1e-06)

    eye = (lax.broadcasted_iota(jnp.int32, (rank, rank), 0)
           == lax.broadcasted_iota(jnp.int32, (rank, rank), 1)).astype(F32) * RIDGE

    hrs = [hcopy(0, j, hpart.at[h_rows(lax.rem(gme + j, group))], hslots.at[j - 1]) for j in range(1, group)]
    hag = [hcopy(1, j, hred, hfull.at[h_rows(gme)]) for j in range(1, group)]

    def gram_part():
        prepare_mt()
        gslots[px] = quads(dot(mtcat[...], mcat[...]))
        start([gcopy(d) for d in range(1, n_x)])

    sq[...] = jnp.zeros_like(sq)
    load_m.wait()
    prepare_rows(own_points, m_out[...])
    load_c.wait()
    prepare_cols(ccat, pl.ds(0, half), c_now[...])
    with jax.named_scope("err0"):
        def first_own(j, carry):
            load_own(j).wait()
            errors(s, e, own_points, own_points, rows, ccat, step_cols(j), STEP)
            return carry
        lax.fori_loop(0, loads, first_own, 0)
        load_c_far.wait()
        prepare_cols(ccat_far, pl.ds(0, half), c_far[...])

        def first_far(j, carry):
            load_far(j).wait()
            errors(s_far, e_far, pl.ds(0, rows), own_points, rows, ccat_far, step_cols(j), STEP)
            return carry
        lax.fori_loop(0, loads, first_far, 0)
    with jax.named_scope("barrier"):
        pl.semaphore_wait(barrier, n_dev - 1)
    send_limit(0)
    swap = [ccopy(2, 0, m_out, m_far), ccopy(2, 1, e_far, e.at[own_points]), ccopy(2, 2, s_far, s.at[own_points])]
    start(swap)
    with jax.named_scope("mswap"):
        swap[0].wait_recv()
    prepare_rows(far_points, m_far[...])
    gram_part()

    amplitudes = ccopy(5, 0, c_out.at[:, side(core)], c_out.at[:, side(core)])

    def outer(o, carry):
        more = o < OUTER - 1

        for inner in range(INNER):
            limit = get_limit(inner)

            if inner == 0:
                @pl.when(o == 0)
                def _():
                    with jax.named_scope("eswap"):
                        swap[1].wait_recv()

            def products(k, carry):
                cols = pl.ds(pl.multiple_of(k * CHUNK, CHUNK), CHUNK)
                hi, lo = split(jnp.clip(e[:, cols], -limit, limit))
                xslots[inner, px, k] = quads(dot(mtcat[...], jnp.concatenate([hi, lo], 1)))
                for d in range(1, n_x):
                    xcopy(inner, k, d).start()
                return carry
            with jax.named_scope("products"):
                lax.fori_loop(0, chunks, products, 0)
            if inner == 0:
                with jax.named_scope("gwait"):
                    for d in range(1, n_x):
                        gcopy(d).wait_recv()
                total = gslots[0]
                for x in range(1, n_x):
                    total = total + gslots[x]
                gfull[...] = total + eye
                sent(gslots.at[pl.ds(0, n_x - 1)], g_send, g_recv.at[0])
                sweep(gfull, 0, rank // PIVOTS)
                h, m, l = split3(gfull[...])
                gcat[...] = jnp.concatenate([h, h, m, h, m, l], 1)

                @pl.when(o == 0)
                def _():
                    with jax.named_scope("sswap"):
                        swap[2].wait_recv()
                    sent(m_out, c_send.at[2], once.at[0])
                    sent(e_far, c_send.at[3], once.at[1])
                    sent(s_far, c_send.at[4], once.at[2])
            wide = CHUNK

            def update(j, carry):
                def own_cols(i, carry):
                    k = j * (wide // CHUNK) + i
                    with jax.named_scope("xw"):
                        for d in range(1, n_x):
                            xcopy(inner, k, d).wait_recv()
                    share = xslots[inner, 0, k]
                    for x in range(1, n_x):
                        share = share + xslots[inner, x, k]
                    h, m, l = split3(share)
                    step = dot(gcat[...], jnp.concatenate([h, m, h, l, m, h], 0))
                    cols = pl.ds(pl.multiple_of(k * CHUNK, CHUNK), CHUNK)
                    value = c_now[:, cols] - step
                    c_now[:, cols] = value
                    prepare_cols(ccat, cols, value)
                    return carry
                lax.fori_loop(0, wide // CHUNK, own_cols, 0)
                errors(s, e, whole, whole, 2 * rows, ccat, pl.ds(pl.multiple_of(j * wide, wide), wide), wide)
                return carry
            with jax.named_scope("update"):
                lax.fori_loop(0, half // wide, update, 0)
            send_limit(inner + 1)

            sent(xslots.at[0, pl.ds(0, n_x - 1)], x_send, x_recv.at[0, 0])

        with jax.named_scope("hpart"):
            hi, lo = split(c_now[...].T)
            ctcat[:, :rank] = hi
            ctcat[:, rank:] = lo
            hpart[...] = quads(dot(ccat[...], ctcat[...]))
            start(hrs)

        @pl.when(jnp.logical_not(more))
        def _():
            c_out[:, side(core)] = c_now[...] * jnp.sqrt(jnp.float32(rows * n_pts))
            amplitudes.start()
        limit = get_limit(INNER)

        def moment(block):
            parts = []
            for q in (1 - core, core):
                part = pl.ds(pl.multiple_of(q * rows + block, rw), rw)
                parts += split(jnp.clip(e[part, :], -limit, limit))
            both = dot(jnp.concatenate(parts, 0), ctcat[...])
            return quads(both[:2 * rw]), quads(both[2 * rw:])

        def over_y(d, h):
            return ycopy(0, d, h, half_of(ypart.at[d], h), half_of(yslots.at[d], h))

        def over_z(d, h):
            return zcopy(0, d, h, half_of(zpart.at[d], h), half_of(zslots.at[d - 1], h))

        def across(t):
            return ccopy(0, t, opart.at[t], oslots.at[t])

        def moments(t, carry):
            @pl.when(t < 2 * n_z)
            def _():
                theirs = t < n_z
                block = row_block(z_peer(far(t % n_z)), jnp.where(theirs, 1 - sy, sy))
                opart[t], value = moment(block)
                across(t).start()

                @pl.when(theirs)
                def _():
                    ypart[far(t % n_z)] = value

                @pl.when(jnp.logical_not(theirs))
                def _():
                    zpart[far(t % n_z)] = value

            @pl.when(t == 1)
            def _():
                finish(hslots, h_send.at[0], h_recv.at[0])
                own = hpart[h_rows(gme), :]
                for j in range(1, group):
                    own = own + hslots[j - 1]
                hred[...] = own
                hfull[h_rows(gme), :] = own
                start(hag)

            @pl.when(t >= LAG)
            def _():
                u = t - LAG
                d = far(u % n_z)
                across(u).wait_recv()

                @pl.when(u < n_z)
                def _():
                    ypart[d] = ypart[d] + oslots[u]
                    over_y(d, 0).start()

                @pl.when(u >= n_z)
                def _():
                    zpart[d] = zpart[d] + oslots[u]

                @pl.when(u == n_z - 1)
                def _():
                    start([over_y(far(v), 1) for v in range(n_z)])
            return carry
        with jax.named_scope("moments"):
            lax.fori_loop(0, 2 * n_z + LAG, moments, 0)

        def forward(t, carry):
            d, h = far(t % n_z), t // n_z
            part = pl.ds(pl.multiple_of(h * rh, rh), rh)
            with jax.named_scope("ywait"):
                over_y(d, h).wait_recv()
            zpart[d, part, :] = zpart[d, part, :] + yslots[d, part, :]

            @pl.when(d > 0)
            def _():
                over_z(d, h).start()
            return carry
        lax.fori_loop(0, n_z, forward, 0)
        with jax.named_scope("hag"):
            finish(hfull.at[pl.ds(0, rank - hw)], h_send.at[1], h_recv.at[1])
        hfull[...] = hfull[...] + eye
        steps = rank // PIVOTS
        per = steps // n_z

        def sweep_forward(t, carry):
            sweep(hfull, t * per, per)
            return forward(n_z + t, carry)
        lax.fori_loop(0, n_z, sweep_forward, 0)
        sweep(hfull, per * n_z, steps - per * n_z)

        a3, b3, c3 = split3(hfull[...])
        hcat[...] = jnp.concatenate([a3, b3, a3, c3, b3, a3], 0)

        def modes_half(z, which, h):
            return m_out.at[pl.ds(pl.multiple_of((z * 2 + which) * rw + h * rh, rh), rh)]

        def gather(d, h):
            ref = modes_half(sz, sy, h)
            return zcopy(1, d, h, ref, ref)

        def pass_on(d, h):
            ref = modes_half(z_from(d), sy, h)
            return ycopy(1, d, h, ref, ref)

        def solve(h, carry):
            with jax.named_scope("zwait"):
                for d in range(1, n_z):
                    over_z(d, h).wait_recv()
            part = pl.ds(pl.multiple_of(h * rh, rh), rh)
            share = zpart[0, part, :]
            for d in range(1, n_z):
                share = share + zslots[d - 1, part, :]
            h3, m3, l3 = split3(share)
            step = dot(jnp.concatenate([h3, h3, m3, h3, m3, l3], 1), hcat[...])
            mine = pl.ds(pl.multiple_of(sme * rw + h * rh, rh), rh)
            m_out[mine, :] = m_out[mine, :] - step
            start([gather(far(t), h) for t in range(n_z - 1)])
            pass_on(0, h).start()
            return carry
        lax.fori_loop(0, 2, solve, 0)

        def near(u):
            return jnp.where(u == 0, 1, n_z - u)

        def block_of(i):
            u = i % n_z
            d = jnp.where(u == 0, 0, near(u - 1))
            return d, row_block(z_from(d), jnp.where(i < n_z, sy, 1 - sy))

        def hand_over(i):
            part = pl.ds(pl.multiple_of(block_of(i)[1], rw), rw)
            return ccopy(1, i, m_out.at[part], m_far.at[part])

        def take(ref, which, i):
            block = block_of(i)[1]
            part = pl.ds(pl.multiple_of(which * rows + block, rw), rw)
            prepare_rows(part, ref[pl.ds(pl.multiple_of(block, rw), rw), :])
            error_rows(part)

        def take_own(i):
            @pl.when(more)
            def _():
                hand_over(i).start()
                take(m_out, core, i)

        def take_far(i):
            @pl.when(more)
            def _():
                with jax.named_scope("farwait"):
                    hand_over(i).wait_recv()
                take(m_far, 1 - core, i)
        take_own(0)

        def first_half(u, carry):
            with jax.named_scope("gatherz"):
                gather(near(u), 0).wait_recv()
            pass_on(near(u), 0).start()
            return carry
        lax.fori_loop(0, n_z - 1, first_half, 0)

        def second_half(u, carry):
            with jax.named_scope("gatherz"):
                gather(near(u), 1).wait_recv()
            pass_on(near(u), 1).start()
            take_own(1 + u)
            take_far(u)
            return carry
        lax.fori_loop(0, n_z - 1, second_half, 0)

        def other(u, carry):
            d = block_of(u)[0]
            with jax.named_scope("gathery"):
                pass_on(d, 0).wait_recv()
                pass_on(d, 1).wait_recv()
            take_own(n_z + u)
            take_far(n_z + u - 1)
            return carry
        with jax.named_scope("other"):
            lax.fori_loop(0, n_z, other, 0)

        take_far(2 * n_z - 1)

        @pl.when(more)
        def _():
            send_limit(0)
            gram_part()
            sent(m_out, c_send.at[1], c_recv.at[1, 0])
        with jax.named_scope("sends"):
            sent(opart, c_send.at[0], c_recv.at[0, 0])
            sent(ypart, y_send.at[0], y_recv.at[0, 0, 0])
            sent(m_out.at[pl.ds(0, n_z * rw)], y_send.at[1], y_recv.at[1, 0, 0])
            sent(zslots, z_send.at[0], z_recv.at[0, 0, 0])
            sent(m_out.at[pl.ds(0, (n_z - 1) * rw)], z_send.at[1], z_recv.at[1, 0, 0])
        return carry
    lax.fori_loop(0, OUTER, outer, 0)
    amplitudes.wait_recv()
    amplitudes.wait_send()


def write_out(modes, amplitudes, m_hbm, a_hbm, sem):
    copies = [pltpu.make_async_copy(modes, m_hbm, sem.at[0]), pltpu.make_async_copy(amplitudes, a_hbm, sem.at[1])]
    for copy in copies:
        copy.start()
    for copy in copies:
        copy.wait()


def shards(n_pts, n_snap, snapshots, modes_init, coefs_init):
    rows, width = snapshots.shape
    rank = modes_init.shape[1]
    rw, half, group = rows // n_snap, width // 2, 2 * n_snap
    chunks, n_x, n_z, n_dev = half // CHUNK, n_pts // 2, n_snap // 2, n_pts * n_snap
    hw = rank // group
    vmem, dma = pltpu.VMEM, pltpu.SemaphoreType.DMA
    scratch = [
        vmem((2 * rows, half), F32), vmem((2 * rows, half), F32), vmem((rows, half), F32), vmem((rows, half), F32),
        vmem((rows, rank), F32), vmem((rank, half), F32), vmem((rank, half), F32),
        vmem((2 * rows, 2 * rank), BF16), vmem((2 * rank, 2 * rows), BF16),
        vmem((2 * rank, half), BF16), vmem((2 * rank, half), BF16), vmem((half, 2 * rank), BF16),
        vmem((8, STEP), F32),
        vmem((n_x, rank, rank), F32), vmem((rank, rank), F32), vmem((rank, 6 * rank), BF16),
        vmem((rank, rank), F32), vmem((group - 1, hw, rank), F32), vmem((hw, rank), F32), vmem((rank, rank), F32),
        vmem((6 * rank, rank), BF16),
        vmem((INNER + 1, n_dev, 128), F32),
        vmem((INNER, n_x, chunks, rank, CHUNK), F32),
        vmem((n_snap, rw, rank), F32), vmem((n_snap, rw, rank), F32),
        vmem((n_z, rw, rank), F32), vmem((n_z, rw, rank), F32),
        vmem((n_z, rw, rank), F32), vmem((n_z - 1, rw, rank), F32),
        dma((3 + width // STEP,)),
        dma, dma((n_x - 1,)),
        dma((2,)), dma((2,)),
        dma((6,)), dma((2, n_snap)), dma((4,)),
        dma, dma((chunks, n_x - 1)),
        dma((INNER + 1,)), dma((INNER + 1,)),
        dma((2,)), dma((2, n_z, 2)),
        dma((2,)), dma((2, n_z - 1, 2)),
    ]
    modes, coefs = pl.pallas_call(
        functools.partial(kernel, n_pts, n_snap),
        out_shape=(vmem((rows, rank), F32), vmem((rank, width), F32)),
        in_specs=[pl.BlockSpec(memory_space=pltpu.HBM)] * 3,
        out_specs=(pl.BlockSpec(memory_space=vmem), pl.BlockSpec(memory_space=vmem)),
        scratch_shapes=scratch,
        compiler_params=pltpu.CompilerParams(collective_id=0, has_side_effects=True, vmem_limit_bytes=67043328 - 5 * 256 * 1024),
    )(snapshots, modes_init, coefs_init)
    return pl.pallas_call(
        write_out,
        out_shape=(jax.ShapeDtypeStruct((rows, rank), F32), jax.ShapeDtypeStruct((rank, width), F32)),
        in_specs=[pl.BlockSpec(memory_space=pl.ANY)] * 2,
        out_specs=(pl.BlockSpec(memory_space=pltpu.HBM), pl.BlockSpec(memory_space=pltpu.HBM)),
        scratch_shapes=[dma((2,))],
    )(pltpu.with_memory_space_constraint(modes, vmem), pltpu.with_memory_space_constraint(coefs, vmem))


def solution(mesh):
    in_specs = (P("pts", "snap"), P("pts", None), P(None, "snap"))
    out_specs = (P("pts", None), P(None, "snap"))
    body = functools.partial(shards, mesh.shape["pts"], mesh.shape["snap"])
    return jax.shard_map(body, mesh=mesh, in_specs=in_specs, out_specs=out_specs, check_vma=False)
```

```python
import functools

import jax
import jax.numpy as jnp
from jax import lax
from jax.experimental import pallas as pl
from jax.experimental.pallas import tpu as pltpu
from jax.sharding import PartitionSpec as P

OUTER = 2
INNER = 2
PIVOTS = 16
CHUNK = 128
STEP = 256
LAG = 3

HUBER = 1.345
RIDGE = 0.01

F32 = jnp.float32
BF16 = jnp.bfloat16
MESH = pl.DeviceIdType.MESH


def split(x):
    hi = x.astype(BF16)
    lo = (x - hi.astype(F32)).astype(BF16)
    return hi, lo


def split3(x):
    hi = x.astype(BF16)
    rest = x - hi.astype(F32)
    mid = rest.astype(BF16)
    lo = (rest - mid.astype(F32)).astype(BF16)
    return hi, mid, lo


def dot(a, b):
    return jnp.dot(a, b, preferred_element_type=F32)


def quads(x):
    r, c = x.shape[0] // 2, x.shape[1] // 2
    return (x[:r, :c] + x[:r, c:]) + (x[r:, :c] + x[r:, c:])


def kernel(n_pts, n_snap, s_hbm, m_hbm, c_hbm, m_out, c_out,
           s, e, s_far, e_far, m_far, c_now, c_far, mcat, mtcat, ccat, ccat_far, ctcat, sq,
           gslots, gfull, hpart, hslots, hred, hfull,
           lslots, xslots, opart, oslots, ypart, yslots, zpart, zslots,
           load_sem, g_send, g_recv, h_send, h_recv, c_send, c_recv, once, x_send, x_recv,
           l_send, l_recv, y_send, y_recv, z_send, z_recv):
    rows, rank = m_out.shape
    width = c_out.shape[1]
    pme = lax.axis_index("pts")
    sme = lax.axis_index("snap")
    n_dev = n_pts * n_snap
    me = pme * n_snap + sme
    rw = rows // n_snap
    rh = rw // 2
    half = width // 2
    chunks = half // CHUNK
    n_x, n_z = n_pts // 2, n_snap // 2
    px, core = pme // 2, lax.rem(pme, 2)
    sz, sy = sme // 2, lax.rem(sme, 2)
    group = 2 * n_snap
    gme = core * n_snap + sme
    hw = rank // group
    count = float(rows * n_pts * width * n_snap)
    loads = half // STEP
    whole = pl.ds(0, 2 * rows)
    own_points = pl.ds(pl.multiple_of(core * rows, rows), rows)
    far_points = pl.ds(pl.multiple_of((1 - core) * rows, rows), rows)

    def offset(d):
        dx, dc, dz, dy = d
        return {"pts": lax.rem(px + dx, n_x) * 2 + lax.rem(core + dc, 2),
                "snap": lax.rem(sz + dz, n_z) * 2 + lax.rem(sy + dy, 2)}

    def hops(d):
        dx, dc, dz, dy = d
        return min(dx, n_x - dx) + dy + min(dz, n_z - dz) + 0.1 * dc
    others = [(dx, dc, dz, dy) for dx in range(n_x) for dc in range(2) for dz in range(n_z) for dy in range(2)][1:]
    others.sort(key=lambda d: -hops(d))

    def step_cols(j):
        return pl.ds(pl.multiple_of(j * STEP, STEP), STEP)

    def snap_cols(which, j):
        return pl.ds(pl.multiple_of(which * half + j * STEP, STEP), STEP)

    def load_own(j):
        return pltpu.make_async_copy(
            s_hbm.at[:, snap_cols(core, j)], s.at[own_points, step_cols(j)], load_sem.at[3 + j])

    def load_far(j):
        return pltpu.make_async_copy(
            s_hbm.at[:, snap_cols(1 - core, j)], s_far.at[:, step_cols(j)], load_sem.at[3 + loads + j])

    def side(which):
        return pl.ds(pl.multiple_of(which * half, half), half)
    load_m = pltpu.make_async_copy(m_hbm, m_out, load_sem.at[0])
    load_c = pltpu.make_async_copy(c_hbm.at[:, side(core)], c_now, load_sem.at[1])
    load_c_far = pltpu.make_async_copy(c_hbm.at[:, side(1 - core)], c_far, load_sem.at[2])
    start_all = [load_m, load_c] + [load_own(j) for j in range(loads)] + [load_c_far] + [load_far(j) for j in range(loads)]
    for copy in start_all:
        copy.start()

    barrier = pltpu.get_barrier_semaphore()
    for d in others:
        pl.semaphore_signal(barrier, inc=1, device_id=offset(d), device_id_type=MESH)

    def gcopy(d):
        ref = gslots.at[px]
        return pltpu.make_async_remote_copy(
            src_ref=ref, dst_ref=ref, send_sem=g_send, recv_sem=g_recv.at[d - 1],
            device_id={"pts": lax.rem(px + d, n_x) * 2 + core}, device_id_type=MESH)

    def hcopy(site, j, src, dst):
        peer = lax.rem(gme + j, group)
        return pltpu.make_async_remote_copy(
            src_ref=src, dst_ref=dst, send_sem=h_send.at[site], recv_sem=h_recv.at[site],
            device_id={"pts": px * 2 + peer // n_snap, "snap": lax.rem(peer, n_snap)}, device_id_type=MESH)

    def h_rows(g):
        return pl.ds(pl.multiple_of(g * hw, hw), hw)

    def ccopy(site, k, src, dst):
        return pltpu.make_async_remote_copy(
            src_ref=src, dst_ref=dst, send_sem=c_send.at[site + k if site == 2 else site],
            recv_sem=c_recv.at[site, k] if site < 2 else once.at[k + site - 2],
            device_id={"pts": px * 2 + 1 - core}, device_id_type=MESH)

    def xcopy(site, k, d):
        ref = xslots.at[site, px, k]
        return pltpu.make_async_remote_copy(
            src_ref=ref, dst_ref=ref, send_sem=x_send, recv_sem=x_recv.at[k, d - 1],
            device_id={"pts": lax.rem(px + d, n_x) * 2 + core}, device_id_type=MESH)

    def lcopy(use, i):
        ref = lslots.at[use, pl.ds(me, 1)]
        return pltpu.make_async_remote_copy(
            src_ref=ref, dst_ref=ref, send_sem=l_send.at[use], recv_sem=l_recv.at[use],
            device_id=offset(others[i]), device_id_type=MESH)

    def lwait(use):
        ref = lslots.at[use, pl.ds(0, n_dev - 1)]
        return pltpu.make_async_remote_copy(
            src_ref=ref, dst_ref=ref, send_sem=l_send.at[use], recv_sem=l_recv.at[use],
            device_id=offset(others[0]), device_id_type=MESH)

    def half_of(ref, h):
        return ref.at[pl.ds(pl.multiple_of(h * rh, rh), rh)]

    def ycopy(site, d, h, src, dst):
        return pltpu.make_async_remote_copy(
            src_ref=src, dst_ref=dst, send_sem=y_send.at[site], recv_sem=y_recv.at[site, d, h],
            device_id={"snap": sz * 2 + 1 - sy}, device_id_type=MESH)

    def zcopy(site, d, h, src, dst):
        return pltpu.make_async_remote_copy(
            src_ref=src, dst_ref=dst, send_sem=z_send.at[site], recv_sem=z_recv.at[site, d - 1, h],
            device_id={"snap": z_peer(d) * 2 + sy}, device_id_type=MESH)

    def z_peer(d):
        return (sz // 2 + d // 2) % (n_z // 2) * 2 + (sz + d) % 2

    def z_from(d):
        return (sz // 2 + n_z // 2 - d // 2) % (n_z // 2) * 2 + (sz + d) % 2

    def row_block(z, which):
        return (z * 2 + which) * rw

    def far(t):
        return n_z - 1 - t

    def start(copies):
        for copy in copies:
            copy.start()

    def all_of(ref, send_sem, recv_sem):
        return pltpu.make_async_remote_copy(
            src_ref=ref, dst_ref=ref, send_sem=send_sem, recv_sem=recv_sem,
            device_id={"pts": px * 2 + 1 - core}, device_id_type=MESH)

    def finish(ref, send_sem, recv_sem):
        all_of(ref, send_sem, recv_sem).wait_recv()
        all_of(ref, send_sem, recv_sem).wait_send()

    def sent(ref, send_sem, recv_sem):
        all_of(ref, send_sem, recv_sem).wait_send()

    def prepare_rows(part, value):
        hi, lo = split(value)
        mcat[part, :rank] = hi
        mcat[part, rank:] = lo

    def prepare_mt():
        for ref, part in ((m_out, own_points), (m_far, far_points)):
            hi, lo = split(ref[...].T)
            mtcat[:rank, part] = hi
            mtcat[rank:, part] = lo

    def prepare_cols(ref, cols, value):
        hi, lo = split(value)
        ref[:rank, cols] = hi
        ref[rank:, cols] = lo

    def sweep(ref, base, steps):
        sub = lax.broadcasted_iota(jnp.int32, (PIVOTS, rank), 0)
        lane = lax.broadcasted_iota(jnp.int32, (PIVOTS, rank), 1)
        wide = lax.broadcasted_iota(jnp.int32, (rank, rank), 1)
        side = sub[:, :1]

        def body(t, carry):
            k = (base + t) * PIVOTS
            rws = pl.ds(pl.multiple_of(k, PIVOTS), PIVOTS)
            before = ref[rws, :]
            after = before
            cols = [jnp.sum(jnp.where(lane == k + p, before, 0.0), axis=1, keepdims=True) for p in range(PIVOTS)]
            for p in range(PIVOTS):
                col = cols[p]
                inv = 1.0 / col[p:p + 1, :]
                row = after[p:p + 1, :] * inv
                for q in range(p + 1, PIVOTS):
                    f = cols[q][p:p + 1, :] * inv
                    cols[q] = jnp.where(side == p, f, cols[q] - col * f)
                after = jnp.where(lane == k + p, col * inv, after - col * row)
                after = jnp.where(sub == p, jnp.where(lane == k + p, -inv, row), after)
            h, m, l = split3(before)
            a, b, c = split3(after)
            change = lax.dot_general(
                jnp.concatenate([h, h, m, h, m, l], 0), jnp.concatenate([a, b, a, c, b, a], 0),
                (((0,), (0,)), ((), ())), preferred_element_type=F32)
            ref[...] = jnp.where((wide >= k) & (wide < k + PIVOTS), 0.0, ref[...]) - change
            ref[rws, :] = after
            return carry
        with jax.named_scope("sweep"):
            lax.fori_loop(0, steps, body, 0)

    def errors(src, dst, part, m_part, n_rows, c_ref, cols, n_cols):
        c = jnp.concatenate([c_ref[:rank, cols], c_ref[rank:, cols]], 1)
        fit = dot(mcat[m_part, :], jnp.concatenate([c, c], 0))
        err = src[part, cols] - (fit[:, :n_cols] + fit[:, n_cols:])
        dst[part, cols] = err
        sq[:, :n_cols] += jnp.sum((err * err).reshape(n_rows // 8, 8, n_cols), axis=0)

    def error_rows(part):
        hi, lo = mcat[part, :rank], mcat[part, rank:]
        both = jnp.concatenate([jnp.concatenate([hi, hi], 1), jnp.concatenate([lo, lo], 1)], 0)
        for j in range(loads):
            cols = pl.ds(j * STEP, STEP)
            fit = dot(both, ccat[:, cols])
            err = s[part, cols] - (fit[:rw] + fit[rw:])
            e[part, cols] = err
            sq[...] += jnp.sum((err * err).reshape(rw // 8, 8, STEP), axis=0)

    def send_limit(use):
        acc = sq[:, :128]
        for k in range(1, STEP // 128):
            acc = acc + sq[:, k * 128:(k + 1) * 128]
        lslots[use, pl.ds(me, 1), :] = jnp.sum(acc, axis=0, keepdims=True)
        start([lcopy(use, i) for i in range(n_dev - 1)])
        sq[...] = jnp.zeros_like(sq)

    def get_limit(use):
        with jax.named_scope("limit"):
            lwait(use).wait_recv()
        total = jnp.sum(jnp.sum(lslots[use], axis=0, keepdims=True), axis=1, keepdims=True)
        lwait(use).wait_send()
        return HUBER * jnp.sqrt(total / count + 1e-06)

    eye = (lax.broadcasted_iota(jnp.int32, (rank, rank), 0)
           == lax.broadcasted_iota(jnp.int32, (rank, rank), 1)).astype(F32) * RIDGE

    hrs = [hcopy(0, j, hpart.at[h_rows(lax.rem(gme + j, group))], hslots.at[j - 1]) for j in range(1, group)]
    hag = [hcopy(1, j, hred, hfull.at[h_rows(gme)]) for j in range(1, group)]

    def gram_part():
        prepare_mt()
        gslots[px] = quads(dot(mtcat[...], mcat[...]))
        start([gcopy(d) for d in range(1, n_x)])

    sq[...] = jnp.zeros_like(sq)
    load_m.wait()
    prepare_rows(own_points, m_out[...])
    load_c.wait()
    prepare_cols(ccat, pl.ds(0, half), c_now[...])
    with jax.named_scope("err0"):
        def first_own(j, carry):
            load_own(j).wait()
            errors(s, e, own_points, own_points, rows, ccat, step_cols(j), STEP)
            return carry
        lax.fori_loop(0, loads, first_own, 0)
        load_c_far.wait()
        prepare_cols(ccat_far, pl.ds(0, half), c_far[...])

        def first_far(j, carry):
            load_far(j).wait()
            errors(s_far, e_far, pl.ds(0, rows), own_points, rows, ccat_far, step_cols(j), STEP)
            return carry
        lax.fori_loop(0, loads, first_far, 0)
    with jax.named_scope("barrier"):
        pl.semaphore_wait(barrier, n_dev - 1)
    send_limit(0)
    swap = [ccopy(2, 0, m_out, m_far), ccopy(2, 1, e_far, e.at[own_points]), ccopy(2, 2, s_far, s.at[own_points])]
    start(swap)
    with jax.named_scope("mswap"):
        swap[0].wait_recv()
    prepare_rows(far_points, m_far[...])
    gram_part()

    amplitudes = ccopy(5, 0, c_out.at[:, side(core)], c_out.at[:, side(core)])

    def outer(o, carry):
        more = o < OUTER - 1

        for inner in range(INNER):
            limit = get_limit(inner)

            if inner == 0:
                @pl.when(o == 0)
                def _():
                    with jax.named_scope("eswap"):
                        swap[1].wait_recv()

            def products(k, carry):
                cols = pl.ds(pl.multiple_of(k * CHUNK, CHUNK), CHUNK)
                hi, lo = split(jnp.clip(e[:, cols], -limit, limit))
                xslots[inner, px, k] = quads(dot(mtcat[...], jnp.concatenate([hi, lo], 1)))
                for d in range(1, n_x):
                    xcopy(inner, k, d).start()
                return carry
            with jax.named_scope("products"):
                lax.fori_loop(0, chunks, products, 0)
            if inner == 0:
                with jax.named_scope("gwait"):
                    for d in range(1, n_x):
                        gcopy(d).wait_recv()
                total = gslots[0]
                for x in range(1, n_x):
                    total = total + gslots[x]
                gfull[...] = total + eye
                sent(gslots.at[pl.ds(0, n_x - 1)], g_send, g_recv.at[0])
                sweep(gfull, 0, rank // PIVOTS)

                @pl.when(o == 0)
                def _():
                    with jax.named_scope("sswap"):
                        swap[2].wait_recv()
                    sent(m_out, c_send.at[2], once.at[0])
                    sent(e_far, c_send.at[3], once.at[1])
                    sent(s_far, c_send.at[4], once.at[2])
            wide = CHUNK

            def update(j, carry):
                def own_cols(i, carry):
                    k = j * (wide // CHUNK) + i
                    with jax.named_scope("xw"):
                        for d in range(1, n_x):
                            xcopy(inner, k, d).wait_recv()
                    share = xslots[inner, 0, k]
                    for x in range(1, n_x):
                        share = share + xslots[inner, x, k]
                    step = jnp.dot(gfull[...], share, preferred_element_type=F32, precision=lax.Precision.HIGHEST)
                    cols = pl.ds(pl.multiple_of(k * CHUNK, CHUNK), CHUNK)
                    value = c_now[:, cols] - step
                    c_now[:, cols] = value
                    prepare_cols(ccat, cols, value)
                    return carry
                lax.fori_loop(0, wide // CHUNK, own_cols, 0)
                errors(s, e, whole, whole, 2 * rows, ccat, pl.ds(pl.multiple_of(j * wide, wide), wide), wide)
                return carry
            with jax.named_scope("update"):
                lax.fori_loop(0, half // wide, update, 0)
            send_limit(inner + 1)

            sent(xslots.at[0, pl.ds(0, n_x - 1)], x_send, x_recv.at[0, 0])

        with jax.named_scope("hpart"):
            hi, lo = split(c_now[...].T)
            ctcat[:, :rank] = hi
            ctcat[:, rank:] = lo
            hpart[...] = quads(dot(ccat[...], ctcat[...]))
            start(hrs)

        @pl.when(jnp.logical_not(more))
        def _():
            c_out[:, side(core)] = c_now[...] * jnp.sqrt(jnp.float32(rows * n_pts))
            amplitudes.start()
        limit = get_limit(INNER)

        def moment(block):
            parts = []
            for q in (1 - core, core):
                part = pl.ds(pl.multiple_of(q * rows + block, rw), rw)
                parts += split(jnp.clip(e[part, :], -limit, limit))
            both = dot(jnp.concatenate(parts, 0), ctcat[...])
            return quads(both[:2 * rw]), quads(both[2 * rw:])

        def over_y(d, h):
            return ycopy(0, d, h, half_of(ypart.at[d], h), half_of(yslots.at[d], h))

        def over_z(d, h):
            return zcopy(0, d, h, half_of(zpart.at[d], h), half_of(zslots.at[d - 1], h))

        def across(t):
            return ccopy(0, t, opart.at[t], oslots.at[t])

        def moments(t, carry):
            @pl.when(t < 2 * n_z)
            def _():
                theirs = t < n_z
                block = row_block(z_peer(far(t % n_z)), jnp.where(theirs, 1 - sy, sy))
                opart[t], value = moment(block)
                across(t).start()

                @pl.when(theirs)
                def _():
                    ypart[far(t % n_z)] = value

                @pl.when(jnp.logical_not(theirs))
                def _():
                    zpart[far(t % n_z)] = value

            @pl.when(t == 1)
            def _():
                finish(hslots, h_send.at[0], h_recv.at[0])
                own = hpart[h_rows(gme), :]
                for j in range(1, group):
                    own = own + hslots[j - 1]
                hred[...] = own
                hfull[h_rows(gme), :] = own
                start(hag)

            @pl.when(t >= LAG)
            def _():
                u = t - LAG
                d = far(u % n_z)
                across(u).wait_recv()

                @pl.when(u < n_z)
                def _():
                    ypart[d] = ypart[d] + oslots[u]
                    over_y(d, 0).start()

                @pl.when(u >= n_z)
                def _():
                    zpart[d] = zpart[d] + oslots[u]

                @pl.when(u == n_z - 1)
                def _():
                    start([over_y(far(v), 1) for v in range(n_z)])
            return carry
        with jax.named_scope("moments"):
            lax.fori_loop(0, 2 * n_z + LAG, moments, 0)

        def forward(t, carry):
            d, h = far(t % n_z), t // n_z
            part = pl.ds(pl.multiple_of(h * rh, rh), rh)
            with jax.named_scope("ywait"):
                over_y(d, h).wait_recv()
            zpart[d, part, :] = zpart[d, part, :] + yslots[d, part, :]

            @pl.when(d > 0)
            def _():
                over_z(d, h).start()
            return carry
        lax.fori_loop(0, n_z, forward, 0)
        with jax.named_scope("hag"):
            finish(hfull.at[pl.ds(0, rank - hw)], h_send.at[1], h_recv.at[1])
        hfull[...] = hfull[...] + eye
        steps = rank // PIVOTS
        per = steps // n_z

        def sweep_forward(t, carry):
            sweep(hfull, t * per, per)
            return forward(n_z + t, carry)
        lax.fori_loop(0, n_z, sweep_forward, 0)
        sweep(hfull, per * n_z, steps - per * n_z)

        def modes_half(z, which, h):
            return m_out.at[pl.ds(pl.multiple_of((z * 2 + which) * rw + h * rh, rh), rh)]

        def gather(d, h):
            ref = modes_half(sz, sy, h)
            return zcopy(1, d, h, ref, ref)

        def pass_on(d, h):
            ref = modes_half(z_from(d), sy, h)
            return ycopy(1, d, h, ref, ref)

        def solve(h, carry):
            with jax.named_scope("zwait"):
                for d in range(1, n_z):
                    over_z(d, h).wait_recv()
            part = pl.ds(pl.multiple_of(h * rh, rh), rh)
            share = zpart[0, part, :]
            for d in range(1, n_z):
                share = share + zslots[d - 1, part, :]
            step = jnp.dot(share, hfull[...], preferred_element_type=F32, precision=lax.Precision.HIGHEST)
            mine = pl.ds(pl.multiple_of(sme * rw + h * rh, rh), rh)
            m_out[mine, :] = m_out[mine, :] - step
            start([gather(far(t), h) for t in range(n_z - 1)])
            pass_on(0, h).start()
            return carry
        lax.fori_loop(0, 2, solve, 0)

        def near(u):
            return jnp.where(u == 0, 1, n_z - u)

        def block_of(i):
            u = i % n_z
            d = jnp.where(u == 0, 0, near(u - 1))
            return d, row_block(z_from(d), jnp.where(i < n_z, sy, 1 - sy))

        def hand_over(i):
            part = pl.ds(pl.multiple_of(block_of(i)[1], rw), rw)
            return ccopy(1, i, m_out.at[part], m_far.at[part])

        def take(ref, which, i):
            block = block_of(i)[1]
            part = pl.ds(pl.multiple_of(which * rows + block, rw), rw)
            prepare_rows(part, ref[pl.ds(pl.multiple_of(block, rw), rw), :])
            error_rows(part)

        def take_own(i):
            @pl.when(more)
            def _():
                hand_over(i).start()
                take(m_out, core, i)

        def take_far(i):
            @pl.when(more)
            def _():
                with jax.named_scope("farwait"):
                    hand_over(i).wait_recv()
                take(m_far, 1 - core, i)
        take_own(0)

        def first_half(u, carry):
            with jax.named_scope("gatherz"):
                gather(near(u), 0).wait_recv()
            pass_on(near(u), 0).start()
            return carry
        lax.fori_loop(0, n_z - 1, first_half, 0)

        def second_half(u, carry):
            with jax.named_scope("gatherz"):
                gather(near(u), 1).wait_recv()
            pass_on(near(u), 1).start()
            take_own(1 + u)
            take_far(u)
            return carry
        lax.fori_loop(0, n_z - 1, second_half, 0)

        def other(u, carry):
            d = block_of(u)[0]
            with jax.named_scope("gathery"):
                pass_on(d, 0).wait_recv()
                pass_on(d, 1).wait_recv()
            take_own(n_z + u)
            take_far(n_z + u - 1)
            return carry
        with jax.named_scope("other"):
            lax.fori_loop(0, n_z, other, 0)

        take_far(2 * n_z - 1)

        @pl.when(more)
        def _():
            send_limit(0)
            gram_part()
            sent(m_out, c_send.at[1], c_recv.at[1, 0])
        with jax.named_scope("sends"):
            sent(opart, c_send.at[0], c_recv.at[0, 0])
            sent(ypart, y_send.at[0], y_recv.at[0, 0, 0])
            sent(m_out.at[pl.ds(0, n_z * rw)], y_send.at[1], y_recv.at[1, 0, 0])
            sent(zslots, z_send.at[0], z_recv.at[0, 0, 0])
            sent(m_out.at[pl.ds(0, (n_z - 1) * rw)], z_send.at[1], z_recv.at[1, 0, 0])
        return carry
    lax.fori_loop(0, OUTER, outer, 0)
    amplitudes.wait_recv()
    amplitudes.wait_send()


def write_out(modes, amplitudes, m_hbm, a_hbm, sem):
    copies = [pltpu.make_async_copy(modes, m_hbm, sem.at[0]), pltpu.make_async_copy(amplitudes, a_hbm, sem.at[1])]
    for copy in copies:
        copy.start()
    for copy in copies:
        copy.wait()


def shards(n_pts, n_snap, snapshots, modes_init, coefs_init):
    rows, width = snapshots.shape
    rank = modes_init.shape[1]
    rw, half, group = rows // n_snap, width // 2, 2 * n_snap
    chunks, n_x, n_z, n_dev = half // CHUNK, n_pts // 2, n_snap // 2, n_pts * n_snap
    hw = rank // group
    vmem, dma = pltpu.VMEM, pltpu.SemaphoreType.DMA
    scratch = [
        vmem((2 * rows, half), F32), vmem((2 * rows, half), F32), vmem((rows, half), F32), vmem((rows, half), F32),
        vmem((rows, rank), F32), vmem((rank, half), F32), vmem((rank, half), F32),
        vmem((2 * rows, 2 * rank), BF16), vmem((2 * rank, 2 * rows), BF16),
        vmem((2 * rank, half), BF16), vmem((2 * rank, half), BF16), vmem((half, 2 * rank), BF16),
        vmem((8, STEP), F32),
        vmem((n_x, rank, rank), F32), vmem((rank, rank), F32),
        vmem((rank, rank), F32), vmem((group - 1, hw, rank), F32), vmem((hw, rank), F32), vmem((rank, rank), F32),
        vmem((INNER + 1, n_dev, 128), F32),
        vmem((INNER, n_x, chunks, rank, CHUNK), F32),
        vmem((n_snap, rw, rank), F32), vmem((n_snap, rw, rank), F32),
        vmem((n_z, rw, rank), F32), vmem((n_z, rw, rank), F32),
        vmem((n_z, rw, rank), F32), vmem((n_z - 1, rw, rank), F32),
        dma((3 + width // STEP,)),
        dma, dma((n_x - 1,)),
        dma((2,)), dma((2,)),
        dma((6,)), dma((2, n_snap)), dma((4,)),
        dma, dma((chunks, n_x - 1)),
        dma((INNER + 1,)), dma((INNER + 1,)),
        dma((2,)), dma((2, n_z, 2)),
        dma((2,)), dma((2, n_z - 1, 2)),
    ]
    modes, coefs = pl.pallas_call(
        functools.partial(kernel, n_pts, n_snap),
        out_shape=(vmem((rows, rank), F32), vmem((rank, width), F32)),
        in_specs=[pl.BlockSpec(memory_space=pltpu.HBM)] * 3,
        out_specs=(pl.BlockSpec(memory_space=vmem), pl.BlockSpec(memory_space=vmem)),
        scratch_shapes=scratch,
        compiler_params=pltpu.CompilerParams(collective_id=0, has_side_effects=True, vmem_limit_bytes=67043328 - 5 * 256 * 1024),
    )(snapshots, modes_init, coefs_init)
    return pl.pallas_call(
        write_out,
        out_shape=(jax.ShapeDtypeStruct((rows, rank), F32), jax.ShapeDtypeStruct((rank, width), F32)),
        in_specs=[pl.BlockSpec(memory_space=pl.ANY)] * 2,
        out_specs=(pl.BlockSpec(memory_space=pltpu.HBM), pl.BlockSpec(memory_space=pltpu.HBM)),
        scratch_shapes=[dma((2,))],
    )(pltpu.with_memory_space_constraint(modes, vmem), pltpu.with_memory_space_constraint(coefs, vmem))


def solution(mesh):
    in_specs = (P("pts", "snap"), P("pts", None), P(None, "snap"))
    out_specs = (P("pts", None), P(None, "snap"))
    body = functools.partial(shards, mesh.shape["pts"], mesh.shape["snap"])
    return jax.shard_map(body, mesh=mesh, in_specs=in_specs, out_specs=out_specs, check_vma=False)
```

```python
import functools

import jax
import jax.numpy as jnp
from jax import lax
from jax.experimental import pallas as pl
from jax.experimental.pallas import tpu as pltpu
from jax.sharding import PartitionSpec as P

OUTER = 2
INNER = 2
PIVOTS = 16
CHUNK = 128
STEP = 256
LAG = 3

HUBER = 1.345
RIDGE = 0.01

F32 = jnp.float32
BF16 = jnp.bfloat16
MESH = pl.DeviceIdType.MESH


def split(x):
    hi = x.astype(BF16)
    lo = (x - hi.astype(F32)).astype(BF16)
    return hi, lo


def split3(x):
    hi = x.astype(BF16)
    rest = x - hi.astype(F32)
    mid = rest.astype(BF16)
    lo = (rest - mid.astype(F32)).astype(BF16)
    return hi, mid, lo


def dot(a, b):
    return jnp.dot(a, b, preferred_element_type=F32)


def quads(x):
    r, c = x.shape[0] // 2, x.shape[1] // 2
    return (x[:r, :c] + x[:r, c:]) + (x[r:, :c] + x[r:, c:])


def kernel(n_pts, n_snap, s_hbm, m_hbm, c_hbm, m_out, c_out,
           s, e, s_far, e_far, m_far, c_now, c_far, mcat, mtcat, ccat, ccat_far, ctcat, sq,
           gslots, gfull, hpart, hslots, hred, hfull,
           lslots, xslots, opart, oslots, ypart, yslots, zpart, zslots,
           load_sem, g_send, g_recv, h_send, h_recv, c_send, c_recv, once, x_send, x_recv,
           l_send, l_recv, y_send, y_recv, z_send, z_recv):
    rows, rank = m_out.shape
    width = c_out.shape[1]
    pme = lax.axis_index("pts")
    sme = lax.axis_index("snap")
    n_dev = n_pts * n_snap
    me = pme * n_snap + sme
    rw = rows // n_snap
    rh = rw // 2
    half = width // 2
    chunks = half // CHUNK
    n_x, n_z = n_pts // 2, n_snap // 2
    px, core = pme // 2, lax.rem(pme, 2)
    sz, sy = sme // 2, lax.rem(sme, 2)
    group = 2 * n_snap
    gme = core * n_snap + sme
    hw = rank // group
    count = float(rows * n_pts * width * n_snap)
    loads = half // STEP
    whole = pl.ds(0, 2 * rows)
    own_points = pl.ds(pl.multiple_of(core * rows, rows), rows)
    far_points = pl.ds(pl.multiple_of((1 - core) * rows, rows), rows)

    def offset(d):
        dx, dc, dz, dy = d
        return {"pts": lax.rem(px + dx, n_x) * 2 + lax.rem(core + dc, 2),
                "snap": lax.rem(sz + dz, n_z) * 2 + lax.rem(sy + dy, 2)}

    def hops(d):
        dx, dc, dz, dy = d
        return min(dx, n_x - dx) + dy + min(dz, n_z - dz) + 0.1 * dc
    others = [(dx, dc, dz, dy) for dx in range(n_x) for dc in range(2) for dz in range(n_z) for dy in range(2)][1:]
    others.sort(key=lambda d: -hops(d))

    def step_cols(j):
        return pl.ds(pl.multiple_of(j * STEP, STEP), STEP)

    def snap_cols(which, j):
        return pl.ds(pl.multiple_of(which * half + j * STEP, STEP), STEP)

    def load_own(j):
        return pltpu.make_async_copy(
            s_hbm.at[:, snap_cols(core, j)], s.at[own_points, step_cols(j)], load_sem.at[3 + j])

    def load_far(j):
        return pltpu.make_async_copy(
            s_hbm.at[:, snap_cols(1 - core, j)], s_far.at[:, step_cols(j)], load_sem.at[3 + loads + j])

    def side(which):
        return pl.ds(pl.multiple_of(which * half, half), half)
    load_m = pltpu.make_async_copy(m_hbm, m_out, load_sem.at[0])
    load_c = pltpu.make_async_copy(c_hbm.at[:, side(core)], c_now, load_sem.at[1])
    load_c_far = pltpu.make_async_copy(c_hbm.at[:, side(1 - core)], c_far, load_sem.at[2])
    start_all = [load_m, load_c, load_own(0), load_c_far] + [load_own(j) for j in range(1, loads)] + [load_far(j) for j in range(loads)]
    for copy in start_all:
        copy.start()

    barrier = pltpu.get_barrier_semaphore()
    for d in others:
        pl.semaphore_signal(barrier, inc=1, device_id=offset(d), device_id_type=MESH)

    def gcopy(d):
        ref = gslots.at[px]
        return pltpu.make_async_remote_copy(
            src_ref=ref, dst_ref=ref, send_sem=g_send, recv_sem=g_recv.at[d - 1],
            device_id={"pts": lax.rem(px + d, n_x) * 2 + core}, device_id_type=MESH)

    def hcopy(site, j, src, dst):
        peer = lax.rem(gme + j, group)
        return pltpu.make_async_remote_copy(
            src_ref=src, dst_ref=dst, send_sem=h_send.at[site], recv_sem=h_recv.at[site],
            device_id={"pts": px * 2 + peer // n_snap, "snap": lax.rem(peer, n_snap)}, device_id_type=MESH)

    def h_rows(g):
        return pl.ds(pl.multiple_of(g * hw, hw), hw)

    def ccopy(site, k, src, dst):
        return pltpu.make_async_remote_copy(
            src_ref=src, dst_ref=dst, send_sem=c_send.at[site + k if site == 2 else site],
            recv_sem=c_recv.at[site, k] if site < 2 else once.at[k + site - 2],
            device_id={"pts": px * 2 + 1 - core}, device_id_type=MESH)

    def xcopy(site, k, d):
        ref = xslots.at[site, px, k]
        return pltpu.make_async_remote_copy(
            src_ref=ref, dst_ref=ref, send_sem=x_send, recv_sem=x_recv.at[k, d - 1],
            device_id={"pts": lax.rem(px + d, n_x) * 2 + core}, device_id_type=MESH)

    def lcopy(use, i):
        ref = lslots.at[use, pl.ds(me, 1)]
        return pltpu.make_async_remote_copy(
            src_ref=ref, dst_ref=ref, send_sem=l_send.at[use], recv_sem=l_recv.at[use],
            device_id=offset(others[i]), device_id_type=MESH)

    def lwait(use):
        ref = lslots.at[use, pl.ds(0, n_dev - 1)]
        return pltpu.make_async_remote_copy(
            src_ref=ref, dst_ref=ref, send_sem=l_send.at[use], recv_sem=l_recv.at[use],
            device_id=offset(others[0]), device_id_type=MESH)

    def half_of(ref, h):
        return ref.at[pl.ds(pl.multiple_of(h * rh, rh), rh)]

    def ycopy(site, d, h, src, dst):
        return pltpu.make_async_remote_copy(
            src_ref=src, dst_ref=dst, send_sem=y_send.at[site], recv_sem=y_recv.at[site, d, h],
            device_id={"snap": sz * 2 + 1 - sy}, device_id_type=MESH)

    def zcopy(site, d, h, src, dst):
        return pltpu.make_async_remote_copy(
            src_ref=src, dst_ref=dst, send_sem=z_send.at[site], recv_sem=z_recv.at[site, d - 1, h],
            device_id={"snap": z_peer(d) * 2 + sy}, device_id_type=MESH)

    def z_peer(d):
        return (sz // 2 + d // 2) % (n_z // 2) * 2 + (sz + d) % 2

    def z_from(d):
        return (sz // 2 + n_z // 2 - d // 2) % (n_z // 2) * 2 + (sz + d) % 2

    def row_block(z, which):
        return (z * 2 + which) * rw

    def far(t):
        return n_z - 1 - t

    def start(copies):
        for copy in copies:
            copy.start()

    def all_of(ref, send_sem, recv_sem):
        return pltpu.make_async_remote_copy(
            src_ref=ref, dst_ref=ref, send_sem=send_sem, recv_sem=recv_sem,
            device_id={"pts": px * 2 + 1 - core}, device_id_type=MESH)

    def finish(ref, send_sem, recv_sem):
        all_of(ref, send_sem, recv_sem).wait_recv()
        all_of(ref, send_sem, recv_sem).wait_send()

    def sent(ref, send_sem, recv_sem):
        all_of(ref, send_sem, recv_sem).wait_send()

    def prepare_rows(part, value):
        hi, lo = split(value)
        mcat[part, :rank] = hi
        mcat[part, rank:] = lo

    def prepare_mt():
        for ref, part in ((m_out, own_points), (m_far, far_points)):
            hi, lo = split(ref[...].T)
            mtcat[:rank, part] = hi
            mtcat[rank:, part] = lo

    def prepare_cols(ref, cols, value):
        hi, lo = split(value)
        ref[:rank, cols] = hi
        ref[rank:, cols] = lo

    def sweep(ref, base, steps):
        sub = lax.broadcasted_iota(jnp.int32, (PIVOTS, rank), 0)
        lane = lax.broadcasted_iota(jnp.int32, (PIVOTS, rank), 1)
        wide = lax.broadcasted_iota(jnp.int32, (rank, rank), 1)
        side = sub[:, :1]

        def body(t, carry):
            k = (base + t) * PIVOTS
            rws = pl.ds(pl.multiple_of(k, PIVOTS), PIVOTS)
            before = ref[rws, :]
            after = before
            cols = [jnp.sum(jnp.where(lane == k + p, before, 0.0), axis=1, keepdims=True) for p in range(PIVOTS)]
            for p in range(PIVOTS):
                col = cols[p]
                inv = 1.0 / col[p:p + 1, :]
                row = after[p:p + 1, :] * inv
                for q in range(p + 1, PIVOTS):
                    f = cols[q][p:p + 1, :] * inv
                    cols[q] = jnp.where(side == p, f, cols[q] - col * f)
                after = jnp.where(lane == k + p, col * inv, after - col * row)
                after = jnp.where(sub == p, jnp.where(lane == k + p, -inv, row), after)
            h, m, l = split3(before)
            a, b, c = split3(after)
            change = lax.dot_general(
                jnp.concatenate([h, h, m, h, m, l], 0), jnp.concatenate([a, b, a, c, b, a], 0),
                (((0,), (0,)), ((), ())), preferred_element_type=F32)
            ref[...] = jnp.where((wide >= k) & (wide < k + PIVOTS), 0.0, ref[...]) - change
            ref[rws, :] = after
            return carry
        with jax.named_scope("sweep"):
            lax.fori_loop(0, steps, body, 0)

    def errors(src, dst, part, m_part, n_rows, c_ref, cols, n_cols):
        c = jnp.concatenate([c_ref[:rank, cols], c_ref[rank:, cols]], 1)
        fit = dot(mcat[m_part, :], jnp.concatenate([c, c], 0))
        err = src[part, cols] - (fit[:, :n_cols] + fit[:, n_cols:])
        dst[part, cols] = err
        sq[:, :n_cols] += jnp.sum((err * err).reshape(n_rows // 8, 8, n_cols), axis=0)

    def error_rows(part):
        hi, lo = mcat[part, :rank], mcat[part, rank:]
        both = jnp.concatenate([jnp.concatenate([hi, hi], 1), jnp.concatenate([lo, lo], 1)], 0)
        for j in range(loads):
            cols = pl.ds(j * STEP, STEP)
            fit = dot(both, ccat[:, cols])
            err = s[part, cols] - (fit[:rw] + fit[rw:])
            e[part, cols] = err
            sq[...] += jnp.sum((err * err).reshape(rw // 8, 8, STEP), axis=0)

    def send_limit(use):
        acc = sq[:, :128]
        for k in range(1, STEP // 128):
            acc = acc + sq[:, k * 128:(k + 1) * 128]
        lslots[use, pl.ds(me, 1), :] = jnp.sum(acc, axis=0, keepdims=True)
        start([lcopy(use, i) for i in range(n_dev - 1)])
        sq[...] = jnp.zeros_like(sq)

    def get_limit(use):
        with jax.named_scope("limit"):
            lwait(use).wait_recv()
        total = jnp.sum(jnp.sum(lslots[use], axis=0, keepdims=True), axis=1, keepdims=True)
        lwait(use).wait_send()
        return HUBER * jnp.sqrt(total / count + 1e-06)

    eye = (lax.broadcasted_iota(jnp.int32, (rank, rank), 0)
           == lax.broadcasted_iota(jnp.int32, (rank, rank), 1)).astype(F32) * RIDGE

    hrs = [hcopy(0, j, hpart.at[h_rows(lax.rem(gme + j, group))], hslots.at[j - 1]) for j in range(1, group)]
    hag = [hcopy(1, j, hred, hfull.at[h_rows(gme)]) for j in range(1, group)]

    def gram_part():
        prepare_mt()
        gslots[px] = quads(dot(mtcat[...], mcat[...]))
        start([gcopy(d) for d in range(1, n_x)])

    sq[...] = jnp.zeros_like(sq)
    load_m.wait()
    prepare_rows(own_points, m_out[...])
    load_c.wait()
    prepare_cols(ccat, pl.ds(0, half), c_now[...])
    with jax.named_scope("err0"):
        def first_own(j, carry):
            load_own(j).wait()
            errors(s, e, own_points, own_points, rows, ccat, step_cols(j), STEP)
            return carry
        lax.fori_loop(0, loads, first_own, 0)
        load_c_far.wait()
        prepare_cols(ccat_far, pl.ds(0, half), c_far[...])

        def first_far(j, carry):
            load_far(j).wait()
            errors(s_far, e_far, pl.ds(0, rows), own_points, rows, ccat_far, step_cols(j), STEP)
            return carry
        lax.fori_loop(0, loads, first_far, 0)
    with jax.named_scope("barrier"):
        pl.semaphore_wait(barrier, n_dev - 1)
    send_limit(0)
    swap = [ccopy(2, 0, m_out, m_far), ccopy(2, 1, e_far, e.at[own_points]), ccopy(2, 2, s_far, s.at[own_points])]
    start(swap)
    with jax.named_scope("mswap"):
        swap[0].wait_recv()
    prepare_rows(far_points, m_far[...])
    gram_part()

    amplitudes = ccopy(5, 0, c_out.at[:, side(core)], c_out.at[:, side(core)])

    def outer(o, carry):
        more = o < OUTER - 1

        for inner in range(INNER):
            limit = get_limit(inner)

            if inner == 0:
                @pl.when(o == 0)
                def _():
                    with jax.named_scope("eswap"):
                        swap[1].wait_recv()

            def products(k, carry):
                cols = pl.ds(pl.multiple_of(k * CHUNK, CHUNK), CHUNK)
                hi, lo = split(jnp.clip(e[:, cols], -limit, limit))
                xslots[inner, px, k] = quads(dot(mtcat[...], jnp.concatenate([hi, lo], 1)))
                for d in range(1, n_x):
                    xcopy(inner, k, d).start()
                return carry
            with jax.named_scope("products"):
                lax.fori_loop(0, chunks, products, 0)
            if inner == 0:
                with jax.named_scope("gwait"):
                    for d in range(1, n_x):
                        gcopy(d).wait_recv()
                total = gslots[0]
                for x in range(1, n_x):
                    total = total + gslots[x]
                gfull[...] = total + eye
                sent(gslots.at[pl.ds(0, n_x - 1)], g_send, g_recv.at[0])
                sweep(gfull, 0, rank // PIVOTS)

                @pl.when(o == 0)
                def _():
                    with jax.named_scope("sswap"):
                        swap[2].wait_recv()
                    sent(m_out, c_send.at[2], once.at[0])
                    sent(e_far, c_send.at[3], once.at[1])
                    sent(s_far, c_send.at[4], once.at[2])
            wide = CHUNK

            def update(j, carry):
                def own_cols(i, carry):
                    k = j * (wide // CHUNK) + i
                    with jax.named_scope("xw"):
                        for d in range(1, n_x):
                            xcopy(inner, k, d).wait_recv()
                    share = xslots[inner, 0, k]
                    for x in range(1, n_x):
                        share = share + xslots[inner, x, k]
                    step = jnp.dot(gfull[...], share, preferred_element_type=F32, precision=lax.Precision.HIGHEST)
                    cols = pl.ds(pl.multiple_of(k * CHUNK, CHUNK), CHUNK)
                    value = c_now[:, cols] - step
                    c_now[:, cols] = value
                    prepare_cols(ccat, cols, value)
                    return carry
                lax.fori_loop(0, wide // CHUNK, own_cols, 0)
                errors(s, e, whole, whole, 2 * rows, ccat, pl.ds(pl.multiple_of(j * wide, wide), wide), wide)
                return carry
            with jax.named_scope("update"):
                lax.fori_loop(0, half // wide, update, 0)
            send_limit(inner + 1)

            sent(xslots.at[0, pl.ds(0, n_x - 1)], x_send, x_recv.at[0, 0])

        with jax.named_scope("hpart"):
            hi, lo = split(c_now[...].T)
            ctcat[:, :rank] = hi
            ctcat[:, rank:] = lo
            hpart[...] = quads(dot(ccat[...], ctcat[...]))
            start(hrs)

        @pl.when(jnp.logical_not(more))
        def _():
            c_out[:, side(core)] = c_now[...] * jnp.sqrt(jnp.float32(rows * n_pts))
            amplitudes.start()
        limit = get_limit(INNER)

        def moment(block):
            parts = []
            for q in (1 - core, core):
                part = pl.ds(pl.multiple_of(q * rows + block, rw), rw)
                parts += split(jnp.clip(e[part, :], -limit, limit))
            both = dot(jnp.concatenate(parts, 0), ctcat[...])
            return quads(both[:2 * rw]), quads(both[2 * rw:])

        def over_y(d, h):
            return ycopy(0, d, h, half_of(ypart.at[d], h), half_of(yslots.at[d], h))

        def over_z(d, h):
            return zcopy(0, d, h, half_of(zpart.at[d], h), half_of(zslots.at[d - 1], h))

        def across(t):
            return ccopy(0, t, opart.at[t], oslots.at[t])

        def moments(t, carry):
            @pl.when(t < 2 * n_z)
            def _():
                theirs = t < n_z
                block = row_block(z_peer(far(t % n_z)), jnp.where(theirs, 1 - sy, sy))
                opart[t], value = moment(block)
                across(t).start()

                @pl.when(theirs)
                def _():
                    ypart[far(t % n_z)] = value

                @pl.when(jnp.logical_not(theirs))
                def _():
                    zpart[far(t % n_z)] = value

            @pl.when(t == 1)
            def _():
                finish(hslots, h_send.at[0], h_recv.at[0])
                own = hpart[h_rows(gme), :]
                for j in range(1, group):
                    own = own + hslots[j - 1]
                hred[...] = own
                hfull[h_rows(gme), :] = own
                start(hag)

            @pl.when(t >= LAG)
            def _():
                u = t - LAG
                d = far(u % n_z)
                across(u).wait_recv()

                @pl.when(u < n_z)
                def _():
                    ypart[d] = ypart[d] + oslots[u]
                    over_y(d, 0).start()

                @pl.when(u >= n_z)
                def _():
                    zpart[d] = zpart[d] + oslots[u]

                @pl.when(u == n_z - 1)
                def _():
                    start([over_y(far(v), 1) for v in range(n_z)])
            return carry
        with jax.named_scope("moments"):
            lax.fori_loop(0, 2 * n_z + LAG, moments, 0)

        def forward(t, carry):
            d, h = far(t % n_z), t // n_z
            part = pl.ds(pl.multiple_of(h * rh, rh), rh)
            with jax.named_scope("ywait"):
                over_y(d, h).wait_recv()
            zpart[d, part, :] = zpart[d, part, :] + yslots[d, part, :]

            @pl.when(d > 0)
            def _():
                over_z(d, h).start()
            return carry
        lax.fori_loop(0, n_z, forward, 0)
        with jax.named_scope("hag"):
            finish(hfull.at[pl.ds(0, rank - hw)], h_send.at[1], h_recv.at[1])
        hfull[...] = hfull[...] + eye
        steps = rank // PIVOTS
        per = steps // n_z

        def sweep_forward(t, carry):
            sweep(hfull, t * per, per)
            return forward(n_z + t, carry)
        lax.fori_loop(0, n_z, sweep_forward, 0)
        sweep(hfull, per * n_z, steps - per * n_z)

        def modes_half(z, which, h):
            return m_out.at[pl.ds(pl.multiple_of((z * 2 + which) * rw + h * rh, rh), rh)]

        def gather(d, h):
            ref = modes_half(sz, sy, h)
            return zcopy(1, d, h, ref, ref)

        def pass_on(d, h):
            ref = modes_half(z_from(d), sy, h)
            return ycopy(1, d, h, ref, ref)

        def solve(h, carry):
            with jax.named_scope("zwait"):
                for d in range(1, n_z):
                    over_z(d, h).wait_recv()
            part = pl.ds(pl.multiple_of(h * rh, rh), rh)
            share = zpart[0, part, :]
            for d in range(1, n_z):
                share = share + zslots[d - 1, part, :]
            step = jnp.dot(share, hfull[...], preferred_element_type=F32, precision=lax.Precision.HIGHEST)
            mine = pl.ds(pl.multiple_of(sme * rw + h * rh, rh), rh)
            m_out[mine, :] = m_out[mine, :] - step
            start([gather(far(t), h) for t in range(n_z - 1)])
            pass_on(0, h).start()
            return carry
        lax.fori_loop(0, 2, solve, 0)

        def near(u):
            return jnp.where(u == 0, 1, n_z - u)

        def block_of(i):
            u = i % n_z
            d = jnp.where(u == 0, 0, near(u - 1))
            return d, row_block(z_from(d), jnp.where(i < n_z, sy, 1 - sy))

        def hand_over(i):
            part = pl.ds(pl.multiple_of(block_of(i)[1], rw), rw)
            return ccopy(1, i, m_out.at[part], m_far.at[part])

        def take(ref, which, i):
            block = block_of(i)[1]
            part = pl.ds(pl.multiple_of(which * rows + block, rw), rw)
            prepare_rows(part, ref[pl.ds(pl.multiple_of(block, rw), rw), :])
            error_rows(part)

        def take_own(i):
            @pl.when(more)
            def _():
                hand_over(i).start()
                take(m_out, core, i)

        def take_far(i):
            @pl.when(more)
            def _():
                with jax.named_scope("farwait"):
                    hand_over(i).wait_recv()
                take(m_far, 1 - core, i)
        take_own(0)

        def first_half(u, carry):
            with jax.named_scope("gatherz"):
                gather(near(u), 0).wait_recv()
            pass_on(near(u), 0).start()
            return carry
        lax.fori_loop(0, n_z - 1, first_half, 0)

        def second_half(u, carry):
            with jax.named_scope("gatherz"):
                gather(near(u), 1).wait_recv()
            pass_on(near(u), 1).start()
            take_own(1 + u)
            take_far(u)
            return carry
        lax.fori_loop(0, n_z - 1, second_half, 0)

        def other(u, carry):
            d = block_of(u)[0]
            with jax.named_scope("gathery"):
                pass_on(d, 0).wait_recv()
                pass_on(d, 1).wait_recv()
            take_own(n_z + u)
            take_far(n_z + u - 1)
            return carry
        with jax.named_scope("other"):
            lax.fori_loop(0, n_z, other, 0)

        take_far(2 * n_z - 1)

        @pl.when(more)
        def _():
            send_limit(0)
            gram_part()
            sent(m_out, c_send.at[1], c_recv.at[1, 0])
        with jax.named_scope("sends"):
            sent(opart, c_send.at[0], c_recv.at[0, 0])
            sent(ypart, y_send.at[0], y_recv.at[0, 0, 0])
            sent(m_out.at[pl.ds(0, n_z * rw)], y_send.at[1], y_recv.at[1, 0, 0])
            sent(zslots, z_send.at[0], z_recv.at[0, 0, 0])
            sent(m_out.at[pl.ds(0, (n_z - 1) * rw)], z_send.at[1], z_recv.at[1, 0, 0])
        return carry
    lax.fori_loop(0, OUTER, outer, 0)
    amplitudes.wait_recv()
    amplitudes.wait_send()


def write_out(modes, amplitudes, m_hbm, a_hbm, sem):
    copies = [pltpu.make_async_copy(modes, m_hbm, sem.at[0]), pltpu.make_async_copy(amplitudes, a_hbm, sem.at[1])]
    for copy in copies:
        copy.start()
    for copy in copies:
        copy.wait()


def shards(n_pts, n_snap, snapshots, modes_init, coefs_init):
    rows, width = snapshots.shape
    rank = modes_init.shape[1]
    rw, half, group = rows // n_snap, width // 2, 2 * n_snap
    chunks, n_x, n_z, n_dev = half // CHUNK, n_pts // 2, n_snap // 2, n_pts * n_snap
    hw = rank // group
    vmem, dma = pltpu.VMEM, pltpu.SemaphoreType.DMA
    scratch = [
        vmem((2 * rows, half), F32), vmem((2 * rows, half), F32), vmem((rows, half), F32), vmem((rows, half), F32),
        vmem((rows, rank), F32), vmem((rank, half), F32), vmem((rank, half), F32),
        vmem((2 * rows, 2 * rank), BF16), vmem((2 * rank, 2 * rows), BF16),
        vmem((2 * rank, half), BF16), vmem((2 * rank, half), BF16), vmem((half, 2 * rank), BF16),
        vmem((8, STEP), F32),
        vmem((n_x, rank, rank), F32), vmem((rank, rank), F32),
        vmem((rank, rank), F32), vmem((group - 1, hw, rank), F32), vmem((hw, rank), F32), vmem((rank, rank), F32),
        vmem((INNER + 1, n_dev, 128), F32),
        vmem((INNER, n_x, chunks, rank, CHUNK), F32),
        vmem((n_snap, rw, rank), F32), vmem((n_snap, rw, rank), F32),
        vmem((n_z, rw, rank), F32), vmem((n_z, rw, rank), F32),
        vmem((n_z, rw, rank), F32), vmem((n_z - 1, rw, rank), F32),
        dma((3 + width // STEP,)),
        dma, dma((n_x - 1,)),
        dma((2,)), dma((2,)),
        dma((6,)), dma((2, n_snap)), dma((4,)),
        dma, dma((chunks, n_x - 1)),
        dma((INNER + 1,)), dma((INNER + 1,)),
        dma((2,)), dma((2, n_z, 2)),
        dma((2,)), dma((2, n_z - 1, 2)),
    ]
    modes, coefs = pl.pallas_call(
        functools.partial(kernel, n_pts, n_snap),
        out_shape=(vmem((rows, rank), F32), vmem((rank, width), F32)),
        in_specs=[pl.BlockSpec(memory_space=pltpu.HBM)] * 3,
        out_specs=(pl.BlockSpec(memory_space=vmem), pl.BlockSpec(memory_space=vmem)),
        scratch_shapes=scratch,
        compiler_params=pltpu.CompilerParams(collective_id=0, has_side_effects=True, vmem_limit_bytes=67043328 - 5 * 256 * 1024),
    )(snapshots, modes_init, coefs_init)
    return pl.pallas_call(
        write_out,
        out_shape=(jax.ShapeDtypeStruct((rows, rank), F32), jax.ShapeDtypeStruct((rank, width), F32)),
        in_specs=[pl.BlockSpec(memory_space=pl.ANY)] * 2,
        out_specs=(pl.BlockSpec(memory_space=pltpu.HBM), pl.BlockSpec(memory_space=pltpu.HBM)),
        scratch_shapes=[dma((2,))],
    )(pltpu.with_memory_space_constraint(modes, vmem), pltpu.with_memory_space_constraint(coefs, vmem))


def solution(mesh):
    in_specs = (P("pts", "snap"), P("pts", None), P(None, "snap"))
    out_specs = (P("pts", None), P(None, "snap"))
    body = functools.partial(shards, mesh.shape["pts"], mesh.shape["snap"])
    return jax.shard_map(body, mesh=mesh, in_specs=in_specs, out_specs=out_specs, check_vma=False)
```
